32 devices in a mesh: groups: 2 (over y), gx: 4 (over z), gy: 4 (over x, core).
Axes of the slice: x: 2, y: 2, z: 4, core: 2. Of those that a mesh axis runs over, the one named last changes fastest.
Arguments:
- populations: float32 [19, 64, 64, 128], P(None, ('groups', 'gx'), 'gy'), parts along dimension 1, may hold values from 0 to 1.1, as said below
- fluid_mask: int32 [64, 64, 128], P(('groups', 'gx'), 'gy'), parts along dimension 0, may hold values 0 or 1
- wet_class: int32 [64, 64, 128], P(('groups', 'gx'), 'gy'), parts along dimension 0, may hold values from 0 to 3
- wall_potential: float32 [8], P('groups'), parts along dimension 0, may hold values from 0 to 1
- relax_rates: float32 [19], replicated, may hold values from 0.8 to 1.6
Outputs:
- populations_out: float32 [19, 64, 64, 128], P(None, ('groups', 'gx'), 'gy'), parts along dimension 1
- velocity: float32 [3, 64, 64, 128], P(None, ('groups', 'gx'), 'gy'), parts along dimension 1
The draws below stay inside these ranges and needn't reach their ends.
There are 2 independent parts, one for each index of `groups`. The reference program is written for one: setup_inputs(seed, part) draws one part's arguments, and reference() takes and returns one part's arrays. A program takes and returns all parts, laid end to end along the dimension named above; an argument that names none is the same for every part. Nothing has to cross between parts.
Inputs may be any that keep to these rules, and one draw needn't show every extreme that they name: `populations`: every population is positive.
All inputs are finite; a program needn't handle non-finite values. No bound on the sum of `fluid_mask` on one device may be relied on, other than what follows from the above.
Results may differ from the reference program's by a relative error of at most 0.0003.
Values sent between devices are 32-bit elements; how exact they have to be, the bound alone decides.
No kernel may reach another device: no remote copies, remote signals or barrier semaphores. Data moves between devices by JAX's collectives and lax.ppermute only.
A program may use at most 64 MiB of HBM per device.

```python
import math
import jax
import jax.numpy as jnp
import numpy as np
from jax import lax

VELOCITIES = 19
WET_CLASSES = 4
STEPS = 4
SLAB = 128
NX = 32
NY = 64


def draw_populations(key, part):
    key_density, key_jitter = jax.random.split(key, 2)
    weights = jnp.array([1.0 / 3.0] + [1.0 / 18.0] * 6 + [1.0 / 36.0] * 12, jnp.float32)
    jitter = jax.random.uniform(key_jitter, (VELOCITIES, NX, NY, SLAB), jnp.float32, -0.3, 0.3)
    density = jnp.exp(jax.random.uniform(key_density, (NX, NY, SLAB), jnp.float32, jnp.log(0.5), jnp.log(2.0)))
    return weights[:, None, None, None] * density[None] * (1.0 + jitter)


def place_ends(entries, rng, low, high):
    spot = [jax.random.randint(jax.random.fold_in(rng, axis), (), 0, length) for axis, length in enumerate(entries.shape)]
    widest = entries.shape.index(max(entries.shape))
    next_to = spot[:widest] + [(spot[widest] + 1) % entries.shape[widest]] + spot[widest + 1:]
    return entries.at[tuple(spot)].set(low).at[tuple(next_to)].set(high)


def setup_inputs(seed: int = 0, part: int = 0) -> dict:
    key_list = jax.random.split(jax.random.key(seed), 6)
    part_keys = jax.random.split(jax.random.fold_in(key_list[5], part), 6)
    populations = draw_populations(jax.random.fold_in(jax.random.fold_in(key_list[5], part), 71), part)
    fluid_mask = place_ends((jax.random.randint(part_keys[1], (NX, NY, SLAB), 0, 10) < 7).astype(jnp.int32), jax.random.fold_in(part_keys[1], 1), 0, 1)
    wet_class = place_ends(jax.random.randint(part_keys[2], (NX, NY, SLAB), 0, WET_CLASSES), jax.random.fold_in(part_keys[2], 1), 0, WET_CLASSES - 1).astype(jnp.int32)
    wall_potential = jnp.clip(jax.random.uniform(part_keys[3], (WET_CLASSES,), jnp.float32, 0.0, 1.0), 0.0, 1.0)
    relax_rates = jnp.clip(jnp.exp(jax.random.uniform(key_list[4], (VELOCITIES,), jnp.float32, math.log(0.8), math.log(1.6))), 0.8, 1.6)
    return {"populations": populations, "fluid_mask": fluid_mask, "wet_class": wet_class, "wall_potential": wall_potential, "relax_rates": relax_rates}


coupling = -2.5

def lattice():
    velocity_set = np.array([[0, 0, 0], [1, 0, 0], [-1, 0, 0], [0, 1, 0], [0, -1, 0], [0, 0, 1], [0, 0, -1], [1, 1, 0], [-1, -1, 0], [1, -1, 0], [-1, 1, 0], [1, 0, 1], [-1, 0, -1], [1, 0, -1], [-1, 0, 1], [0, 1, 1], [0, -1, -1], [0, 1, -1], [0, -1, 1]])
    weights = [1.0 / 3.0] + [1.0 / 18.0] * 6 + [1.0 / 36.0] * 12
    opposite = [0] + [index + 1 if index % 2 == 1 else index - 1 for index in range(1, 19)]
    lattice_vel = jnp.asarray(velocity_set, jnp.float32)
    along_x = lattice_vel[:, 0]
    along_y = lattice_vel[:, 1]
    along_z = lattice_vel[:, 2]
    moment_basis = jnp.stack([jnp.ones(19, jnp.float32), along_x, along_y, along_z, along_x * along_y, along_x * along_z, along_y * along_z, along_x * along_x, along_y * along_y, along_z * along_z, along_x * along_y * along_y, along_x * along_z * along_z, along_y * along_x * along_x, along_y * along_z * along_z, along_z * along_x * along_x, along_z * along_y * along_y, along_x * along_x * along_y * along_y, along_x * along_x * along_z * along_z, along_y * along_y * along_z * along_z])
    return (velocity_set, weights, opposite, moment_basis)

def collide_matrix(moment_basis, relax_rates):
    gram = jnp.dot(moment_basis, moment_basis.T, precision=lax.Precision.HIGHEST)
    factor = jnp.linalg.cholesky(gram)
    scaled = relax_rates[:, None] * moment_basis
    solved = jax.scipy.linalg.cho_solve((factor, True), scaled)
    return jnp.dot(moment_basis.T, solved, precision=lax.Precision.HIGHEST)

def collision(populations, fluid, potential, near_list, collide, velocity_set, weights):
    pull = [jnp.zeros_like(potential), jnp.zeros_like(potential), jnp.zeros_like(potential)]
    for index in range(1, 19):
        for column in range(3):
            if velocity_set[index][column] != 0:
                pull[column] = pull[column] + float(weights[index] * int(velocity_set[index][column])) * near_list[index]
    force = -coupling * potential[None] * jnp.stack(pull)
    density = jnp.sum(populations, axis=0)
    safe_density = jnp.where(fluid, density, 1.0)
    lattice_vel = jnp.asarray(velocity_set, jnp.float32)
    momentum = jnp.einsum('kc,kxyz->cxyz', lattice_vel, populations, precision=lax.Precision.HIGHEST)
    speed = (momentum + 0.5 * force) / safe_density[None]
    along = jnp.einsum('kc,cxyz->kxyz', lattice_vel, speed, precision=lax.Precision.HIGHEST)
    push = jnp.einsum('kc,cxyz->kxyz', lattice_vel, force, precision=lax.Precision.HIGHEST)
    speed_sq = jnp.sum(speed * speed, axis=0)
    speed_force = jnp.sum(speed * force, axis=0)
    weight_col = jnp.asarray(weights, jnp.float32)[:, None, None, None]
    equil = weight_col * safe_density[None] * (1.0 + 3.0 * along + 4.5 * along * along - 1.5 * speed_sq[None])
    source = weight_col * (3.0 * (push - speed_force[None]) + 9.0 * along * push)
    excess = populations - equil + 0.5 * source
    shape = populations.shape
    relaxed = jnp.dot(collide, excess.reshape(shape[0], -1), precision=lax.Precision.HIGHEST).reshape(shape)
    return (populations + source - relaxed, speed)

def reference(populations, fluid_mask, wet_class, wall_potential, relax_rates):
    velocity_set, weights, opposite, moment_basis = lattice()
    collide = collide_matrix(moment_basis, relax_rates)
    fluid = fluid_mask == 1
    classes = jnp.arange(WET_CLASSES, dtype=jnp.int32)[:, None, None, None]
    wall_values = jnp.sum(jnp.where(wet_class[None] == classes, wall_potential[:, None, None, None], 0.0), axis=0)
    shifts = [tuple((int(value) for value in velocity_set[index])) for index in range(19)]
    inflow = jnp.stack([jnp.roll(fluid, shifts[index], axis=(0, 1, 2)) for index in range(19)])
    speed = None
    for step in range(STEPS):
        density = jnp.sum(populations, axis=0)
        safe_density = jnp.where(fluid, density, 1.0)
        potential = jnp.where(fluid, 1.0 - jnp.exp(-safe_density), wall_values)
        near_list = [None] + [jnp.roll(potential, tuple((-value for value in shifts[index])), axis=(0, 1, 2)) for index in range(1, 19)]
        post, speed = collision(populations, fluid, potential, near_list, collide, velocity_set, weights)
        passed = jnp.stack([jnp.roll(post[index], shifts[index], axis=(0, 1, 2)) for index in range(19)])
        bounced = jnp.stack([post[opposite[index]] for index in range(19)])
        populations = jnp.where(fluid[None], jnp.where(inflow, passed, bounced), 0.0)
    velocity = jnp.where(fluid[None], speed, 0.0)
    return (populations, velocity)
```

```python
import functools

import jax
import jax.numpy as jnp
from jax import lax
from jax.experimental import pallas as pl
from jax.experimental.pallas import tpu as pltpu
from jax.sharding import PartitionSpec as P

STEPS = 4
STRENGTH = 2.5
VELOCITY = (
    (0, 0, 0),
    (1, 0, 0),
    (-1, 0, 0),
    (0, 1, 0),
    (0, -1, 0),
    (0, 0, 1),
    (0, 0, -1),
    (1, 1, 0),
    (-1, -1, 0),
    (1, -1, 0),
    (-1, 1, 0),
    (1, 0, 1),
    (-1, 0, -1),
    (1, 0, -1),
    (-1, 0, 1),
    (0, 1, 1),
    (0, -1, -1),
    (0, 1, -1),
    (0, -1, 1),
)
N = len(VELOCITY)
OPPOSITE = [0] + [k + 1 if k % 2 == 1 else k - 1 for k in range(1, N)]
RIGHT = [k for k in range(N) if VELOCITY[k][0] == 1]
LEFT = [k for k in range(N) if VELOCITY[k][0] == -1]
UP = [k for k in range(N) if VELOCITY[k][1] == 1]
DOWN = [k for k in range(N) if VELOCITY[k][1] == -1]
TILE = 8
PAD = 2 * TILE

C_UP, C_DN, H_UP, H_DN = 0, 1, 2, 3
RC_L, RC_R, G_L, G_R = 0, 1, 2, 3


def roll_z(value, step):
    if step == 0:
        return value
    return pltpu.roll(value, step % value.shape[-1], value.ndim - 1)


def total(values):
    values = list(values)
    while len(values) > 1:
        values = [
            values[i] + values[i + 1] if i + 1 < len(values) else values[i]
            for i in range(0, len(values), 2)
        ]
    return values[0]


def potential_of(density, fluid, solid_value):
    return jnp.where(fluid, 1.0 - jnp.exp(-density), solid_value)


def collide(f, fluid, force, rate):
    fx, fy, fz = force
    s = {k: f[k] + f[k + 1] for k in range(1, N, 2)}
    d = {k: f[k] - f[k + 1] for k in range(1, N, 2)}
    xxyy, xxzz, yyzz = s[7] + s[9], s[11] + s[13], s[15] + s[17]
    xy, xz, yz = s[7] - s[9], s[11] - s[13], s[15] - s[17]
    xyy, yxx = d[7] + d[9], d[7] - d[9]
    xzz, zxx = d[11] + d[13], d[11] - d[13]
    yzz, zyy = d[15] + d[17], d[15] - d[17]
    jx, jy, jz = d[1] + (xyy + xzz), d[3] + (yxx + yzz), d[5] + (zxx + zyy)
    xx, yy, zz = s[1] + (xxyy + xxzz), s[3] + (xxyy + yyzz), s[5] + (xxzz + yyzz)
    rho = (f[0] + s[1]) + (s[3] + s[5]) + (xxyy + (xxzz + yyzz))
    safe = jnp.where(fluid, rho, 1.0)
    inverse = 1.0 / safe
    hx, hy, hz = 0.5 * fx, 0.5 * fy, 0.5 * fz
    gx, gy, gz = jx + hx, jy + hy, jz + hz
    ux, uy, uz = gx * inverse, gy * inverse, gz * inverse
    third = safe * (1.0 / 3.0)
    ninth = safe * (1.0 / 9.0)
    px, py, pz = gx - fx, gy - fy, gz - fz
    txx, tyy, tzz = ux * px, uy * py, uz * pz
    sx, sy, sz = ux * fx, uy * fy, uz * fz
    pxy = ux * fy + uy * fx
    pxz = ux * fz + uz * fx
    pyz = uy * fz + uz * fy
    t3, s3 = (txx + tyy + tzz) * (1.0 / 3.0), (sx + sy + sz) * (2.0 / 3.0)
    rho = rho - rate(0) * (rho - safe)
    nx = jx + fx - rate(1) * (jx - safe * ux + hx)
    ny = jy + fy - rate(2) * (jy - safe * uy + hy)
    nz = jz + fz - rate(3) * (jz - safe * uz + hz)
    xy = xy + rate(4) * (gx * uy - 0.5 * pxy - xy) + pxy
    xz = xz + rate(5) * (gx * uz - 0.5 * pxz - xz) + pxz
    yz = yz + rate(6) * (gy * uz - 0.5 * pyz - yz) + pyz
    xx = xx + rate(7) * (third + txx - xx) + 2.0 * sx
    yy = yy + rate(8) * (third + tyy - yy) + 2.0 * sy
    zz = zz + rate(9) * (third + tzz - zz) + 2.0 * sz
    ex, ey, ez = jx * (1.0 / 3.0), jy * (1.0 / 3.0), jz * (1.0 / 3.0)
    qx, qy, qz = fx * (1.0 / 3.0), fy * (1.0 / 3.0), fz * (1.0 / 3.0)
    xyy = xyy + rate(10) * (ex - xyy) + qx
    xzz = xzz + rate(11) * (ex - xzz) + qx
    yxx = yxx + rate(12) * (ey - yxx) + qy
    yzz = yzz + rate(13) * (ey - yzz) + qy
    zxx = zxx + rate(14) * (ez - zxx) + qz
    zyy = zyy + rate(15) * (ez - zyy) + qz
    base = ninth + t3
    xxyy = xxyy + rate(16) * (base - 0.5 * tzz - xxyy) + (s3 - sz)
    xxzz = xxzz + rate(17) * (base - 0.5 * tyy - xxzz) + (s3 - sy)
    yyzz = yyzz + rate(18) * (base - 0.5 * txx - yyzz) + (s3 - sx)
    out = [None] * N
    for first, even, cross, odd1, odd2 in (
        (7, xxyy, xy, xyy, yxx),
        (11, xxzz, xz, xzz, zxx),
        (15, yyzz, yz, yzz, zyy),
    ):
        even, cross, odd1, odd2 = 0.25 * even, 0.25 * cross, 0.25 * odd1, 0.25 * odd2
        plus, minus = even + cross, even - cross
        both, diff = odd1 + odd2, odd1 - odd2
        out[first], out[first + 1] = plus + both, plus - both
        out[first + 2], out[first + 3] = minus + diff, minus - diff
    pairs = []
    for first, even, odd in (
        (1, xx - (xxyy + xxzz), nx - (xyy + xzz)),
        (3, yy - (xxyy + yyzz), ny - (yxx + yzz)),
        (5, zz - (xxzz + yyzz), nz - (zxx + zyy)),
    ):
        half_even, half_odd = 0.5 * even, 0.5 * odd
        out[first], out[first + 1] = half_even + half_odd, half_even - half_odd
        pairs.append(even)
    out[0] = rho - (pairs[0] + pairs[1] + pairs[2]) - (xxyy + xxzz + yyzz)
    return out, (ux, uy, uz)


def start_kernel(f_ref, mask_ref, wet_ref, wall_ref, pot_ref, right_ref, left_ref):
    size_x, size_y = mask_ref.shape[0], mask_ref.shape[1]
    for x in range(size_x):
        density = total([f_ref[k, x] for k in range(N)])
        wet = wet_ref[x]
        wall = jnp.zeros_like(density)
        for c in range(wall_ref.shape[0]):
            wall = jnp.where(wet == c, wall_ref[c], wall)
        pot_ref[x] = potential_of(density, mask_ref[x] == 1, wall)
    for ref, x in ((right_ref, size_x - 1), (left_ref, 0)):
        ref[:size_y] = pot_ref[x]
        ref[size_y:] = jnp.where(mask_ref[x] == 1, 1.0, 0.0)


def start_pack_kernel(pot_ref, mask_ref, from_left, from_right, up_ref, down_ref):
    size_x, size_y = mask_ref.shape[0], mask_ref.shape[1]
    for ref, y in ((up_ref, size_y - 1), (down_ref, 0)):
        ref[2 * size_x :] = jnp.zeros((TILE, ref.shape[1]), jnp.float32)
        for x in range(size_x):
            ref[x : x + 1] = pot_ref[x, y : y + 1]
            ref[size_x + x : size_x + x + 1] = jnp.where(mask_ref[x, y : y + 1] == 1, 1.0, 0.0)
        for i, side in enumerate((from_left, from_right)):
            row = 2 * size_x + i
            ref[row : row + 1] = side[y : y + 1]
            ref[row + 2 : row + 3] = side[size_y + y : size_y + y + 1]


def bits_kernel(mask_ref, x0l, x0r, y0d, y0u, bits_ref, pad_ref):
    size_x, size_y = mask_ref.shape[0], mask_ref.shape[1]
    for x in range(size_x):
        pad_ref[1 + x, TILE : TILE + size_y] = jnp.where(mask_ref[x] == 1, 1.0, 0.0)
    for x, side in ((0, x0l), (1 + size_x, x0r)):
        pad_ref[x, TILE : TILE + size_y] = side[size_y:]
    for y, side in ((TILE - 1, y0d), (TILE + size_y, y0u)):
        for x in range(size_x):
            pad_ref[1 + x, y : y + 1] = side[size_x + x : size_x + x + 1]
        for x, row in ((0, 2 * size_x + 2), (1 + size_x, 2 * size_x + 3)):
            pad_ref[x, y : y + 1] = side[row : row + 1]
    for x in range(size_x):
        for y in range(0, size_y, TILE):
            bits = jnp.zeros((TILE, mask_ref.shape[2]), jnp.int32)
            for k in range(N):
                ex, ey, ez = VELOCITY[k]
                row = TILE + y - ey
                source = roll_z(pad_ref[1 + x - ex, row : row + TILE], ez)
                bits = bits | jnp.where(source > 0.5, 1 << k, 0)
            bits_ref[x, y : y + TILE] = bits


def step_kernel(first, last, *refs):
    refs = list(refs)
    take = lambda count: [refs.pop(0) for _ in range(count)]
    rates, f_ref, bits_ref, pot0_ref, x0l, x0r, y0d, y0u = take(8)
    if not first:
        rho_ref, xl, xr, yd, yu, own_right, own_left, own_up, own_down = take(9)
    f_out, right_ref, left_ref, up_ref, down_ref = take(5)
    if last:
        speed_ref = take(1)[0]
    else:
        rho_out = take(1)[0]
    post, pot = take(2)
    size_x, size_y, size_z = bits_ref.shape
    blocks = [(x, y) for x in range(size_x) for y in range(0, size_y, TILE)]
    row_of = lax.broadcasted_iota(jnp.int32, (TILE, size_z), 0)

    def fluid_at(x, y):
        return (bits_ref[x, y : y + TILE] & 1) != 0

    nothing = jnp.zeros((TILE, size_z), jnp.float32)
    for k in UP:
        for x in range(size_x):
            post[k, x, :TILE] = nothing
    for k in DOWN:
        for x in range(size_x):
            post[k, x, TILE + size_y :] = nothing

    for x in range(size_x):
        if first:
            pot[1 + x, TILE : TILE + size_y] = pot0_ref[x]
            continue
        density = rho_ref[x]
        for at, side in ((0, xl), (size_x - 1, xr)):
            if x == at:
                density = density + total([side[j * size_y : (j + 1) * size_y] for j in range(5)])
        pot[1 + x, TILE : TILE + size_y] = density
    if first:
        for x, side in ((0, x0l), (1 + size_x, x0r)):
            pot[x, TILE : TILE + size_y] = side[:size_y]
        for y, side in ((TILE - 1, y0d), (TILE + size_y, y0u)):
            for x in range(size_x):
                pot[1 + x, y : y + 1] = side[x : x + 1]
            for x, row in ((0, 2 * size_x), (1 + size_x, 2 * size_x + 1)):
                pot[x, y : y + 1] = side[row : row + 1]
    else:
        end = 6 * size_x
        for y, side in ((TILE, yd), (TILE + size_y - 1, yu)):
            entering = total([side[j * size_x : (j + 1) * size_x] for j in range(5)])
            for x in range(size_x):
                pot[1 + x, y : y + 1] += entering[x : x + 1]
        for x in range(size_x):
            for y in range(0, size_y, TILE):
                rows = slice(TILE + y, 2 * TILE + y)
                pot[1 + x, rows] = potential_of(
                    pot[1 + x, rows], fluid_at(x, y), pot0_ref[x, y : y + TILE]
                )
        for x, side, own, side0, g in (
            (0, xl, own_left, x0l, G_L),
            (1 + size_x, xr, own_right, x0r, G_R),
        ):
            pot[x, TILE : TILE + size_y] = side[5 * size_y : 6 * size_y] + total(
                [own[j * size_y : (j + 1) * size_y] for j in range(5)]
            )
            for y, row in ((TILE, yd), (TILE + size_y - 1, yu)):
                pot[x, y : y + 1] += row[end + g : end + g + 1]
            for y in range(0, size_y, TILE):
                rows = slice(TILE + y, 2 * TILE + y)
                pot[x, rows] = potential_of(
                    pot[x, rows],
                    side0[size_y + y : size_y + y + TILE] > 0.5,
                    side0[y : y + TILE],
                )
        for y, side, own, side0 in (
            (TILE - 1, yd, own_down, y0d),
            (TILE + size_y, yu, own_up, y0u),
        ):
            density = side[5 * size_x : 6 * size_x] + total(
                [own[j * size_x : (j + 1) * size_x] for j in range(5)]
            )
            value = potential_of(density, side0[size_x : 2 * size_x] > 0.5, side0[:size_x])
            for x in range(size_x):
                pot[1 + x, y : y + 1] = value[x : x + 1]
            for x, rc, g, i in ((0, RC_L, G_L, 0), (1 + size_x, RC_R, G_R, 1)):
                density = side[end + rc : end + rc + 1] + own[end + g : end + g + 1]
                row = 2 * size_x + i
                pot[x, y : y + 1] = potential_of(
                    density, side0[row + 2 : row + 3] > 0.5, side0[row : row + 1]
                )

    for x, y in blocks:
        near = {
            (i, j): pot[1 + x + i, TILE + y + j : 2 * TILE + y + j]
            for i in (-1, 0, 1)
            for j in (-1, 0, 1)
        }
        scale = near[0, 0] * (STRENGTH / 36.0)
        dx = near[1, 0] - near[-1, 0]
        dy = near[0, 1] - near[0, -1]
        pp, pm, mp, mm = near[1, 1], near[1, -1], near[-1, 1], near[-1, -1]
        both = near[1, 0] + near[-1, 0] + near[0, 1] + near[0, -1] + 2.0 * near[0, 0]
        diag1, diag2 = pp - mm, pm - mp
        force = (
            scale * (2.0 * dx + (diag1 + diag2) + (roll_z(dx, 1) + roll_z(dx, -1))),
            scale * (2.0 * dy + (diag1 - diag2) + (roll_z(dy, 1) + roll_z(dy, -1))),
            scale * (roll_z(both, -1) - roll_z(both, 1)),
        )
        f = [f_ref[k, x, y : y + TILE] for k in range(N)]
        if not first:
            for at, side, ks in ((0, xl, RIGHT), (size_x - 1, xr, LEFT)):
                if x == at:
                    for j, k in enumerate(ks):
                        f[k] = f[k] + side[j * size_y + y : j * size_y + y + TILE]
            for at, side, ks in ((0, yd, UP), (size_y - 1, yu, DOWN)):
                if y <= at < y + TILE:
                    for j, k in enumerate(ks):
                        entering = side[j * size_x + x : j * size_x + x + 1]
                        f[k] = f[k] + jnp.where(row_of == at - y, entering, 0.0)
        fluid = fluid_at(x, y)
        after, speed = collide(f, fluid, force, lambda r: rates[r])
        for k in range(N):
            post[k, x, TILE + y : 2 * TILE + y] = jnp.where(fluid, after[k], 0.0)
        if last:
            for c in range(3):
                speed_ref[c, x, y : y + TILE] = jnp.where(fluid, speed[c], 0.0)

    for x, y in blocks:
        bits = bits_ref[x, y : y + TILE]
        arrived = []
        for k in range(N):
            ex, ey, ez = VELOCITY[k]
            own = post[OPPOSITE[k], x, TILE + y : 2 * TILE + y]
            if k == 0:
                value = own
            else:
                come = 0.0
                if 0 <= x - ex < size_x:
                    row = TILE + y - ey
                    come = roll_z(post[k, x - ex, row : row + TILE], ez)
                value = jnp.where((bits & (1 << k)) != 0, come, own)
            f_out[k, x, y : y + TILE] = value
            arrived.append(value)
        if not last:
            rho_out[x, y : y + TILE] = total(arrived)

    parts = 5 if last else 6
    for ref, x, ks in ((right_ref, size_x - 1, RIGHT), (left_ref, 0, LEFT)):
        for j, k in enumerate(ks):
            _, ey, ez = VELOCITY[k]
            for y in range(0, size_y, TILE):
                row = TILE + y - ey
                ref[j * size_y + y : j * size_y + y + TILE] = roll_z(
                    post[k, x, row : row + TILE], ez
                )
        if not last:
            ref[5 * size_y : 6 * size_y] = rho_out[x]
    for ref, y, ks in ((up_ref, size_y - 1, UP), (down_ref, 0, DOWN)):
        sums = []
        for j, k in enumerate(ks):
            ex, _, ez = VELOCITY[k]
            for x in range(size_x):
                row = j * size_x + x
                if 0 <= x - ex < size_x:
                    ref[row : row + 1] = post[k, x - ex, TILE + y : TILE + y + 1]
                else:
                    ref[row : row + 1] = nothing[:1]
            if ez != 0:
                rows = slice(j * size_x, (j + 1) * size_x)
                ref[rows] = roll_z(ref[rows], ez)
        if not last:
            for x in range(size_x):
                ref[5 * size_x + x : 5 * size_x + x + 1] = rho_out[x, y : y + 1]
    for ref, x, dirs in ((right_ref, size_x - 1, (7, 9)), (left_ref, 0, (10, 8))):
        at = parts * size_y
        ref[at : at + TILE] = nothing
        ref[at + C_UP : at + C_UP + 1] = post[dirs[0], x, TILE + size_y - 1 : TILE + size_y]
        ref[at + C_DN : at + C_DN + 1] = post[dirs[1], x, TILE : TILE + 1]
        if not last:
            for h, y_ref in ((H_UP, up_ref), (H_DN, down_ref)):
                ref[at + h : at + h + 1] = total(
                    [y_ref[j * size_x + x : j * size_x + x + 1] for j in range(5)]
                )


def pack_kernel(last, size_x, size_y, up_in, down_in, xl, xr, own_right, own_left, up_ref, down_ref):
    parts = 5 if last else 6
    at = parts * size_y
    for ref, source, y, ks, c, h in (
        (up_ref, up_in, size_y - 1, UP, C_UP, H_UP),
        (down_ref, down_in, 0, DOWN, C_DN, H_DN),
    ):
        ref[: parts * size_x] = source[: parts * size_x]
        for side, own, x, ex, rc, g in (
            (xl, own_left, 0, 1, RC_L, G_L),
            (xr, own_right, size_x - 1, -1, RC_R, G_R),
        ):
            j = [i for i, k in enumerate(ks) if VELOCITY[k][0] == ex][0]
            row = j * size_x + x
            ref[row : row + 1] = side[at + c : at + c + 1]
            if not last:
                row = 5 * size_x + x
                ref[row : row + 1] = source[row : row + 1] + total(
                    [side[i * size_y + y : i * size_y + y + 1] for i in range(5)]
                )
                row = 6 * size_x
                ref[row + rc : row + rc + 1] = side[5 * size_y + y : 5 * size_y + y + 1] + total(
                    [own[i * size_y + y : i * size_y + y + 1] for i in range(5)]
                )
                ref[row + g : row + g + 1] = (
                    side[at + h : at + h + 1] + own[at + c : at + c + 1]
                )


def end_kernel(f_ref, bits_ref, xl, xr, yd, yu, out_ref):
    size_x, size_y, size_z = bits_ref.shape
    row_of = lax.broadcasted_iota(jnp.int32, (TILE, size_z), 0)
    for x in range(size_x):
        for y in range(0, size_y, TILE):
            fluid = (bits_ref[x, y : y + TILE] & 1) != 0
            for k in range(N):
                value = f_ref[k, x, y : y + TILE]
                for at, side, ks in ((0, xl, RIGHT), (size_x - 1, xr, LEFT)):
                    if x == at and k in ks:
                        row = ks.index(k) * size_y + y
                        value = value + side[row : row + TILE]
                for at, side, ks in ((0, yd, UP), (size_y - 1, yu, DOWN)):
                    if y <= at < y + TILE and k in ks:
                        row = ks.index(k) * size_x + x
                        value = value + jnp.where(row_of == at - y, side[row : row + 1], 0.0)
                out_ref[k, x, y : y + TILE] = jnp.where(fluid, value, 0.0)


VMEM = pl.BlockSpec(memory_space=pltpu.VMEM)
SMEM = pl.BlockSpec(memory_space=pltpu.SMEM)


def call(kernel, outs, args, smem=(), scratch=(), **kwargs):
    return pl.pallas_call(
        kernel,
        out_shape=[jax.ShapeDtypeStruct(shape, dtype) for shape, dtype in outs],
        in_specs=[SMEM if i in smem else VMEM for i in range(len(args))],
        out_specs=[VMEM] * len(outs),
        scratch_shapes=[pltpu.VMEM(shape, jnp.float32) for shape in scratch],
        compiler_params=pltpu.CompilerParams(vmem_limit_bytes=16 * 2**20),
        **kwargs,
    )(*args)


def shift(forward, backward, axis):
    count = lax.axis_size(axis)
    ahead = [(i, (i + 1) % count) for i in range(count)]
    return (
        lax.ppermute(forward, axis, ahead),
        lax.ppermute(backward, axis, [(b, a) for a, b in ahead]),
    )


def per_device(populations, fluid_mask, wet_class, wall_potential, relax_rates):
    size_x, size_y, size_z = fluid_mask.shape
    f32, i32 = jnp.float32, jnp.int32
    whole = ((size_x, size_y, size_z), f32)
    fields = ((N, size_x, size_y, size_z), f32)
    rows = lambda count: ((count, size_z), f32)

    pot0, right, left = call(
        start_kernel,
        [whole, rows(2 * size_y), rows(2 * size_y)],
        (populations, fluid_mask, wet_class, wall_potential),
        smem=(3,),
    )
    x0l, x0r = shift(right, left, "gx")
    up, down = call(
        start_pack_kernel, [rows(2 * size_x + TILE)] * 2, (pot0, fluid_mask, x0l, x0r)
    )
    y0d, y0u = shift(up, down, "gy")
    padded = (size_x + 2, size_y + PAD, size_z)
    (bits,) = call(
        bits_kernel,
        [((size_x, size_y, size_z), i32)],
        (fluid_mask, x0l, x0r, y0d, y0u),
        scratch=[padded],
    )
    f, carried = populations, ()
    for step in range(STEPS):
        first, last = step == 0, step == STEPS - 1
        parts = 5 if last else 6
        x_rows, y_rows = rows(parts * size_y + TILE), rows(parts * size_x + (0 if last else TILE))
        outs = [fields, x_rows, x_rows, y_rows, y_rows]
        outs.append(((3, size_x, size_y, size_z), f32) if last else whole)
        f, right, left, up, down, extra = call(
            functools.partial(step_kernel, first, last),
            outs,
            (relax_rates, f, bits, pot0, x0l, x0r, y0d, y0u, *carried),
            smem=(0,),
            scratch=[(N, size_x, size_y + PAD, size_z), padded],
        )
        xl, xr = shift(right, left, "gx")
        up, down = call(
            functools.partial(pack_kernel, last, size_x, size_y),
            [y_rows, y_rows],
            (up, down, xl, xr, right, left),
        )
        yd, yu = shift(up, down, "gy")
        carried = (extra, xl, xr, yd, yu, right, left, up, down)
    (out,) = call(end_kernel, [fields], (f, bits, xl, xr, yd, yu))
    return out, extra


def solution(mesh):
    return jax.shard_map(
        per_device,
        mesh=mesh,
        in_specs=(
            P(None, ("groups", "gx"), "gy", None),
            P(("groups", "gx"), "gy", None),
            P(("groups", "gx"), "gy", None),
            P("groups"),
            P(),
        ),
        out_specs=(P(None, ("groups", "gx"), "gy", None), P(None, ("groups", "gx"), "gy", None)),
        check_vma=False,
    )
```

```python
import functools

import jax
import jax.numpy as jnp
from jax import lax
from jax.experimental import pallas as pl
from jax.experimental.pallas import tpu as pltpu
from jax.sharding import PartitionSpec as P

STEPS = 4
STRENGTH = 2.5
VELOCITY = (
    (0, 0, 0),
    (1, 0, 0),
    (-1, 0, 0),
    (0, 1, 0),
    (0, -1, 0),
    (0, 0, 1),
    (0, 0, -1),
    (1, 1, 0),
    (-1, -1, 0),
    (1, -1, 0),
    (-1, 1, 0),
    (1, 0, 1),
    (-1, 0, -1),
    (1, 0, -1),
    (-1, 0, 1),
    (0, 1, 1),
    (0, -1, -1),
    (0, 1, -1),
    (0, -1, 1),
)
N = len(VELOCITY)
OPPOSITE = [0] + [k + 1 if k % 2 == 1 else k - 1 for k in range(1, N)]
RIGHT = [k for k in range(N) if VELOCITY[k][0] == 1]
LEFT = [k for k in range(N) if VELOCITY[k][0] == -1]
UP = [k for k in range(N) if VELOCITY[k][1] == 1]
DOWN = [k for k in range(N) if VELOCITY[k][1] == -1]
TILE = 8
PAD = 2 * TILE

C_UP, C_DN, H_UP, H_DN = 0, 1, 2, 3
RC_L, RC_R, G_L, G_R = 0, 1, 2, 3


def roll_z(value, step):
    if step == 0:
        return value
    return pltpu.roll(value, step % value.shape[-1], value.ndim - 1)


def total(values):
    values = list(values)
    while len(values) > 1:
        values = [
            values[i] + values[i + 1] if i + 1 < len(values) else values[i]
            for i in range(0, len(values), 2)
        ]
    return values[0]


def potential_of(density, fluid, solid_value):
    return jnp.where(fluid, 1.0 - jnp.exp(-density), solid_value)


def collide(f, fluid, force, rate):
    fx, fy, fz = force
    s = {k: f[k] + f[k + 1] for k in range(1, N, 2)}
    d = {k: f[k] - f[k + 1] for k in range(1, N, 2)}
    xxyy, xxzz, yyzz = s[7] + s[9], s[11] + s[13], s[15] + s[17]
    xy, xz, yz = s[7] - s[9], s[11] - s[13], s[15] - s[17]
    xyy, yxx = d[7] + d[9], d[7] - d[9]
    xzz, zxx = d[11] + d[13], d[11] - d[13]
    yzz, zyy = d[15] + d[17], d[15] - d[17]
    jx, jy, jz = d[1] + (xyy + xzz), d[3] + (yxx + yzz), d[5] + (zxx + zyy)
    xx, yy, zz = s[1] + (xxyy + xxzz), s[3] + (xxyy + yyzz), s[5] + (xxzz + yyzz)
    rho = (f[0] + s[1]) + (s[3] + s[5]) + (xxyy + (xxzz + yyzz))
    safe = jnp.where(fluid, rho, 1.0)
    inverse = 1.0 / safe
    hx, hy, hz = 0.5 * fx, 0.5 * fy, 0.5 * fz
    gx, gy, gz = jx + hx, jy + hy, jz + hz
    ux, uy, uz = gx * inverse, gy * inverse, gz * inverse
    third = safe * (1.0 / 3.0)
    ninth = safe * (1.0 / 9.0)
    px, py, pz = gx - fx, gy - fy, gz - fz
    txx, tyy, tzz = ux * px, uy * py, uz * pz
    sx, sy, sz = ux * fx, uy * fy, uz * fz
    pxy = ux * fy + uy * fx
    pxz = ux * fz + uz * fx
    pyz = uy * fz + uz * fy
    t3, s3 = (txx + tyy + tzz) * (1.0 / 3.0), (sx + sy + sz) * (2.0 / 3.0)
    rho = rho - rate(0) * (rho - safe)
    nx = jx + fx - rate(1) * (jx - safe * ux + hx)
    ny = jy + fy - rate(2) * (jy - safe * uy + hy)
    nz = jz + fz - rate(3) * (jz - safe * uz + hz)
    xy = xy + rate(4) * (gx * uy - 0.5 * pxy - xy) + pxy
    xz = xz + rate(5) * (gx * uz - 0.5 * pxz - xz) + pxz
    yz = yz + rate(6) * (gy * uz - 0.5 * pyz - yz) + pyz
    xx = xx + rate(7) * (third + txx - xx) + 2.0 * sx
    yy = yy + rate(8) * (third + tyy - yy) + 2.0 * sy
    zz = zz + rate(9) * (third + tzz - zz) + 2.0 * sz
    ex, ey, ez = jx * (1.0 / 3.0), jy * (1.0 / 3.0), jz * (1.0 / 3.0)
    qx, qy, qz = fx * (1.0 / 3.0), fy * (1.0 / 3.0), fz * (1.0 / 3.0)
    xyy = xyy + rate(10) * (ex - xyy) + qx
    xzz = xzz + rate(11) * (ex - xzz) + qx
    yxx = yxx + rate(12) * (ey - yxx) + qy
    yzz = yzz + rate(13) * (ey - yzz) + qy
    zxx = zxx + rate(14) * (ez - zxx) + qz
    zyy = zyy + rate(15) * (ez - zyy) + qz
    base = ninth + t3
    xxyy = xxyy + rate(16) * (base - 0.5 * tzz - xxyy) + (s3 - sz)
    xxzz = xxzz + rate(17) * (base - 0.5 * tyy - xxzz) + (s3 - sy)
    yyzz = yyzz + rate(18) * (base - 0.5 * txx - yyzz) + (s3 - sx)
    out = [None] * N
    for first, even, cross, odd1, odd2 in (
        (7, xxyy, xy, xyy, yxx),
        (11, xxzz, xz, xzz, zxx),
        (15, yyzz, yz, yzz, zyy),
    ):
        even, cross, odd1, odd2 = 0.25 * even, 0.25 * cross, 0.25 * odd1, 0.25 * odd2
        plus, minus = even + cross, even - cross
        both, diff = odd1 + odd2, odd1 - odd2
        out[first], out[first + 1] = plus + both, plus - both
        out[first + 2], out[first + 3] = minus + diff, minus - diff
    pairs = []
    for first, even, odd in (
        (1, xx - (xxyy + xxzz), nx - (xyy + xzz)),
        (3, yy - (xxyy + yyzz), ny - (yxx + yzz)),
        (5, zz - (xxzz + yyzz), nz - (zxx + zyy)),
    ):
        half_even, half_odd = 0.5 * even, 0.5 * odd
        out[first], out[first + 1] = half_even + half_odd, half_even - half_odd
        pairs.append(even)
    out[0] = rho - (pairs[0] + pairs[1] + pairs[2]) - (xxyy + xxzz + yyzz)
    return out, (ux, uy, uz)


def start_kernel(f_hbm, mask_hbm, wet_hbm, wall_hbm, f_ref, mask_ref, pot_ref, right_ref, left_ref, *scratch):
    mask_in, wet_in, wall_in, f_sems, sems = scratch
    size_x, size_y = mask_ref.shape[0], mask_ref.shape[1]
    small = [
        pltpu.make_async_copy(source, target, sems.at[i])
        for i, (source, target) in enumerate(
            ((wall_hbm, wall_in), (mask_hbm, mask_in), (wet_hbm, wet_in))
        )
    ]
    large = [pltpu.make_async_copy(f_hbm.at[k], f_ref.at[k], f_sems.at[k]) for k in range(N)]
    for copy in small + large:
        copy.start()
    for copy in small:
        copy.wait()
    for x in range(size_x):
        wet = wet_in[x]
        wall = jnp.zeros(wet.shape, jnp.float32)
        for c in range(wall_in.shape[0]):
            wall = jnp.where(wet == c, wall_in[c], wall)
        pot_ref[x] = wall
        mask_ref[x] = jnp.where(mask_in[x] == 1, 1.0, 0.0)
    for copy in large:
        copy.wait()
    for x in range(size_x):
        density = total([f_ref[k, x] for k in range(N)])
        pot_ref[x] = potential_of(density, mask_ref[x] > 0.5, pot_ref[x])
    for ref, x in ((right_ref, size_x - 1), (left_ref, 0)):
        ref[:size_y] = pot_ref[x]
        ref[size_y:] = mask_ref[x]


def start_pack_kernel(pairs, pot_ref, mask_ref, from_left, from_right, a_ref, b_ref, up_ref, down_ref):
    size_x, size_y = mask_ref.shape[0], mask_ref.shape[1]
    for ref, y in ((up_ref, size_y - 1), (down_ref, 0)):
        ref[2 * size_x :] = jnp.zeros((TILE, ref.shape[1]), jnp.float32)
        for x in range(size_x):
            ref[x : x + 1] = pot_ref[x, y : y + 1]
            ref[size_x + x : size_x + x + 1] = mask_ref[x, y : y + 1]
        for i, side in enumerate((from_left, from_right)):
            row = 2 * size_x + i
            ref[row : row + 1] = side[y : y + 1]
            ref[row + 2 : row + 3] = side[size_y + y : size_y + y + 1]
    to_pairs(pairs, up_ref, down_ref, a_ref, b_ref)


def to_pairs(pairs, up_ref, down_ref, a_ref, b_ref):
    up, down = up_ref[...], down_ref[...]
    if not pairs:
        a_ref[...], b_ref[...] = up, down
        return
    odd = lax.axis_index("gy") % 2 == 1
    a_ref[...] = jnp.where(odd, down, up)
    b_ref[...] = jnp.where(odd, up, down)


def from_pairs(pairs, a_ref, b_ref, below_ref, above_ref):
    a, b = a_ref[...], b_ref[...]
    if not pairs:
        below_ref[...], above_ref[...] = a, b
        return
    odd = lax.axis_index("gy") % 2 == 1
    below_ref[...] = jnp.where(odd, a, b)
    above_ref[...] = jnp.where(odd, b, a)


def bits_kernel(pairs, mask_ref, x0l, x0r, a_ref, b_ref, bits_ref, y0d, y0u, pad_ref):
    size_x, size_y = mask_ref.shape[0], mask_ref.shape[1]
    from_pairs(pairs, a_ref, b_ref, y0d, y0u)
    for x in range(size_x):
        pad_ref[1 + x, TILE : TILE + size_y] = mask_ref[x]
    for x, side in ((0, x0l), (1 + size_x, x0r)):
        pad_ref[x, TILE : TILE + size_y] = side[size_y:]
    for y, side in ((TILE - 1, y0d), (TILE + size_y, y0u)):
        for x in range(size_x):
            pad_ref[1 + x, y : y + 1] = side[size_x + x : size_x + x + 1]
        for x, row in ((0, 2 * size_x + 2), (1 + size_x, 2 * size_x + 3)):
            pad_ref[x, y : y + 1] = side[row : row + 1]
    for x in range(size_x):
        for y in range(0, size_y, TILE):
            bits = jnp.zeros((TILE, mask_ref.shape[2]), jnp.int32)
            for k in range(N):
                ex, ey, ez = VELOCITY[k]
                row = TILE + y - ey
                source = roll_z(pad_ref[1 + x - ex, row : row + TILE], ez)
                bits = bits | jnp.where(source > 0.5, 1 << k, 0)
            bits_ref[x, y : y + TILE] = bits


class Layers:
    def __init__(self, edge_ref, middle_ref, size_x, edge):
        self.where = {}
        middle = [x for x in range(size_x) if x not in edge]
        for ref, xs in ((edge_ref, edge), (middle_ref, middle)):
            for i, x in enumerate(xs):
                self.where[x] = (ref, i)

    def load(self, x, y, k=None):
        ref, i = self.where[x]
        return ref[i, y : y + TILE] if k is None else ref[k, i, y : y + TILE]

    def row(self, x, y, k=None):
        ref, i = self.where[x]
        return ref[i, y : y + 1] if k is None else ref[k, i, y : y + 1]

    def store(self, x, y, value, k=None):
        ref, i = self.where[x]
        if k is None:
            ref[i, y : y + TILE] = value
        else:
            ref[k, i, y : y + TILE] = value


def two_layers(size_x):
    return [0, 1, size_x - 2, size_x - 1]


def one_layer(size_x):
    return [0, size_x - 1]


def fluid_at(bits_ref, x, y):
    return (bits_ref[x, y : y + TILE] & 1) != 0


def clear_outside(post, layers, size_y):
    nothing = jnp.zeros((TILE, post.shape[-1]), jnp.float32)
    for i in range(layers):
        for k in UP:
            post[k, i, :TILE] = nothing
        for k in DOWN:
            post[k, i, TILE + size_y :] = nothing


def collide_layers(xs, rates, f, bits_ref, pot, sides, post, speed):
    size_x, size_y, size_z = bits_ref.shape
    row_of = lax.broadcasted_iota(jnp.int32, (TILE, size_z), 0)
    for x in xs:
        for y in range(0, size_y, TILE):
            near = {
                (i, j): pot[1 + x + i, TILE + y + j : 2 * TILE + y + j]
                for i in (-1, 0, 1)
                for j in (-1, 0, 1)
            }
            scale = near[0, 0] * (STRENGTH / 36.0)
            dx = near[1, 0] - near[-1, 0]
            dy = near[0, 1] - near[0, -1]
            pp, pm, mp, mm = near[1, 1], near[1, -1], near[-1, 1], near[-1, -1]
            both = near[1, 0] + near[-1, 0] + near[0, 1] + near[0, -1] + 2.0 * near[0, 0]
            diag1, diag2 = pp - mm, pm - mp
            force = (
                scale * (2.0 * dx + (diag1 + diag2) + (roll_z(dx, 1) + roll_z(dx, -1))),
                scale * (2.0 * dy + (diag1 - diag2) + (roll_z(dy, 1) + roll_z(dy, -1))),
                scale * (roll_z(both, -1) - roll_z(both, 1)),
            )
            now = [f(k, x, y) for k in range(N)]
            if sides is not None:
                xl, xr, yd, yu = sides
                for at, side, ks in ((0, xl, RIGHT), (size_x - 1, xr, LEFT)):
                    if x == at:
                        for j, k in enumerate(ks):
                            now[k] = now[k] + side[j * size_y + y : j * size_y + y + TILE]
                for at, side, ks in ((0, yd, UP), (size_y - 1, yu, DOWN)):
                    if y <= at < y + TILE:
                        for j, k in enumerate(ks):
                            entering = side[j * size_x + x : j * size_x + x + 1]
                            now[k] = now[k] + jnp.where(row_of == at - y, entering, 0.0)
            fluid = fluid_at(bits_ref, x, y)
            after, at_speed = collide(now, fluid, force, lambda r: rates[r])
            for k in range(N):
                post.store(x, TILE + y, jnp.where(fluid, after[k], 0.0), k)
            if speed is not None:
                for c in range(3):
                    speed.store(x, y, jnp.where(fluid, at_speed[c], 0.0), c)


def stream_layers(xs, bits_ref, post, f, rho):
    size_x, size_y, _ = bits_ref.shape
    for x in xs:
        for y in range(0, size_y, TILE):
            bits = bits_ref[x, y : y + TILE]
            arrived = []
            for k in range(N):
                ex, ey, ez = VELOCITY[k]
                value = post.load(x, TILE + y, OPPOSITE[k])
                if k > 0:
                    come = 0.0
                    if 0 <= x - ex < size_x:
                        come = roll_z(post.load(x - ex, TILE + y - ey, k), ez)
                    value = jnp.where((bits & (1 << k)) != 0, come, value)
                f.store(x, y, value, k)
                arrived.append(value)
            if rho is not None:
                rho.store(x, y, total(arrived))


def edge_kernel(first, last, pairs, *refs):
    refs = list(refs)
    take = lambda count: [refs.pop(0) for _ in range(count)]
    rates, bits_ref, pot0_ref, x0l, x0r, y0d, y0u = take(7)
    if first:
        f_ref = take(1)[0]
    else:
        f_edge, f_middle, rho_edge, rho_middle, xl, xr, ya, yb = take(8)
        own_right, own_left, own_a, own_b = take(4)
    pot, post_out, f_out, right_ref, left_ref = take(5)
    rest = take(1)[0]
    size_x, size_y, size_z = bits_ref.shape
    edge2, edge1 = two_layers(size_x), one_layer(size_x)
    sides = None
    if first:
        f = lambda k, x, y: f_ref[k, x, y : y + TILE]
    else:
        yd, yu, own_down, own_up = take(4)
        from_pairs(pairs, ya, yb, yd, yu)
        if pairs:
            from_pairs(pairs, own_a, own_b, own_down, own_up)
        else:
            own_down, own_up = own_b, own_a
        sides = (xl, xr, yd, yu)
        held = Layers(f_edge, f_middle, size_x, edge1)
        density_of = Layers(rho_edge, rho_middle, size_x, edge1)
        f = lambda k, x, y: held.load(x, y, k)
    clear_outside(post_out, len(edge2), size_y)

    if first:
        for x in range(size_x):
            pot[1 + x, TILE : TILE + size_y] = pot0_ref[x]
        for x, side in ((0, x0l), (1 + size_x, x0r)):
            pot[x, TILE : TILE + size_y] = side[:size_y]
        for y, side in ((TILE - 1, y0d), (TILE + size_y, y0u)):
            for x in range(size_x):
                pot[1 + x, y : y + 1] = side[x : x + 1]
            for x, row in ((0, 2 * size_x), (1 + size_x, 2 * size_x + 1)):
                pot[x, y : y + 1] = side[row : row + 1]
    else:
        end = 6 * size_x
        row_of = lax.broadcasted_iota(jnp.int32, (TILE, size_z), 0)
        entering = {
            at: total([side[j * size_x : (j + 1) * size_x] for j in range(5)])
            for at, side in ((0, yd), (size_y - 1, yu))
        }
        for x in range(size_x):
            for y in range(0, size_y, TILE):
                density = density_of.load(x, y)
                for at, side in ((0, xl), (size_x - 1, xr)):
                    if x == at:
                        density = density + total(
                            [side[j * size_y + y : j * size_y + y + TILE] for j in range(5)]
                        )
                for at, rows in entering.items():
                    if y <= at < y + TILE:
                        density = density + jnp.where(row_of == at - y, rows[x : x + 1], 0.0)
                pot[1 + x, TILE + y : 2 * TILE + y] = potential_of(
                    density, fluid_at(bits_ref, x, y), pot0_ref[x, y : y + TILE]
                )
        for x, side, own, side0, g in (
            (0, xl, own_left, x0l, G_L),
            (1 + size_x, xr, own_right, x0r, G_R),
        ):
            for y in range(0, size_y, TILE):
                density = side[5 * size_y + y : 5 * size_y + y + TILE] + total(
                    [own[j * size_y + y : j * size_y + y + TILE] for j in range(5)]
                )
                for at, row in ((0, yd), (size_y - 1, yu)):
                    if y <= at < y + TILE:
                        more = row[end + g : end + g + 1]
                        density = density + jnp.where(row_of == at - y, more, 0.0)
                pot[x, TILE + y : 2 * TILE + y] = potential_of(
                    density,
                    side0[size_y + y : size_y + y + TILE] > 0.5,
                    side0[y : y + TILE],
                )
        for y, side, own, side0 in (
            (TILE - 1, yd, own_down, y0d),
            (TILE + size_y, yu, own_up, y0u),
        ):
            density = side[5 * size_x : 6 * size_x] + total(
                [own[j * size_x : (j + 1) * size_x] for j in range(5)]
            )
            value = potential_of(density, side0[size_x : 2 * size_x] > 0.5, side0[:size_x])
            for x in range(size_x):
                pot[1 + x, y : y + 1] = value[x : x + 1]
            for x, rc, g, i in ((0, RC_L, G_L, 0), (1 + size_x, RC_R, G_R, 1)):
                density = side[end + rc : end + rc + 1] + own[end + g : end + g + 1]
                row = 2 * size_x + i
                pot[x, y : y + 1] = potential_of(
                    density, side0[row + 2 : row + 3] > 0.5, side0[row : row + 1]
                )

    post = Layers(post_out, None, size_x, edge2)
    speed = Layers(rest, None, size_x, edge2) if last else None
    collide_layers(edge2, rates, f, bits_ref, pot, sides, post, speed)
    rho = None if last else Layers(rest, None, size_x, edge1)
    stream_layers(edge1, bits_ref, post, Layers(f_out, None, size_x, edge1), rho)

    at = (5 if last else 6) * size_y
    for i, (ref, x, ks, dirs) in enumerate(
        ((left_ref, 0, LEFT, (10, 8)), (right_ref, size_x - 1, RIGHT, (7, 9)))
    ):
        for j, k in enumerate(ks):
            _, ey, ez = VELOCITY[k]
            for y in range(0, size_y, TILE):
                row = j * size_y + y
                ref[row : row + TILE] = roll_z(post.load(x, TILE + y - ey, k), ez)
        ref[at : at + TILE] = jnp.zeros((TILE, size_z), jnp.float32)
        ref[at + C_UP : at + C_UP + 1] = post.row(x, TILE + size_y - 1, dirs[0])
        ref[at + C_DN : at + C_DN + 1] = post.row(x, TILE, dirs[1])
        if not last:
            ref[5 * size_y : 6 * size_y] = rest[i]
            for h, y, leave in ((H_UP, size_y - 1, UP), (H_DN, 0, DOWN)):
                ref[at + h : at + h + 1] = total(
                    [
                        roll_z(post.row(x - VELOCITY[k][0], TILE + y, k), VELOCITY[k][2])
                        for k in leave
                        if 0 <= x - VELOCITY[k][0] < size_x
                    ]
                )


def middle_kernel(first, last, pairs, *refs):
    refs = list(refs)
    take = lambda count: [refs.pop(0) for _ in range(count)]
    rates, bits_ref, pot, post_edge, edge_rest = take(5)
    if first:
        f_ref = take(1)[0]
    else:
        f_edge, f_middle, ya, yb = take(4)
    f_out, up_ref, down_ref, rest = take(4)
    post_middle = take(1)[0]
    size_x, size_y, size_z = bits_ref.shape
    edge2, edge1 = two_layers(size_x), one_layer(size_x)
    sides = None
    if first:
        f = lambda k, x, y: f_ref[k, x, y : y + TILE]
    else:
        yd, yu = take(2)
        from_pairs(pairs, ya, yb, yd, yu)
        sides = (None, None, yd, yu)
        held = Layers(f_edge, f_middle, size_x, edge1)
        f = lambda k, x, y: held.load(x, y, k)
    clear_outside(post_middle, size_x - len(edge2), size_y)
    post = Layers(post_edge, post_middle, size_x, edge2)
    speed = None
    if last:
        speed = Layers(None, None, size_x, [])
        speed.where = {x: (rest, x) for x in range(size_x)}
        for c in range(3):
            for i, x in enumerate(edge2):
                rest[c, x] = edge_rest[c, i]
    inner = [x for x in range(size_x) if x not in edge2]
    collide_layers(inner, rates, f, bits_ref, pot, sides, post, speed)
    rho = None if last else Layers(edge_rest, rest, size_x, edge1)
    inner = [x for x in range(size_x) if x not in edge1]
    stream_layers(inner, bits_ref, post, Layers(None, f_out, size_x, edge1), rho)
    for ref, y, ks in ((up_ref, size_y - 1, UP), (down_ref, 0, DOWN)):
        for j, k in enumerate(ks):
            ex, _, ez = VELOCITY[k]
            for x in range(size_x):
                row = j * size_x + x
                if 0 <= x - ex < size_x:
                    ref[row : row + 1] = post.row(x - ex, TILE + y, k)
                else:
                    ref[row : row + 1] = jnp.zeros((1, size_z), jnp.float32)
            if ez != 0:
                rows = slice(j * size_x, (j + 1) * size_x)
                ref[rows] = roll_z(ref[rows], ez)
        if not last:
            for x in range(size_x):
                ref[5 * size_x + x : 5 * size_x + x + 1] = rho.row(x, y)


def pack_kernel(last, pairs, size_x, size_y, *refs):
    up_in, down_in, xl, xr, own_right, own_left, a_ref, b_ref, up_ref, down_ref = refs
    parts = 5 if last else 6
    at = parts * size_y
    for ref, source, y, ks, c, h in (
        (up_ref, up_in, size_y - 1, UP, C_UP, H_UP),
        (down_ref, down_in, 0, DOWN, C_DN, H_DN),
    ):
        ref[...] = jnp.zeros(ref.shape, jnp.float32)
        ref[: parts * size_x] = source[: parts * size_x]
        for side, own, x, ex, rc, g in (
            (xl, own_left, 0, 1, RC_L, G_L),
            (xr, own_right, size_x - 1, -1, RC_R, G_R),
        ):
            j = [i for i, k in enumerate(ks) if VELOCITY[k][0] == ex][0]
            row = j * size_x + x
            ref[row : row + 1] = side[at + c : at + c + 1]
            if not last:
                row = 5 * size_x + x
                ref[row : row + 1] = source[row : row + 1] + total(
                    [side[i * size_y + y : i * size_y + y + 1] for i in range(5)]
                )
                row = 6 * size_x
                ref[row + rc : row + rc + 1] = side[5 * size_y + y : 5 * size_y + y + 1] + total(
                    [own[i * size_y + y : i * size_y + y + 1] for i in range(5)]
                )
                ref[row + g : row + g + 1] = (
                    side[at + h : at + h + 1] + own[at + c : at + c + 1]
                )
    to_pairs(pairs, up_ref, down_ref, a_ref, b_ref)


def end_kernel(pairs, f_edge, f_middle, bits_ref, xl, xr, ya, yb, out_ref, yd, yu):
    size_x, size_y, size_z = bits_ref.shape
    row_of = lax.broadcasted_iota(jnp.int32, (TILE, size_z), 0)
    from_pairs(pairs, ya, yb, yd, yu)
    held = Layers(f_edge, f_middle, size_x, one_layer(size_x))
    for x in range(size_x):
        for y in range(0, size_y, TILE):
            fluid = fluid_at(bits_ref, x, y)
            for k in range(N):
                value = held.load(x, y, k)
                for at, side, ks in ((0, xl, RIGHT), (size_x - 1, xr, LEFT)):
                    if x == at and k in ks:
                        row = ks.index(k) * size_y + y
                        value = value + side[row : row + TILE]
                for at, side, ks in ((0, yd, UP), (size_y - 1, yu, DOWN)):
                    if y <= at < y + TILE and k in ks:
                        row = ks.index(k) * size_x + x
                        value = value + jnp.where(row_of == at - y, side[row : row + 1], 0.0)
                out_ref[k, x, y : y + TILE] = jnp.where(fluid, value, 0.0)


VMEM = pl.BlockSpec(memory_space=pltpu.VMEM)
SMEM = pl.BlockSpec(memory_space=pltpu.SMEM)
ANY = pl.BlockSpec(memory_space=pl.ANY)


def call(kernel, outs, args, special=None, scratch=(), cost=None):
    special = special or {}
    return pl.pallas_call(
        kernel,
        out_shape=[jax.ShapeDtypeStruct(shape, dtype) for shape, dtype in outs],
        in_specs=[special.get(i, VMEM) for i in range(len(args))],
        out_specs=[VMEM] * len(outs),
        scratch_shapes=[
            pltpu.VMEM(item, jnp.float32) if isinstance(item, tuple) else item for item in scratch
        ],
        compiler_params=pltpu.CompilerParams(vmem_limit_bytes=16 * 2**20),
        cost_estimate=cost,
    )(*args)


def shift(forward, backward, axis):
    count = lax.axis_size(axis)
    ahead = [(i, (i + 1) % count) for i in range(count)]
    return (
        lax.ppermute(forward, axis, ahead),
        lax.ppermute(backward, axis, [(b, a) for a, b in ahead]),
    )


def exchange(pairs, a, b, axis):
    if not pairs:
        return shift(a, b, axis)
    count = lax.axis_size(axis)
    partners = [
        [(i, (i + (1 if i % 2 == parity else -1)) % count) for i in range(count)]
        for parity in range(2)
    ]
    b = lax.ppermute(b, axis, partners[1])
    return lax.ppermute(a, axis, partners[0]), b


def per_device(populations, fluid_mask, wet_class, wall_potential, relax_rates):
    size_x, size_y, size_z = fluid_mask.shape
    f32, i32 = jnp.float32, jnp.int32
    pairs = lax.axis_size("gy") % 2 == 0
    whole = ((size_x, size_y, size_z), f32)
    rows = lambda count: ((count, size_z), f32)
    fields = lambda count: ((N, count, size_y, size_z), f32)
    padded = (size_x + 2, size_y + PAD, size_z)
    start_rows = rows(2 * size_x + TILE)

    f, mask, pot0, right, left = call(
        start_kernel,
        [fields(size_x), whole, whole, rows(2 * size_y), rows(2 * size_y)],
        (populations, fluid_mask, wet_class, wall_potential),
        special={i: ANY for i in range(4)},
        scratch=[
            pltpu.VMEM(fluid_mask.shape, i32),
            pltpu.VMEM(wet_class.shape, i32),
            pltpu.SMEM(wall_potential.shape, f32),
            pltpu.SemaphoreType.DMA((N,)),
            pltpu.SemaphoreType.DMA((3,)),
        ],
    )
    x0l, x0r = shift(right, left, "gx")
    a, b = call(
        functools.partial(start_pack_kernel, pairs),
        [start_rows] * 2,
        (pot0, mask, x0l, x0r),
        scratch=[start_rows[0]] * 2,
    )
    a, b = exchange(pairs, a, b, "gy")
    bits, y0d, y0u = call(
        functools.partial(bits_kernel, pairs),
        [((size_x, size_y, size_z), i32), start_rows, start_rows],
        (mask, x0l, x0r, a, b),
        scratch=[padded],
    )
    edge2, edge1 = len(two_layers(size_x)), len(one_layer(size_x))
    operations = 400 * size_x * size_y * size_z
    cost = pl.CostEstimate(flops=operations, bytes_accessed=4 * operations // 20, transcendentals=0)
    held, sent = (f,), ()
    for step in range(STEPS):
        first, last = step == 0, step == STEPS - 1
        parts = 5 if last else 6
        x_rows, y_rows = rows(parts * size_y + TILE), rows(parts * size_x + (0 if last else TILE))
        halo_rows = (6 * size_x + TILE, size_z)
        pot, post, f_edge, right, left, rest = call(
            functools.partial(edge_kernel, first, last, pairs),
            [
                (padded, f32),
                ((N, edge2, size_y + PAD, size_z), f32),
                fields(edge1),
                x_rows,
                x_rows,
                ((3, edge2, size_y, size_z) if last else (edge1, size_y, size_z), f32),
            ],
            (relax_rates, bits, pot0, x0l, x0r, y0d, y0u, *held, *sent),
            special={0: SMEM},
            scratch=[] if first else [halo_rows] * 4,
            cost=cost,
        )
        xl, xr = shift(right, left, "gx")
        f_middle, up, down, more = call(
            functools.partial(middle_kernel, first, last, pairs),
            [
                fields(size_x - edge1),
                y_rows,
                y_rows,
                ((3, *whole[0]) if last else (size_x - edge1, size_y, size_z), f32),
            ],
            (relax_rates, bits, pot, post, rest, *held[:2], *sent[2:4]),
            special={0: SMEM},
            scratch=[(N, size_x - edge2, size_y + PAD, size_z)]
            + ([] if first else [halo_rows] * 2),
            cost=cost,
        )
        a, b = call(
            functools.partial(pack_kernel, last, pairs, size_x, size_y),
            [y_rows, y_rows],
            (up, down, xl, xr, right, left),
            scratch=[y_rows[0]] * 2,
        )
        ya, yb = exchange(pairs, a, b, "gy")
        held = (f_edge, f_middle, rest, more)
        sent = (xl, xr, ya, yb, right, left, a, b)
    (out,) = call(
        functools.partial(end_kernel, pairs),
        [fields(size_x)],
        (f_edge, f_middle, bits, xl, xr, ya, yb),
        scratch=[y_rows[0]] * 2,
    )
    return out, more


def solution(mesh):
    return jax.shard_map(
        per_device,
        mesh=mesh,
        in_specs=(
            P(None, ("groups", "gx"), "gy", None),
            P(("groups", "gx"), "gy", None),
            P(("groups", "gx"), "gy", None),
            P("groups"),
            P(),
        ),
        out_specs=(P(None, ("groups", "gx"), "gy", None), P(None, ("groups", "gx"), "gy", None)),
        check_vma=False,
    )
```

```python
import functools

import jax
import jax.numpy as jnp
from jax import lax
from jax.experimental import pallas as pl
from jax.experimental.pallas import tpu as pltpu
from jax.sharding import PartitionSpec as P

STEPS = 4
STRENGTH = 2.5
VELOCITY = (
    (0, 0, 0),
    (1, 0, 0),
    (-1, 0, 0),
    (0, 1, 0),
    (0, -1, 0),
    (0, 0, 1),
    (0, 0, -1),
    (1, 1, 0),
    (-1, -1, 0),
    (1, -1, 0),
    (-1, 1, 0),
    (1, 0, 1),
    (-1, 0, -1),
    (1, 0, -1),
    (-1, 0, 1),
    (0, 1, 1),
    (0, -1, -1),
    (0, 1, -1),
    (0, -1, 1),
)
N = len(VELOCITY)
OPPOSITE = [0] + [k + 1 if k % 2 == 1 else k - 1 for k in range(1, N)]
RIGHT = [k for k in range(N) if VELOCITY[k][0] == 1]
LEFT = [k for k in range(N) if VELOCITY[k][0] == -1]
UP = [k for k in range(N) if VELOCITY[k][1] == 1]
DOWN = [k for k in range(N) if VELOCITY[k][1] == -1]
TILE = 8
PAD = 2 * TILE

C_UP, C_DN, H_UP, H_DN = 0, 1, 2, 3
RC_L, RC_R, G_L, G_R = 0, 1, 2, 3


def roll_z(value, step):
    if step == 0:
        return value
    return pltpu.roll(value, step % value.shape[-1], value.ndim - 1)


def total(values):
    values = list(values)
    while len(values) > 1:
        values = [
            values[i] + values[i + 1] if i + 1 < len(values) else values[i]
            for i in range(0, len(values), 2)
        ]
    return values[0]


def potential_of(density, fluid, solid_value):
    return jnp.where(fluid, 1.0 - jnp.exp(-density), solid_value)


def collide(f, fluid, force, rate):
    fx, fy, fz = force
    s = {k: f[k] + f[k + 1] for k in range(1, N, 2)}
    d = {k: f[k] - f[k + 1] for k in range(1, N, 2)}
    xxyy, xxzz, yyzz = s[7] + s[9], s[11] + s[13], s[15] + s[17]
    xy, xz, yz = s[7] - s[9], s[11] - s[13], s[15] - s[17]
    xyy, yxx = d[7] + d[9], d[7] - d[9]
    xzz, zxx = d[11] + d[13], d[11] - d[13]
    yzz, zyy = d[15] + d[17], d[15] - d[17]
    jx, jy, jz = d[1] + (xyy + xzz), d[3] + (yxx + yzz), d[5] + (zxx + zyy)
    xx, yy, zz = s[1] + (xxyy + xxzz), s[3] + (xxyy + yyzz), s[5] + (xxzz + yyzz)
    rho = (f[0] + s[1]) + (s[3] + s[5]) + (xxyy + (xxzz + yyzz))
    safe = jnp.where(fluid, rho, 1.0)
    inverse = 1.0 / safe
    hx, hy, hz = 0.5 * fx, 0.5 * fy, 0.5 * fz
    gx, gy, gz = jx + hx, jy + hy, jz + hz
    ux, uy, uz = gx * inverse, gy * inverse, gz * inverse
    third = safe * (1.0 / 3.0)
    ninth = safe * (1.0 / 9.0)
    px, py, pz = gx - fx, gy - fy, gz - fz
    txx, tyy, tzz = ux * px, uy * py, uz * pz
    sx, sy, sz = ux * fx, uy * fy, uz * fz
    pxy = ux * fy + uy * fx
    pxz = ux * fz + uz * fx
    pyz = uy * fz + uz * fy
    t3, s3 = (txx + tyy + tzz) * (1.0 / 3.0), (sx + sy + sz) * (2.0 / 3.0)
    rho = rho - rate(0) * (rho - safe)
    nx = jx + fx - rate(1) * (jx - safe * ux + hx)
    ny = jy + fy - rate(2) * (jy - safe * uy + hy)
    nz = jz + fz - rate(3) * (jz - safe * uz + hz)
    xy = xy + rate(4) * (gx * uy - 0.5 * pxy - xy) + pxy
    xz = xz + rate(5) * (gx * uz - 0.5 * pxz - xz) + pxz
    yz = yz + rate(6) * (gy * uz - 0.5 * pyz - yz) + pyz
    xx = xx + rate(7) * (third + txx - xx) + 2.0 * sx
    yy = yy + rate(8) * (third + tyy - yy) + 2.0 * sy
    zz = zz + rate(9) * (third + tzz - zz) + 2.0 * sz
    ex, ey, ez = jx * (1.0 / 3.0), jy * (1.0 / 3.0), jz * (1.0 / 3.0)
    qx, qy, qz = fx * (1.0 / 3.0), fy * (1.0 / 3.0), fz * (1.0 / 3.0)
    xyy = xyy + rate(10) * (ex - xyy) + qx
    xzz = xzz + rate(11) * (ex - xzz) + qx
    yxx = yxx + rate(12) * (ey - yxx) + qy
    yzz = yzz + rate(13) * (ey - yzz) + qy
    zxx = zxx + rate(14) * (ez - zxx) + qz
    zyy = zyy + rate(15) * (ez - zyy) + qz
    base = ninth + t3
    xxyy = xxyy + rate(16) * (base - 0.5 * tzz - xxyy) + (s3 - sz)
    xxzz = xxzz + rate(17) * (base - 0.5 * tyy - xxzz) + (s3 - sy)
    yyzz = yyzz + rate(18) * (base - 0.5 * txx - yyzz) + (s3 - sx)
    out = [None] * N
    for first, even, cross, odd1, odd2 in (
        (7, xxyy, xy, xyy, yxx),
        (11, xxzz, xz, xzz, zxx),
        (15, yyzz, yz, yzz, zyy),
    ):
        even, cross, odd1, odd2 = 0.25 * even, 0.25 * cross, 0.25 * odd1, 0.25 * odd2
        plus, minus = even + cross, even - cross
        both, diff = odd1 + odd2, odd1 - odd2
        out[first], out[first + 1] = plus + both, plus - both
        out[first + 2], out[first + 3] = minus + diff, minus - diff
    pairs = []
    for first, even, odd in (
        (1, xx - (xxyy + xxzz), nx - (xyy + xzz)),
        (3, yy - (xxyy + yyzz), ny - (yxx + yzz)),
        (5, zz - (xxzz + yyzz), nz - (zxx + zyy)),
    ):
        half_even, half_odd = 0.5 * even, 0.5 * odd
        out[first], out[first + 1] = half_even + half_odd, half_even - half_odd
        pairs.append(even)
    out[0] = rho - (pairs[0] + pairs[1] + pairs[2]) - (xxyy + xxzz + yyzz)
    return out, (ux, uy, uz)


def start_kernel(f_hbm, mask_hbm, wet_hbm, wall_hbm, f_ref, mask_ref, pot_ref, right_ref, left_ref, *scratch):
    mask_in, wet_in, wall_in, f_sems, sems = scratch
    size_x, size_y = mask_ref.shape[0], mask_ref.shape[1]
    small = [
        pltpu.make_async_copy(source, target, sems.at[i])
        for i, (source, target) in enumerate(
            ((wall_hbm, wall_in), (mask_hbm, mask_in), (wet_hbm, wet_in))
        )
    ]
    large = [pltpu.make_async_copy(f_hbm.at[k], f_ref.at[k], f_sems.at[k]) for k in range(N)]
    for copy in small + large:
        copy.start()
    for copy in small:
        copy.wait()
    for x in range(size_x):
        wet = wet_in[x]
        wall = jnp.zeros(wet.shape, jnp.float32)
        for c in range(wall_in.shape[0]):
            wall = jnp.where(wet == c, wall_in[c], wall)
        pot_ref[x] = wall
        mask_ref[x] = jnp.where(mask_in[x] == 1, 1.0, 0.0)
    for copy in large:
        copy.wait()
    for x in range(size_x):
        density = total([f_ref[k, x] for k in range(N)])
        pot_ref[x] = potential_of(density, mask_ref[x] > 0.5, pot_ref[x])
    for ref, x in ((right_ref, size_x - 1), (left_ref, 0)):
        ref[:size_y] = pot_ref[x]
        ref[size_y:] = mask_ref[x]


def start_pack_kernel(pairs, pot_ref, mask_ref, from_left, from_right, a_ref, b_ref, up_ref, down_ref):
    size_x, size_y = mask_ref.shape[0], mask_ref.shape[1]
    for ref, y in ((up_ref, size_y - 1), (down_ref, 0)):
        ref[2 * size_x :] = jnp.zeros((TILE, ref.shape[1]), jnp.float32)
        for x in range(size_x):
            ref[x : x + 1] = pot_ref[x, y : y + 1]
            ref[size_x + x : size_x + x + 1] = mask_ref[x, y : y + 1]
        for i, side in enumerate((from_left, from_right)):
            row = 2 * size_x + i
            ref[row : row + 1] = side[y : y + 1]
            ref[row + 2 : row + 3] = side[size_y + y : size_y + y + 1]
    to_pairs(pairs, up_ref, down_ref, a_ref, b_ref)


def to_pairs(pairs, up_ref, down_ref, a_ref, b_ref):
    up, down = up_ref[...], down_ref[...]
    if not pairs:
        a_ref[...], b_ref[...] = up, down
        return
    odd = lax.axis_index("gy") % 2 == 1
    a_ref[...] = jnp.where(odd, down, up)
    b_ref[...] = jnp.where(odd, up, down)


def from_pairs(pairs, a_ref, b_ref, below_ref, above_ref):
    a, b = a_ref[...], b_ref[...]
    if not pairs:
        below_ref[...], above_ref[...] = a, b
        return
    odd = lax.axis_index("gy") % 2 == 1
    below_ref[...] = jnp.where(odd, a, b)
    above_ref[...] = jnp.where(odd, b, a)


def bits_kernel(pairs, mask_ref, x0l, x0r, a_ref, b_ref, bits_ref, y0d, y0u, pad_ref):
    size_x, size_y = mask_ref.shape[0], mask_ref.shape[1]
    from_pairs(pairs, a_ref, b_ref, y0d, y0u)
    for x in range(size_x):
        pad_ref[1 + x, TILE : TILE + size_y] = mask_ref[x]
    for x, side in ((0, x0l), (1 + size_x, x0r)):
        pad_ref[x, TILE : TILE + size_y] = side[size_y:]
    for y, side in ((TILE - 1, y0d), (TILE + size_y, y0u)):
        for x in range(size_x):
            pad_ref[1 + x, y : y + 1] = side[size_x + x : size_x + x + 1]
        for x, row in ((0, 2 * size_x + 2), (1 + size_x, 2 * size_x + 3)):
            pad_ref[x, y : y + 1] = side[row : row + 1]
    for x in range(size_x):
        for y in range(0, size_y, TILE):
            bits = jnp.zeros((TILE, mask_ref.shape[2]), jnp.int32)
            for k in range(N):
                ex, ey, ez = VELOCITY[k]
                row = TILE + y - ey
                source = roll_z(pad_ref[1 + x - ex, row : row + TILE], ez)
                bits = bits | jnp.where(source > 0.5, 1 << k, 0)
            bits_ref[x, y : y + TILE] = bits


class Layers:
    def __init__(self, edge_ref, middle_ref, size_x, edge):
        self.where = {}
        middle = [x for x in range(size_x) if x not in edge]
        for ref, xs in ((edge_ref, edge), (middle_ref, middle)):
            for i, x in enumerate(xs):
                self.where[x] = (ref, i)

    def load(self, x, y, k=None):
        ref, i = self.where[x]
        return ref[i, y : y + TILE] if k is None else ref[k, i, y : y + TILE]

    def row(self, x, y, k=None):
        ref, i = self.where[x]
        return ref[i, y : y + 1] if k is None else ref[k, i, y : y + 1]

    def store(self, x, y, value, k=None):
        ref, i = self.where[x]
        if k is None:
            ref[i, y : y + TILE] = value
        else:
            ref[k, i, y : y + TILE] = value


def two_layers(size_x):
    return [0, 1, size_x - 2, size_x - 1]


def one_layer(size_x):
    return [0, size_x - 1]


def fluid_at(bits_ref, x, y):
    return (bits_ref[x, y : y + TILE] & 1) != 0


def clear_outside(post, layers, size_y):
    nothing = jnp.zeros((TILE, post.shape[-1]), jnp.float32)
    for i in range(layers):
        for k in UP:
            post[k, i, :TILE] = nothing
        for k in DOWN:
            post[k, i, TILE + size_y :] = nothing


def collide_layers(xs, rates, f, bits_ref, pot, sides, post, speed):
    size_x, size_y, size_z = bits_ref.shape
    row_of = lax.broadcasted_iota(jnp.int32, (TILE, size_z), 0)
    for x in xs:
        for y in range(0, size_y, TILE):
            near = {
                (i, j): pot[1 + x + i, TILE + y + j : 2 * TILE + y + j]
                for i in (-1, 0, 1)
                for j in (-1, 0, 1)
            }
            scale = near[0, 0] * (STRENGTH / 36.0)
            dx = near[1, 0] - near[-1, 0]
            dy = near[0, 1] - near[0, -1]
            pp, pm, mp, mm = near[1, 1], near[1, -1], near[-1, 1], near[-1, -1]
            both = near[1, 0] + near[-1, 0] + near[0, 1] + near[0, -1] + 2.0 * near[0, 0]
            diag1, diag2 = pp - mm, pm - mp
            force = (
                scale * (2.0 * dx + (diag1 + diag2) + (roll_z(dx, 1) + roll_z(dx, -1))),
                scale * (2.0 * dy + (diag1 - diag2) + (roll_z(dy, 1) + roll_z(dy, -1))),
                scale * (roll_z(both, -1) - roll_z(both, 1)),
            )
            now = [f(k, x, y) for k in range(N)]
            if sides is not None:
                xl, xr, yd, yu = sides
                for at, side, ks in ((0, xl, RIGHT), (size_x - 1, xr, LEFT)):
                    if x == at:
                        for j, k in enumerate(ks):
                            now[k] = now[k] + side[j * size_y + y : j * size_y + y + TILE]
                for at, side, ks in ((0, yd, UP), (size_y - 1, yu, DOWN)):
                    if y <= at < y + TILE:
                        for j, k in enumerate(ks):
                            entering = side[j * size_x + x : j * size_x + x + 1]
                            now[k] = now[k] + jnp.where(row_of == at - y, entering, 0.0)
            fluid = fluid_at(bits_ref, x, y)
            after, at_speed = collide(now, fluid, force, lambda r: rates[r])
            for k in range(N):
                post.store(x, TILE + y, jnp.where(fluid, after[k], 0.0), k)
            if speed is not None:
                for c in range(3):
                    speed.store(x, y, jnp.where(fluid, at_speed[c], 0.0), c)


def stream_layers(xs, bits_ref, post, f, rho):
    size_x, size_y, _ = bits_ref.shape
    for x in xs:
        for y in range(0, size_y, TILE):
            bits = bits_ref[x, y : y + TILE]
            arrived = []
            for k in range(N):
                ex, ey, ez = VELOCITY[k]
                value = post.load(x, TILE + y, OPPOSITE[k])
                if k > 0:
                    come = 0.0
                    if 0 <= x - ex < size_x:
                        come = roll_z(post.load(x - ex, TILE + y - ey, k), ez)
                    value = jnp.where((bits & (1 << k)) != 0, come, value)
                f.store(x, y, value, k)
                arrived.append(value)
            if rho is not None:
                rho.store(x, y, total(arrived))


def edge_kernel(first, last, pairs, *refs):
    refs = list(refs)
    take = lambda count: [refs.pop(0) for _ in range(count)]
    rates, bits_ref, pot0_ref, x0l, x0r, y0d, y0u = take(7)
    if first:
        f_ref = take(1)[0]
    else:
        f_edge, f_middle, rho_edge, rho_middle, xl, xr, ya, yb = take(8)
        own_right, own_left, own_a, own_b = take(4)
    pot, post_out, f_out, right_ref, left_ref = take(5)
    rest = take(1)[0]
    size_x, size_y, size_z = bits_ref.shape
    edge2, edge1 = two_layers(size_x), one_layer(size_x)
    sides = None
    if first:
        f = lambda k, x, y: f_ref[k, x, y : y + TILE]
    else:
        yd, yu, own_down, own_up = take(4)
        from_pairs(pairs, ya, yb, yd, yu)
        if pairs:
            from_pairs(pairs, own_a, own_b, own_down, own_up)
        else:
            own_down, own_up = own_b, own_a
        sides = (xl, xr, yd, yu)
        held = Layers(f_edge, f_middle, size_x, edge1)
        density_of = Layers(rho_edge, rho_middle, size_x, edge1)
        f = lambda k, x, y: held.load(x, y, k)
    clear_outside(post_out, len(edge2), size_y)

    if first:
        for x in range(size_x):
            pot[1 + x, TILE : TILE + size_y] = pot0_ref[x]
        for x, side in ((0, x0l), (1 + size_x, x0r)):
            pot[x, TILE : TILE + size_y] = side[:size_y]
        for y, side in ((TILE - 1, y0d), (TILE + size_y, y0u)):
            for x in range(size_x):
                pot[1 + x, y : y + 1] = side[x : x + 1]
            for x, row in ((0, 2 * size_x), (1 + size_x, 2 * size_x + 1)):
                pot[x, y : y + 1] = side[row : row + 1]
    else:
        end = 6 * size_x
        row_of = lax.broadcasted_iota(jnp.int32, (TILE, size_z), 0)
        entering = {
            at: total([side[j * size_x : (j + 1) * size_x] for j in range(5)])
            for at, side in ((0, yd), (size_y - 1, yu))
        }
        for x in range(size_x):
            for y in range(0, size_y, TILE):
                density = density_of.load(x, y)
                for at, side in ((0, xl), (size_x - 1, xr)):
                    if x == at:
                        density = density + total(
                            [side[j * size_y + y : j * size_y + y + TILE] for j in range(5)]
                        )
                for at, rows in entering.items():
                    if y <= at < y + TILE:
                        density = density + jnp.where(row_of == at - y, rows[x : x + 1], 0.0)
                pot[1 + x, TILE + y : 2 * TILE + y] = potential_of(
                    density, fluid_at(bits_ref, x, y), pot0_ref[x, y : y + TILE]
                )
        for x, side, own, side0, g in (
            (0, xl, own_left, x0l, G_L),
            (1 + size_x, xr, own_right, x0r, G_R),
        ):
            for y in range(0, size_y, TILE):
                density = side[5 * size_y + y : 5 * size_y + y + TILE] + total(
                    [own[j * size_y + y : j * size_y + y + TILE] for j in range(5)]
                )
                for at, row in ((0, yd), (size_y - 1, yu)):
                    if y <= at < y + TILE:
                        more = row[end + g : end + g + 1]
                        density = density + jnp.where(row_of == at - y, more, 0.0)
                pot[x, TILE + y : 2 * TILE + y] = potential_of(
                    density,
                    side0[size_y + y : size_y + y + TILE] > 0.5,
                    side0[y : y + TILE],
                )
        for y, side, own, side0 in (
            (TILE - 1, yd, own_down, y0d),
            (TILE + size_y, yu, own_up, y0u),
        ):
            density = side[5 * size_x : 6 * size_x] + total(
                [own[j * size_x : (j + 1) * size_x] for j in range(5)]
            )
            value = potential_of(density, side0[size_x : 2 * size_x] > 0.5, side0[:size_x])
            for x in range(size_x):
                pot[1 + x, y : y + 1] = value[x : x + 1]
            for x, rc, g, i in ((0, RC_L, G_L, 0), (1 + size_x, RC_R, G_R, 1)):
                density = side[end + rc : end + rc + 1] + own[end + g : end + g + 1]
                row = 2 * size_x + i
                pot[x, y : y + 1] = potential_of(
                    density, side0[row + 2 : row + 3] > 0.5, side0[row : row + 1]
                )

    post = Layers(post_out, None, size_x, edge2)
    speed = Layers(rest, None, size_x, edge2) if last else None
    collide_layers(edge2, rates, f, bits_ref, pot, sides, post, speed)
    rho = None if last else Layers(rest, None, size_x, edge1)
    stream_layers(edge1, bits_ref, post, Layers(f_out, None, size_x, edge1), rho)

    at = (5 if last else 6) * size_y
    for i, (ref, x, ks, dirs) in enumerate(
        ((left_ref, 0, LEFT, (10, 8)), (right_ref, size_x - 1, RIGHT, (7, 9)))
    ):
        for j, k in enumerate(ks):
            _, ey, ez = VELOCITY[k]
            for y in range(0, size_y, TILE):
                row = j * size_y + y
                ref[row : row + TILE] = roll_z(post.load(x, TILE + y - ey, k), ez)
        ref[at : at + TILE] = jnp.zeros((TILE, size_z), jnp.float32)
        ref[at + C_UP : at + C_UP + 1] = post.row(x, TILE + size_y - 1, dirs[0])
        ref[at + C_DN : at + C_DN + 1] = post.row(x, TILE, dirs[1])
        if not last:
            ref[5 * size_y : 6 * size_y] = rest[i]
            for h, y, leave in ((H_UP, size_y - 1, UP), (H_DN, 0, DOWN)):
                ref[at + h : at + h + 1] = total(
                    [
                        roll_z(post.row(x - VELOCITY[k][0], TILE + y, k), VELOCITY[k][2])
                        for k in leave
                        if 0 <= x - VELOCITY[k][0] < size_x
                    ]
                )


def middle_kernel(first, last, pairs, *refs):
    refs = list(refs)
    take = lambda count: [refs.pop(0) for _ in range(count)]
    rates, bits_ref, pot, post_edge, edge_rest = take(5)
    if first:
        f_ref = take(1)[0]
    else:
        f_edge, f_middle, ya, yb = take(4)
    f_out, up_ref, down_ref, rest = take(4)
    post_middle = take(1)[0]
    size_x, size_y, size_z = bits_ref.shape
    edge2, edge1 = two_layers(size_x), one_layer(size_x)
    sides = None
    if first:
        f = lambda k, x, y: f_ref[k, x, y : y + TILE]
    else:
        yd, yu = take(2)
        from_pairs(pairs, ya, yb, yd, yu)
        sides = (None, None, yd, yu)
        held = Layers(f_edge, f_middle, size_x, edge1)
        f = lambda k, x, y: held.load(x, y, k)
    clear_outside(post_middle, size_x - len(edge2), size_y)
    post = Layers(post_edge, post_middle, size_x, edge2)
    speed = None
    if last:
        speed = Layers(None, None, size_x, [])
        speed.where = {x: (rest, x) for x in range(size_x)}
        for c in range(3):
            for i, x in enumerate(edge2):
                rest[c, x] = edge_rest[c, i]
    inner = [x for x in range(size_x) if x not in edge2]
    collide_layers(inner, rates, f, bits_ref, pot, sides, post, speed)
    rho = None if last else Layers(edge_rest, rest, size_x, edge1)
    inner = [x for x in range(size_x) if x not in edge1]
    stream_layers(inner, bits_ref, post, Layers(None, f_out, size_x, edge1), rho)
    for ref, y, ks in ((up_ref, size_y - 1, UP), (down_ref, 0, DOWN)):
        for j, k in enumerate(ks):
            ex, _, ez = VELOCITY[k]
            for x in range(size_x):
                row = j * size_x + x
                if 0 <= x - ex < size_x:
                    ref[row : row + 1] = post.row(x - ex, TILE + y, k)
                else:
                    ref[row : row + 1] = jnp.zeros((1, size_z), jnp.float32)
            if ez != 0:
                rows = slice(j * size_x, (j + 1) * size_x)
                ref[rows] = roll_z(ref[rows], ez)
        if not last:
            for x in range(size_x):
                ref[5 * size_x + x : 5 * size_x + x + 1] = rho.row(x, y)


def pack_kernel(last, pairs, size_x, size_y, *refs):
    up_in, down_in, xl, xr, own_right, own_left, a_ref, b_ref, up_ref, down_ref = refs
    parts = 5 if last else 6
    at = parts * size_y
    for ref, source, y, ks, c, h in (
        (up_ref, up_in, size_y - 1, UP, C_UP, H_UP),
        (down_ref, down_in, 0, DOWN, C_DN, H_DN),
    ):
        ref[...] = jnp.zeros(ref.shape, jnp.float32)
        ref[: parts * size_x] = source[: parts * size_x]
        for side, own, x, ex, rc, g in (
            (xl, own_left, 0, 1, RC_L, G_L),
            (xr, own_right, size_x - 1, -1, RC_R, G_R),
        ):
            j = [i for i, k in enumerate(ks) if VELOCITY[k][0] == ex][0]
            row = j * size_x + x
            ref[row : row + 1] = side[at + c : at + c + 1]
            if not last:
                row = 5 * size_x + x
                ref[row : row + 1] = source[row : row + 1] + total(
                    [side[i * size_y + y : i * size_y + y + 1] for i in range(5)]
                )
                row = 6 * size_x
                ref[row + rc : row + rc + 1] = side[5 * size_y + y : 5 * size_y + y + 1] + total(
                    [own[i * size_y + y : i * size_y + y + 1] for i in range(5)]
                )
                ref[row + g : row + g + 1] = (
                    side[at + h : at + h + 1] + own[at + c : at + c + 1]
                )
    to_pairs(pairs, up_ref, down_ref, a_ref, b_ref)


def end_kernel(pairs, f_edge, f_middle, bits_ref, xl, xr, ya, yb, out_ref, yd, yu):
    size_x, size_y, size_z = bits_ref.shape
    row_of = lax.broadcasted_iota(jnp.int32, (TILE, size_z), 0)
    from_pairs(pairs, ya, yb, yd, yu)
    held = Layers(f_edge, f_middle, size_x, one_layer(size_x))
    for x in range(size_x):
        for y in range(0, size_y, TILE):
            fluid = fluid_at(bits_ref, x, y)
            for k in range(N):
                value = held.load(x, y, k)
                for at, side, ks in ((0, xl, RIGHT), (size_x - 1, xr, LEFT)):
                    if x == at and k in ks:
                        row = ks.index(k) * size_y + y
                        value = value + side[row : row + TILE]
                for at, side, ks in ((0, yd, UP), (size_y - 1, yu, DOWN)):
                    if y <= at < y + TILE and k in ks:
                        row = ks.index(k) * size_x + x
                        value = value + jnp.where(row_of == at - y, side[row : row + 1], 0.0)
                out_ref[k, x, y : y + TILE] = jnp.where(fluid, value, 0.0)


VMEM = pl.BlockSpec(memory_space=pltpu.VMEM)
SMEM = pl.BlockSpec(memory_space=pltpu.SMEM)
HBM = pl.BlockSpec(memory_space=pltpu.HBM)


def call(kernel, outs, args, special=None, scratch=(), cost=None):
    special = special or {}
    return pl.pallas_call(
        kernel,
        out_shape=[jax.ShapeDtypeStruct(shape, dtype) for shape, dtype in outs],
        in_specs=[special.get(i, VMEM) for i in range(len(args))],
        out_specs=[VMEM] * len(outs),
        scratch_shapes=[
            pltpu.VMEM(item, jnp.float32) if isinstance(item, tuple) else item for item in scratch
        ],
        compiler_params=pltpu.CompilerParams(vmem_limit_bytes=16 * 2**20),
        cost_estimate=cost,
    )(*args)


def shift(forward, backward, axis):
    count = lax.axis_size(axis)
    ahead = [(i, (i + 1) % count) for i in range(count)]
    return (
        lax.ppermute(forward, axis, ahead),
        lax.ppermute(backward, axis, [(b, a) for a, b in ahead]),
    )


def exchange(pairs, a, b, axis):
    if not pairs:
        return shift(a, b, axis)
    count = lax.axis_size(axis)
    partners = [
        [(i, (i + (1 if i % 2 == parity else -1)) % count) for i in range(count)]
        for parity in range(2)
    ]
    b = lax.ppermute(b, axis, partners[1])
    return lax.ppermute(a, axis, partners[0]), b


def per_device(populations, fluid_mask, wet_class, wall_potential, relax_rates):
    size_x, size_y, size_z = fluid_mask.shape
    f32, i32 = jnp.float32, jnp.int32
    pairs = lax.axis_size("gy") % 2 == 0
    whole = ((size_x, size_y, size_z), f32)
    rows = lambda count: ((count, size_z), f32)
    fields = lambda count: ((N, count, size_y, size_z), f32)
    padded = (size_x + 2, size_y + PAD, size_z)
    start_rows = rows(2 * size_x + TILE)

    f, mask, pot0, right, left = call(
        start_kernel,
        [fields(size_x), whole, whole, rows(2 * size_y), rows(2 * size_y)],
        [
            pltpu.with_memory_space_constraint(item, pltpu.HBM)
            for item in (populations, fluid_mask, wet_class, wall_potential)
        ],
        special={i: HBM for i in range(4)},
        scratch=[
            pltpu.VMEM(fluid_mask.shape, i32),
            pltpu.VMEM(wet_class.shape, i32),
            pltpu.SMEM(wall_potential.shape, f32),
            pltpu.SemaphoreType.DMA((N,)),
            pltpu.SemaphoreType.DMA((3,)),
        ],
    )
    x0l, x0r = shift(right, left, "gx")
    a, b = call(
        functools.partial(start_pack_kernel, pairs),
        [start_rows] * 2,
        (pot0, mask, x0l, x0r),
        scratch=[start_rows[0]] * 2,
    )
    a, b = exchange(pairs, a, b, "gy")
    bits, y0d, y0u = call(
        functools.partial(bits_kernel, pairs),
        [((size_x, size_y, size_z), i32), start_rows, start_rows],
        (mask, x0l, x0r, a, b),
        scratch=[padded],
    )
    edge2, edge1 = len(two_layers(size_x)), len(one_layer(size_x))
    operations = 400 * size_x * size_y * size_z
    cost = pl.CostEstimate(flops=operations, bytes_accessed=4 * operations // 20, transcendentals=0)
    held, sent = (f,), ()
    for step in range(STEPS):
        first, last = step == 0, step == STEPS - 1
        parts = 5 if last else 6
        x_rows, y_rows = rows(parts * size_y + TILE), rows(parts * size_x + (0 if last else TILE))
        halo_rows = (6 * size_x + TILE, size_z)
        pot, post, f_edge, right, left, rest = call(
            functools.partial(edge_kernel, first, last, pairs),
            [
                (padded, f32),
                ((N, edge2, size_y + PAD, size_z), f32),
                fields(edge1),
                x_rows,
                x_rows,
                ((3, edge2, size_y, size_z) if last else (edge1, size_y, size_z), f32),
            ],
            (relax_rates, bits, pot0, x0l, x0r, y0d, y0u, *held, *sent),
            special={0: SMEM},
            scratch=[] if first else [halo_rows] * 4,
            cost=cost,
        )
        xl, xr = shift(right, left, "gx")
        f_middle, up, down, more = call(
            functools.partial(middle_kernel, first, last, pairs),
            [
                fields(size_x - edge1),
                y_rows,
                y_rows,
                ((3, *whole[0]) if last else (size_x - edge1, size_y, size_z), f32),
            ],
            (relax_rates, bits, pot, post, rest, *held[:2], *sent[2:4]),
            special={0: SMEM},
            scratch=[(N, size_x - edge2, size_y + PAD, size_z)]
            + ([] if first else [halo_rows] * 2),
            cost=cost,
        )
        a, b = call(
            functools.partial(pack_kernel, last, pairs, size_x, size_y),
            [y_rows, y_rows],
            (up, down, xl, xr, right, left),
            scratch=[y_rows[0]] * 2,
        )
        ya, yb = exchange(pairs, a, b, "gy")
        held = (f_edge, f_middle, rest, more)
        sent = (xl, xr, ya, yb, right, left, a, b)
    (out,) = call(
        functools.partial(end_kernel, pairs),
        [fields(size_x)],
        (f_edge, f_middle, bits, xl, xr, ya, yb),
        scratch=[y_rows[0]] * 2,
    )
    return out, more


def solution(mesh):
    return jax.shard_map(
        per_device,
        mesh=mesh,
        in_specs=(
            P(None, ("groups", "gx"), "gy", None),
            P(("groups", "gx"), "gy", None),
            P(("groups", "gx"), "gy", None),
            P("groups"),
            P(),
        ),
        out_specs=(P(None, ("groups", "gx"), "gy", None), P(None, ("groups", "gx"), "gy", None)),
        check_vma=False,
    )
```

```python
import functools

import jax
import jax.numpy as jnp
from jax import lax
from jax.experimental import pallas as pl
from jax.experimental.pallas import tpu as pltpu
from jax.sharding import PartitionSpec as P

STEPS = 4
STRENGTH = 2.5
VELOCITY = (
    (0, 0, 0),
    (1, 0, 0),
    (-1, 0, 0),
    (0, 1, 0),
    (0, -1, 0),
    (0, 0, 1),
    (0, 0, -1),
    (1, 1, 0),
    (-1, -1, 0),
    (1, -1, 0),
    (-1, 1, 0),
    (1, 0, 1),
    (-1, 0, -1),
    (1, 0, -1),
    (-1, 0, 1),
    (0, 1, 1),
    (0, -1, -1),
    (0, 1, -1),
    (0, -1, 1),
)
N = len(VELOCITY)
OPPOSITE = [0] + [k + 1 if k % 2 == 1 else k - 1 for k in range(1, N)]
SHIFT = [(y, x, z) for x, y, z in VELOCITY]
RIGHT = [k for k in range(N) if SHIFT[k][0] == 1]
LEFT = [k for k in range(N) if SHIFT[k][0] == -1]
UP = [k for k in range(N) if SHIFT[k][1] == 1]
DOWN = [k for k in range(N) if SHIFT[k][1] == -1]
TILE = 8
PAD = 2 * TILE

C_UP, C_DN, H_UP, H_DN = 0, 1, 2, 3
RC_L, RC_R, G_L, G_R = 0, 1, 2, 3


def roll_z(value, step):
    if step == 0:
        return value
    return pltpu.roll(value, step % value.shape[-1], value.ndim - 1)


def total(values):
    values = list(values)
    while len(values) > 1:
        values = [
            values[i] + values[i + 1] if i + 1 < len(values) else values[i]
            for i in range(0, len(values), 2)
        ]
    return values[0]


def potential_of(density, fluid, solid_value):
    return jnp.where(fluid, 1.0 - jnp.exp(-density), solid_value)


def collide(f, fluid, force, rate):
    fx, fy, fz = force
    s = {k: f[k] + f[k + 1] for k in range(1, N, 2)}
    d = {k: f[k] - f[k + 1] for k in range(1, N, 2)}
    xxyy, xxzz, yyzz = s[7] + s[9], s[11] + s[13], s[15] + s[17]
    xy, xz, yz = s[7] - s[9], s[11] - s[13], s[15] - s[17]
    xyy, yxx = d[7] + d[9], d[7] - d[9]
    xzz, zxx = d[11] + d[13], d[11] - d[13]
    yzz, zyy = d[15] + d[17], d[15] - d[17]
    jx, jy, jz = d[1] + (xyy + xzz), d[3] + (yxx + yzz), d[5] + (zxx + zyy)
    xx, yy, zz = s[1] + (xxyy + xxzz), s[3] + (xxyy + yyzz), s[5] + (xxzz + yyzz)
    rho = (f[0] + s[1]) + (s[3] + s[5]) + (xxyy + (xxzz + yyzz))
    safe = jnp.where(fluid, rho, 1.0)
    inverse = 1.0 / safe
    hx, hy, hz = 0.5 * fx, 0.5 * fy, 0.5 * fz
    gx, gy, gz = jx + hx, jy + hy, jz + hz
    ux, uy, uz = gx * inverse, gy * inverse, gz * inverse
    third = safe * (1.0 / 3.0)
    ninth = safe * (1.0 / 9.0)
    px, py, pz = gx - fx, gy - fy, gz - fz
    txx, tyy, tzz = ux * px, uy * py, uz * pz
    sx, sy, sz = ux * fx, uy * fy, uz * fz
    pxy = ux * fy + uy * fx
    pxz = ux * fz + uz * fx
    pyz = uy * fz + uz * fy
    t3, s3 = (txx + tyy + tzz) * (1.0 / 3.0), (sx + sy + sz) * (2.0 / 3.0)
    rho = rho - rate(0) * (rho - safe)
    nx = jx + fx - rate(1) * (jx - safe * ux + hx)
    ny = jy + fy - rate(2) * (jy - safe * uy + hy)
    nz = jz + fz - rate(3) * (jz - safe * uz + hz)
    xy = xy + rate(4) * (gx * uy - 0.5 * pxy - xy) + pxy
    xz = xz + rate(5) * (gx * uz - 0.5 * pxz - xz) + pxz
    yz = yz + rate(6) * (gy * uz - 0.5 * pyz - yz) + pyz
    xx = xx + rate(7) * (third + txx - xx) + 2.0 * sx
    yy = yy + rate(8) * (third + tyy - yy) + 2.0 * sy
    zz = zz + rate(9) * (third + tzz - zz) + 2.0 * sz
    ex, ey, ez = jx * (1.0 / 3.0), jy * (1.0 / 3.0), jz * (1.0 / 3.0)
    qx, qy, qz = fx * (1.0 / 3.0), fy * (1.0 / 3.0), fz * (1.0 / 3.0)
    xyy = xyy + rate(10) * (ex - xyy) + qx
    xzz = xzz + rate(11) * (ex - xzz) + qx
    yxx = yxx + rate(12) * (ey - yxx) + qy
    yzz = yzz + rate(13) * (ey - yzz) + qy
    zxx = zxx + rate(14) * (ez - zxx) + qz
    zyy = zyy + rate(15) * (ez - zyy) + qz
    base = ninth + t3
    xxyy = xxyy + rate(16) * (base - 0.5 * tzz - xxyy) + (s3 - sz)
    xxzz = xxzz + rate(17) * (base - 0.5 * tyy - xxzz) + (s3 - sy)
    yyzz = yyzz + rate(18) * (base - 0.5 * txx - yyzz) + (s3 - sx)
    out = [None] * N
    for first, even, cross, odd1, odd2 in (
        (7, xxyy, xy, xyy, yxx),
        (11, xxzz, xz, xzz, zxx),
        (15, yyzz, yz, yzz, zyy),
    ):
        even, cross, odd1, odd2 = 0.25 * even, 0.25 * cross, 0.25 * odd1, 0.25 * odd2
        plus, minus = even + cross, even - cross
        both, diff = odd1 + odd2, odd1 - odd2
        out[first], out[first + 1] = plus + both, plus - both
        out[first + 2], out[first + 3] = minus + diff, minus - diff
    pairs = []
    for first, even, odd in (
        (1, xx - (xxyy + xxzz), nx - (xyy + xzz)),
        (3, yy - (xxyy + yyzz), ny - (yxx + yzz)),
        (5, zz - (xxzz + yyzz), nz - (zxx + zyy)),
    ):
        half_even, half_odd = 0.5 * even, 0.5 * odd
        out[first], out[first + 1] = half_even + half_odd, half_even - half_odd
        pairs.append(even)
    out[0] = rho - (pairs[0] + pairs[1] + pairs[2]) - (xxyy + xxzz + yyzz)
    return out, (ux, uy, uz)


def corner_pops(side):
    return SHIFT.index((side, 1, 0)), SHIFT.index((side, -1, 0))


def start_kernel(f_hbm, mask_hbm, wet_hbm, wall_hbm, raw_ref, flat_ref, mask_ref, pot_ref, right_ref, left_ref, *scratch):
    mask_in, wet_in, wall_in, f_sems, sems = scratch
    layers, rows = mask_ref.shape[0], mask_ref.shape[1]
    small = [
        pltpu.make_async_copy(source, target, sems.at[i])
        for i, (source, target) in enumerate(
            ((wall_hbm, wall_in), (mask_hbm, mask_in), (wet_hbm, wet_in))
        )
    ]
    large = [pltpu.make_async_copy(f_hbm.at[k], raw_ref.at[k], f_sems.at[k]) for k in range(N)]
    for copy in small + large:
        copy.start()
    for copy in small:
        copy.wait()
    blocks = [slice(i, i + TILE) for i in range(0, layers * rows, TILE)]
    for at in blocks:
        wet = wet_in[at]
        wall = jnp.zeros(wet.shape, jnp.float32)
        for c in range(wall_in.shape[0]):
            wall = jnp.where(wet == c, wall_in[c], wall)
        flat_ref[1, at] = wall
        flat_ref[0, at] = jnp.where(mask_in[at] == 1, 1.0, 0.0)
    for copy in large:
        copy.wait()
    for at in blocks:
        density = total([raw_ref[k, at] for k in range(N)])
        flat_ref[1, at] = potential_of(density, flat_ref[0, at] > 0.5, flat_ref[1, at])
    for i in range(layers):
        mask_ref[i] = flat_ref[0, pl.ds(i, rows, stride=layers)]
        pot_ref[i] = flat_ref[1, pl.ds(i, rows, stride=layers)]
    for ref, i in ((right_ref, layers - 1), (left_ref, 0)):
        ref[:rows] = pot_ref[i]
        ref[rows:] = mask_ref[i]


def turn_kernel(raw_ref, f_ref):
    layers, rows = f_ref.shape[1], f_ref.shape[2]
    for k in range(N):
        for i in range(layers):
            f_ref[k, i] = raw_ref[k, pl.ds(i, rows, stride=layers)]


def start_pack_kernel(pot_ref, mask_ref, from_left, from_right, up_ref, down_ref):
    size_x, size_y = mask_ref.shape[0], mask_ref.shape[1]
    for ref, y in ((up_ref, size_y - 1), (down_ref, 0)):
        ref[2 * size_x :] = jnp.zeros((TILE, ref.shape[1]), jnp.float32)
        for x in range(size_x):
            ref[x : x + 1] = pot_ref[x, y : y + 1]
            ref[size_x + x : size_x + x + 1] = mask_ref[x, y : y + 1]
        for i, side in enumerate((from_left, from_right)):
            row = 2 * size_x + i
            ref[row : row + 1] = side[y : y + 1]
            ref[row + 2 : row + 3] = side[size_y + y : size_y + y + 1]


def bits_kernel(mask_ref, x0l, x0r, y0d, y0u, bits_ref, pad_ref):
    size_x, size_y = mask_ref.shape[0], mask_ref.shape[1]
    for x in range(size_x):
        pad_ref[1 + x, TILE : TILE + size_y] = mask_ref[x]
    for x, side in ((0, x0l), (1 + size_x, x0r)):
        pad_ref[x, TILE : TILE + size_y] = side[size_y:]
    for y, side in ((TILE - 1, y0d), (TILE + size_y, y0u)):
        for x in range(size_x):
            pad_ref[1 + x, y : y + 1] = side[size_x + x : size_x + x + 1]
        for x, row in ((0, 2 * size_x + 2), (1 + size_x, 2 * size_x + 3)):
            pad_ref[x, y : y + 1] = side[row : row + 1]
    for x in range(size_x):
        for y in range(0, size_y, TILE):
            bits = jnp.zeros((TILE, mask_ref.shape[2]), jnp.int32)
            for k in range(N):
                ex, ey, ez = SHIFT[k]
                row = TILE + y - ey
                source = roll_z(pad_ref[1 + x - ex, row : row + TILE], ez)
                bits = bits | jnp.where(source > 0.5, 1 << k, 0)
            bits_ref[x, y : y + TILE] = bits


class Layers:
    def __init__(self, edge_ref, middle_ref, size_x, edge):
        self.where = {}
        middle = [x for x in range(size_x) if x not in edge]
        for ref, xs in ((edge_ref, edge), (middle_ref, middle)):
            for i, x in enumerate(xs):
                self.where[x] = (ref, i)

    def load(self, x, y, k=None):
        ref, i = self.where[x]
        return ref[i, y : y + TILE] if k is None else ref[k, i, y : y + TILE]

    def row(self, x, y, k=None):
        ref, i = self.where[x]
        return ref[i, y : y + 1] if k is None else ref[k, i, y : y + 1]

    def store(self, x, y, value, k=None):
        ref, i = self.where[x]
        if k is None:
            ref[i, y : y + TILE] = value
        else:
            ref[k, i, y : y + TILE] = value


def two_layers(size_x):
    return [0, 1, size_x - 2, size_x - 1]


def one_layer(size_x):
    return [0, size_x - 1]


def fluid_at(bits_ref, x, y):
    return (bits_ref[x, y : y + TILE] & 1) != 0


def clear_outside(post, layers, size_y):
    nothing = jnp.zeros((TILE, post.shape[-1]), jnp.float32)
    for i in range(layers):
        for k in UP:
            post[k, i, :TILE] = nothing
        for k in DOWN:
            post[k, i, TILE + size_y :] = nothing


def collide_layers(xs, rates, f, bits_ref, pot, sides, post, speed):
    size_x, size_y, size_z = bits_ref.shape
    row_of = lax.broadcasted_iota(jnp.int32, (TILE, size_z), 0)
    for x in xs:
        for y in range(0, size_y, TILE):
            near = {
                (i, j): pot[1 + x + i, TILE + y + j : 2 * TILE + y + j]
                for i in (-1, 0, 1)
                for j in (-1, 0, 1)
            }
            scale = near[0, 0] * (STRENGTH / 36.0)
            dx = near[1, 0] - near[-1, 0]
            dy = near[0, 1] - near[0, -1]
            pp, pm, mp, mm = near[1, 1], near[1, -1], near[-1, 1], near[-1, -1]
            both = near[1, 0] + near[-1, 0] + near[0, 1] + near[0, -1] + 2.0 * near[0, 0]
            diag1, diag2 = pp - mm, pm - mp
            force = (
                scale * (2.0 * dy + (diag1 - diag2) + (roll_z(dy, 1) + roll_z(dy, -1))),
                scale * (2.0 * dx + (diag1 + diag2) + (roll_z(dx, 1) + roll_z(dx, -1))),
                scale * (roll_z(both, -1) - roll_z(both, 1)),
            )
            now = [f(k, x, y) for k in range(N)]
            if sides is not None:
                xl, xr, yd, yu = sides
                for at, side, ks in ((0, xl, RIGHT), (size_x - 1, xr, LEFT)):
                    if x == at:
                        for j, k in enumerate(ks):
                            now[k] = now[k] + side[j * size_y + y : j * size_y + y + TILE]
                for at, side, ks in ((0, yd, UP), (size_y - 1, yu, DOWN)):
                    if y <= at < y + TILE:
                        for j, k in enumerate(ks):
                            entering = side[j * size_x + x : j * size_x + x + 1]
                            now[k] = now[k] + jnp.where(row_of == at - y, entering, 0.0)
            fluid = fluid_at(bits_ref, x, y)
            after, at_speed = collide(now, fluid, force, lambda r: rates[r])
            for k in range(N):
                post.store(x, TILE + y, jnp.where(fluid, after[k], 0.0), k)
            if speed is not None:
                for c in range(3):
                    speed.store(x, y, jnp.where(fluid, at_speed[c], 0.0), c)


def stream_layers(xs, bits_ref, post, f, rho):
    size_x, size_y, _ = bits_ref.shape
    for x in xs:
        for y in range(0, size_y, TILE):
            bits = bits_ref[x, y : y + TILE]
            arrived = []
            for k in range(N):
                ex, ey, ez = SHIFT[k]
                value = post.load(x, TILE + y, OPPOSITE[k])
                if k > 0:
                    come = 0.0
                    if 0 <= x - ex < size_x:
                        come = roll_z(post.load(x - ex, TILE + y - ey, k), ez)
                    value = jnp.where((bits & (1 << k)) != 0, come, value)
                f.store(x, y, value, k)
                arrived.append(value)
            if rho is not None:
                rho.store(x, y, total(arrived))


def edge_kernel(first, last, *refs):
    refs = list(refs)
    take = lambda count: [refs.pop(0) for _ in range(count)]
    rates, bits_ref, pot0_ref, x0l, x0r, y0d, y0u = take(7)
    if first:
        f_ref = take(1)[0]
    else:
        f_edge, f_middle, rho_edge, rho_middle, xl, xr, yd, yu = take(8)
        own_right, own_left, own_up, own_down = take(4)
    pot, post_out, f_out, right_ref, left_ref = take(5)
    rest = take(1)[0]
    size_x, size_y, size_z = bits_ref.shape
    edge2, edge1 = two_layers(size_x), one_layer(size_x)
    sides = None
    if first:
        f = lambda k, x, y: f_ref[k, x, y : y + TILE]
    else:
        sides = (xl, xr, yd, yu)
        held = Layers(f_edge, f_middle, size_x, edge1)
        density_of = Layers(rho_edge, rho_middle, size_x, edge1)
        f = lambda k, x, y: held.load(x, y, k)
    clear_outside(post_out, len(edge2), size_y)

    if first:
        for x in range(size_x):
            pot[1 + x, TILE : TILE + size_y] = pot0_ref[x]
        for x, side in ((0, x0l), (1 + size_x, x0r)):
            pot[x, TILE : TILE + size_y] = side[:size_y]
        for y, side in ((TILE - 1, y0d), (TILE + size_y, y0u)):
            for x in range(size_x):
                pot[1 + x, y : y + 1] = side[x : x + 1]
            for x, row in ((0, 2 * size_x), (1 + size_x, 2 * size_x + 1)):
                pot[x, y : y + 1] = side[row : row + 1]
    else:
        end = 6 * size_x
        row_of = lax.broadcasted_iota(jnp.int32, (TILE, size_z), 0)
        entering = {
            at: total([side[j * size_x : (j + 1) * size_x] for j in range(5)])
            for at, side in ((0, yd), (size_y - 1, yu))
        }
        for x in range(size_x):
            for y in range(0, size_y, TILE):
                density = density_of.load(x, y)
                for at, side in ((0, xl), (size_x - 1, xr)):
                    if x == at:
                        density = density + total(
                            [side[j * size_y + y : j * size_y + y + TILE] for j in range(5)]
                        )
                for at, rows in entering.items():
                    if y <= at < y + TILE:
                        density = density + jnp.where(row_of == at - y, rows[x : x + 1], 0.0)
                pot[1 + x, TILE + y : 2 * TILE + y] = potential_of(
                    density, fluid_at(bits_ref, x, y), pot0_ref[x, y : y + TILE]
                )
        for x, side, own, side0, g in (
            (0, xl, own_left, x0l, G_L),
            (1 + size_x, xr, own_right, x0r, G_R),
        ):
            for y in range(0, size_y, TILE):
                density = side[5 * size_y + y : 5 * size_y + y + TILE] + total(
                    [own[j * size_y + y : j * size_y + y + TILE] for j in range(5)]
                )
                for at, row in ((0, yd), (size_y - 1, yu)):
                    if y <= at < y + TILE:
                        more = row[end + g : end + g + 1]
                        density = density + jnp.where(row_of == at - y, more, 0.0)
                pot[x, TILE + y : 2 * TILE + y] = potential_of(
                    density,
                    side0[size_y + y : size_y + y + TILE] > 0.5,
                    side0[y : y + TILE],
                )
        for y, side, own, side0 in (
            (TILE - 1, yd, own_down, y0d),
            (TILE + size_y, yu, own_up, y0u),
        ):
            density = side[5 * size_x : 6 * size_x] + total(
                [own[j * size_x : (j + 1) * size_x] for j in range(5)]
            )
            value = potential_of(density, side0[size_x : 2 * size_x] > 0.5, side0[:size_x])
            for x in range(size_x):
                pot[1 + x, y : y + 1] = value[x : x + 1]
            for x, rc, g, i in ((0, RC_L, G_L, 0), (1 + size_x, RC_R, G_R, 1)):
                density = side[end + rc : end + rc + 1] + own[end + g : end + g + 1]
                row = 2 * size_x + i
                pot[x, y : y + 1] = potential_of(
                    density, side0[row + 2 : row + 3] > 0.5, side0[row : row + 1]
                )

    post = Layers(post_out, None, size_x, edge2)
    speed = Layers(rest, None, size_x, edge2) if last else None
    collide_layers(edge2, rates, f, bits_ref, pot, sides, post, speed)
    rho = None if last else Layers(rest, None, size_x, edge1)
    stream_layers(edge1, bits_ref, post, Layers(f_out, None, size_x, edge1), rho)

    at = (5 if last else 6) * size_y
    for i, (ref, x, ks, dirs) in enumerate(
        ((left_ref, 0, LEFT, corner_pops(-1)), (right_ref, size_x - 1, RIGHT, corner_pops(1)))
    ):
        for j, k in enumerate(ks):
            _, ey, ez = SHIFT[k]
            for y in range(0, size_y, TILE):
                row = j * size_y + y
                ref[row : row + TILE] = roll_z(post.load(x, TILE + y - ey, k), ez)
        ref[at : at + TILE] = jnp.zeros((TILE, size_z), jnp.float32)
        ref[at + C_UP : at + C_UP + 1] = post.row(x, TILE + size_y - 1, dirs[0])
        ref[at + C_DN : at + C_DN + 1] = post.row(x, TILE, dirs[1])
        if not last:
            ref[5 * size_y : 6 * size_y] = rest[i]
            for h, y, leave in ((H_UP, size_y - 1, UP), (H_DN, 0, DOWN)):
                ref[at + h : at + h + 1] = total(
                    [
                        roll_z(post.row(x - SHIFT[k][0], TILE + y, k), SHIFT[k][2])
                        for k in leave
                        if 0 <= x - SHIFT[k][0] < size_x
                    ]
                )


def middle_kernel(first, last, *refs):
    refs = list(refs)
    take = lambda count: [refs.pop(0) for _ in range(count)]
    rates, bits_ref, pot, post_edge, edge_rest = take(5)
    if first:
        f_ref = take(1)[0]
    else:
        f_edge, f_middle, yd, yu = take(4)
    f_out, up_ref, down_ref, rest = take(4)
    post_middle = take(1)[0]
    size_x, size_y, size_z = bits_ref.shape
    edge2, edge1 = two_layers(size_x), one_layer(size_x)
    sides = None
    if first:
        f = lambda k, x, y: f_ref[k, x, y : y + TILE]
    else:
        sides = (None, None, yd, yu)
        held = Layers(f_edge, f_middle, size_x, edge1)
        f = lambda k, x, y: held.load(x, y, k)
    clear_outside(post_middle, size_x - len(edge2), size_y)
    post = Layers(post_edge, post_middle, size_x, edge2)
    speed = None
    if last:
        speed = Layers(None, None, size_x, [])
        speed.store = lambda x, y, value, c: rest.__setitem__((c, turned(x, y, size_x)), value)
        for c in range(3):
            for i, x in enumerate(edge2):
                for y in range(0, size_y, TILE):
                    rest[c, turned(x, y, size_x)] = edge_rest[c, i, y : y + TILE]
    inner = [x for x in range(size_x) if x not in edge2]
    collide_layers(inner, rates, f, bits_ref, pot, sides, post, speed)
    rho = None if last else Layers(edge_rest, rest, size_x, edge1)
    inner = [x for x in range(size_x) if x not in edge1]
    stream_layers(inner, bits_ref, post, Layers(None, f_out, size_x, edge1), rho)
    for ref, y, ks in ((up_ref, size_y - 1, UP), (down_ref, 0, DOWN)):
        for j, k in enumerate(ks):
            ex, _, ez = SHIFT[k]
            for x in range(size_x):
                row = j * size_x + x
                if 0 <= x - ex < size_x:
                    ref[row : row + 1] = post.row(x - ex, TILE + y, k)
                else:
                    ref[row : row + 1] = jnp.zeros((1, size_z), jnp.float32)
            if ez != 0:
                rows = slice(j * size_x, (j + 1) * size_x)
                ref[rows] = roll_z(ref[rows], ez)
        if not last:
            for x in range(size_x):
                ref[5 * size_x + x : 5 * size_x + x + 1] = rho.row(x, y)


def pack_kernel(last, size_x, size_y, *refs):
    up_in, down_in, xl, xr, own_right, own_left, up_ref, down_ref = refs
    parts = 5 if last else 6
    at = parts * size_y
    for ref, source, y, ks, c, h in (
        (up_ref, up_in, size_y - 1, UP, C_UP, H_UP),
        (down_ref, down_in, 0, DOWN, C_DN, H_DN),
    ):
        ref[...] = jnp.zeros(ref.shape, jnp.float32)
        ref[: parts * size_x] = source[: parts * size_x]
        for side, own, x, ex, rc, g in (
            (xl, own_left, 0, 1, RC_L, G_L),
            (xr, own_right, size_x - 1, -1, RC_R, G_R),
        ):
            j = [i for i, k in enumerate(ks) if SHIFT[k][0] == ex][0]
            row = j * size_x + x
            ref[row : row + 1] = side[at + c : at + c + 1]
            if not last:
                row = 5 * size_x + x
                ref[row : row + 1] = source[row : row + 1] + total(
                    [side[i * size_y + y : i * size_y + y + 1] for i in range(5)]
                )
                row = 6 * size_x
                ref[row + rc : row + rc + 1] = side[5 * size_y + y : 5 * size_y + y + 1] + total(
                    [own[i * size_y + y : i * size_y + y + 1] for i in range(5)]
                )
                ref[row + g : row + g + 1] = (
                    side[at + h : at + h + 1] + own[at + c : at + c + 1]
                )


def turned(layer, row, layers):
    return pl.ds(layer + row * layers, TILE, stride=layers)


def write_kernel(f_edge, f_middle, bits_ref, xl, xr, out_hbm, flat_ref, sems):
    size_x, size_y, _ = bits_ref.shape
    held = Layers(f_edge, f_middle, size_x, one_layer(size_x))
    copies = []
    for k in range(N):
        for x in range(size_x):
            for y in range(0, size_y, TILE):
                value = held.load(x, y, k)
                for at, side, ks in ((0, xl, RIGHT), (size_x - 1, xr, LEFT)):
                    if x == at and k in ks:
                        row = ks.index(k) * size_y + y
                        value = value + side[row : row + TILE]
                value = jnp.where(fluid_at(bits_ref, x, y), value, 0.0)
                flat_ref[k, turned(x, y, size_x)] = value
        copies.append(pltpu.make_async_copy(flat_ref.at[k], out_hbm.at[k], sems.at[k]))
        copies[-1].start()
    for copy in copies:
        copy.wait()


def end_kernel(out_in, flat_ref, mask_ref, yd, yu, out_hbm, planes, sems):
    del out_in
    layers = planes.shape[1]
    last = flat_ref.shape[1] - layers
    copies = []
    for at, side, ks in ((0, yd, UP), (last, yu, DOWN)):
        for j, k in enumerate(ks):
            i = len(copies)
            entering = side[j * layers : (j + 1) * layers]
            fluid = mask_ref[0, at : at + layers] > 0.5
            planes[i] = jnp.where(fluid, flat_ref[k, at : at + layers] + entering, 0.0)
            target = out_hbm.at[k, pl.ds(at, layers)]
            copies.append(pltpu.make_async_copy(planes.at[i], target, sems.at[i]))
            copies[-1].start()
    for copy in copies:
        copy.wait()


VMEM = pl.BlockSpec(memory_space=pltpu.VMEM)
SMEM = pl.BlockSpec(memory_space=pltpu.SMEM)
HBM = pl.BlockSpec(memory_space=pltpu.HBM)


def call(kernel, outs, args, special=None, special_out=None, scratch=(), cost=None, **kwargs):
    special, special_out = special or {}, special_out or {}
    return pl.pallas_call(
        kernel,
        out_shape=[jax.ShapeDtypeStruct(shape, dtype) for shape, dtype in outs],
        in_specs=[special.get(i, VMEM) for i in range(len(args))],
        out_specs=[special_out.get(i, VMEM) for i in range(len(outs))],
        scratch_shapes=[
            pltpu.VMEM(item, jnp.float32) if isinstance(item, tuple) else item for item in scratch
        ],
        compiler_params=pltpu.CompilerParams(vmem_limit_bytes=16 * 2**20),
        cost_estimate=cost,
        **kwargs,
    )(*args)


def shift(forward, backward, axis):
    count = lax.axis_size(axis)
    ahead = [(i, (i + 1) % count) for i in range(count)]
    return (
        lax.ppermute(forward, axis, ahead),
        lax.ppermute(backward, axis, [(b, a) for a, b in ahead]),
    )


def per_device(populations, fluid_mask, wet_class, wall_potential, relax_rates):
    rows_x, rows_y, size_z = fluid_mask.shape
    size_x, size_y = rows_y, rows_x
    cells = size_x * size_y
    f32, i32 = jnp.float32, jnp.int32
    whole = ((size_x, size_y, size_z), f32)
    rows = lambda count: ((count, size_z), f32)
    fields = lambda count: ((N, count, size_y, size_z), f32)
    flat = lambda count: ((count, cells, size_z), f32)
    padded = (size_x + 2, size_y + PAD, size_z)
    operations = 400 * cells * size_z
    cost = pl.CostEstimate(flops=operations, bytes_accessed=4 * operations // 20, transcendentals=0)

    operands = [
        pltpu.with_memory_space_constraint(item, pltpu.HBM)
        for item in (
            populations.reshape(N, cells, size_z),
            fluid_mask.reshape(cells, size_z),
            wet_class.reshape(cells, size_z),
            wall_potential,
        )
    ]
    raw, flat_mask, mask, pot0, right, left = call(
        start_kernel,
        [flat(N), flat(2), whole, whole, rows(2 * size_y), rows(2 * size_y)],
        operands,
        special={i: HBM for i in range(4)},
        scratch=[
            pltpu.VMEM((cells, size_z), i32),
            pltpu.VMEM((cells, size_z), i32),
            pltpu.SMEM(wall_potential.shape, f32),
            pltpu.SemaphoreType.DMA((N,)),
            pltpu.SemaphoreType.DMA((3,)),
        ],
    )
    x0l, x0r = shift(right, left, "gy")
    (f,) = call(turn_kernel, [fields(size_x)], (raw,), cost=cost)
    up, down = call(start_pack_kernel, [rows(2 * size_x + TILE)] * 2, (pot0, mask, x0l, x0r))
    y0d, y0u = shift(up, down, "gx")
    (bits,) = call(
        bits_kernel,
        [((size_x, size_y, size_z), i32)],
        (mask, x0l, x0r, y0d, y0u),
        scratch=[padded],
    )
    edge2, edge1 = len(two_layers(size_x)), len(one_layer(size_x))
    held, sent = (f,), ()
    for step in range(STEPS):
        first, last = step == 0, step == STEPS - 1
        parts = 5 if last else 6
        x_rows, y_rows = rows(parts * size_y + TILE), rows(parts * size_x + (0 if last else TILE))
        pot, post, f_edge, right, left, rest = call(
            functools.partial(edge_kernel, first, last),
            [
                (padded, f32),
                ((N, edge2, size_y + PAD, size_z), f32),
                fields(edge1),
                x_rows,
                x_rows,
                ((3, edge2, size_y, size_z) if last else (edge1, size_y, size_z), f32),
            ],
            (relax_rates, bits, pot0, x0l, x0r, y0d, y0u, *held, *sent),
            special={0: SMEM},
            cost=cost,
        )
        xl, xr = shift(right, left, "gy")
        f_middle, up, down, more = call(
            functools.partial(middle_kernel, first, last),
            [
                fields(size_x - edge1),
                y_rows,
                y_rows,
                flat(3) if last else ((size_x - edge1, size_y, size_z), f32),
            ],
            (relax_rates, bits, pot, post, rest, *held[:2], *sent[2:4]),
            special={0: SMEM},
            scratch=[(N, size_x - edge2, size_y + PAD, size_z)],
            cost=cost,
        )
        up, down = call(
            functools.partial(pack_kernel, last, size_x, size_y),
            [y_rows, y_rows],
            (up, down, xl, xr, right, left),
        )
        yd, yu = shift(up, down, "gx")
        held = (f_edge, f_middle, rest, more)
        sent = (xl, xr, yd, yu, right, left, up, down)
    out, flat_f = call(
        write_kernel,
        [flat(N), flat(N)],
        (f_edge, f_middle, bits, xl, xr),
        special_out={0: HBM},
        scratch=[pltpu.SemaphoreType.DMA((N,))],
        cost=cost,
    )
    (out,) = call(
        end_kernel,
        [flat(N)],
        (out, flat_f, flat_mask, yd, yu),
        special={0: HBM},
        special_out={0: HBM},
        scratch=[(10, size_x, size_z), pltpu.SemaphoreType.DMA((10,))],
        input_output_aliases={0: 0},
    )
    shape = (rows_x, rows_y, size_z)
    return out.reshape(N, *shape), more.reshape(3, *shape)


def solution(mesh):
    return jax.shard_map(
        per_device,
        mesh=mesh,
        in_specs=(
            P(None, ("groups", "gx"), "gy", None),
            P(("groups", "gx"), "gy", None),
            P(("groups", "gx"), "gy", None),
            P("groups"),
            P(),
        ),
        out_specs=(P(None, ("groups", "gx"), "gy", None), P(None, ("groups", "gx"), "gy", None)),
        check_vma=False,
    )
```

```python
import functools

import jax
import jax.numpy as jnp
from jax import lax
from jax.experimental import pallas as pl
from jax.experimental.pallas import tpu as pltpu
from jax.sharding import PartitionSpec as P

STEPS = 4
STRENGTH = 2.5
VELOCITY = (
    (0, 0, 0),
    (1, 0, 0),
    (-1, 0, 0),
    (0, 1, 0),
    (0, -1, 0),
    (0, 0, 1),
    (0, 0, -1),
    (1, 1, 0),
    (-1, -1, 0),
    (1, -1, 0),
    (-1, 1, 0),
    (1, 0, 1),
    (-1, 0, -1),
    (1, 0, -1),
    (-1, 0, 1),
    (0, 1, 1),
    (0, -1, -1),
    (0, 1, -1),
    (0, -1, 1),
)
N = len(VELOCITY)
OPPOSITE = [0] + [k + 1 if k % 2 == 1 else k - 1 for k in range(1, N)]
SHIFT = [(y, x, z) for x, y, z in VELOCITY]
RIGHT = [k for k in range(N) if SHIFT[k][0] == 1]
LEFT = [k for k in range(N) if SHIFT[k][0] == -1]
UP = [k for k in range(N) if SHIFT[k][1] == 1]
DOWN = [k for k in range(N) if SHIFT[k][1] == -1]
TILE = 8
PAD = 2 * TILE

C_UP, C_DN, H_UP, H_DN = 0, 1, 2, 3
RC_L, RC_R, G_L, G_R = 0, 1, 2, 3


def roll_z(value, step):
    if step == 0:
        return value
    return pltpu.roll(value, step % value.shape[-1], value.ndim - 1)


def total(values):
    values = list(values)
    while len(values) > 1:
        values = [
            values[i] + values[i + 1] if i + 1 < len(values) else values[i]
            for i in range(0, len(values), 2)
        ]
    return values[0]


def potential_of(density, fluid, solid_value):
    return jnp.where(fluid, 1.0 - jnp.exp(-density), solid_value)


def collide(f, fluid, force, rate):
    fx, fy, fz = force
    s = {k: f[k] + f[k + 1] for k in range(1, N, 2)}
    d = {k: f[k] - f[k + 1] for k in range(1, N, 2)}
    xxyy, xxzz, yyzz = s[7] + s[9], s[11] + s[13], s[15] + s[17]
    xy, xz, yz = s[7] - s[9], s[11] - s[13], s[15] - s[17]
    xyy, yxx = d[7] + d[9], d[7] - d[9]
    xzz, zxx = d[11] + d[13], d[11] - d[13]
    yzz, zyy = d[15] + d[17], d[15] - d[17]
    jx, jy, jz = d[1] + (xyy + xzz), d[3] + (yxx + yzz), d[5] + (zxx + zyy)
    xx, yy, zz = s[1] + (xxyy + xxzz), s[3] + (xxyy + yyzz), s[5] + (xxzz + yyzz)
    rho = (f[0] + s[1]) + (s[3] + s[5]) + (xxyy + (xxzz + yyzz))
    safe = jnp.where(fluid, rho, 1.0)
    inverse = 1.0 / safe
    hx, hy, hz = 0.5 * fx, 0.5 * fy, 0.5 * fz
    gx, gy, gz = jx + hx, jy + hy, jz + hz
    ux, uy, uz = gx * inverse, gy * inverse, gz * inverse
    third = safe * (1.0 / 3.0)
    ninth = safe * (1.0 / 9.0)
    px, py, pz = gx - fx, gy - fy, gz - fz
    txx, tyy, tzz = ux * px, uy * py, uz * pz
    sx, sy, sz = ux * fx, uy * fy, uz * fz
    pxy = ux * fy + uy * fx
    pxz = ux * fz + uz * fx
    pyz = uy * fz + uz * fy
    t3, s3 = (txx + tyy + tzz) * (1.0 / 3.0), (sx + sy + sz) * (2.0 / 3.0)
    rho = rho - rate(0) * (rho - safe)
    nx = jx + fx - rate(1) * (jx - safe * ux + hx)
    ny = jy + fy - rate(2) * (jy - safe * uy + hy)
    nz = jz + fz - rate(3) * (jz - safe * uz + hz)
    xy = xy + rate(4) * (gx * uy - 0.5 * pxy - xy) + pxy
    xz = xz + rate(5) * (gx * uz - 0.5 * pxz - xz) + pxz
    yz = yz + rate(6) * (gy * uz - 0.5 * pyz - yz) + pyz
    xx = xx + rate(7) * (third + txx - xx) + 2.0 * sx
    yy = yy + rate(8) * (third + tyy - yy) + 2.0 * sy
    zz = zz + rate(9) * (third + tzz - zz) + 2.0 * sz
    ex, ey, ez = jx * (1.0 / 3.0), jy * (1.0 / 3.0), jz * (1.0 / 3.0)
    qx, qy, qz = fx * (1.0 / 3.0), fy * (1.0 / 3.0), fz * (1.0 / 3.0)
    xyy = xyy + rate(10) * (ex - xyy) + qx
    xzz = xzz + rate(11) * (ex - xzz) + qx
    yxx = yxx + rate(12) * (ey - yxx) + qy
    yzz = yzz + rate(13) * (ey - yzz) + qy
    zxx = zxx + rate(14) * (ez - zxx) + qz
    zyy = zyy + rate(15) * (ez - zyy) + qz
    base = ninth + t3
    xxyy = xxyy + rate(16) * (base - 0.5 * tzz - xxyy) + (s3 - sz)
    xxzz = xxzz + rate(17) * (base - 0.5 * tyy - xxzz) + (s3 - sy)
    yyzz = yyzz + rate(18) * (base - 0.5 * txx - yyzz) + (s3 - sx)
    out = [None] * N
    for first, even, cross, odd1, odd2 in (
        (7, xxyy, xy, xyy, yxx),
        (11, xxzz, xz, xzz, zxx),
        (15, yyzz, yz, yzz, zyy),
    ):
        even, cross, odd1, odd2 = 0.25 * even, 0.25 * cross, 0.25 * odd1, 0.25 * odd2
        plus, minus = even + cross, even - cross
        both, diff = odd1 + odd2, odd1 - odd2
        out[first], out[first + 1] = plus + both, plus - both
        out[first + 2], out[first + 3] = minus + diff, minus - diff
    pairs = []
    for first, even, odd in (
        (1, xx - (xxyy + xxzz), nx - (xyy + xzz)),
        (3, yy - (xxyy + yyzz), ny - (yxx + yzz)),
        (5, zz - (xxzz + yyzz), nz - (zxx + zyy)),
    ):
        half_even, half_odd = 0.5 * even, 0.5 * odd
        out[first], out[first + 1] = half_even + half_odd, half_even - half_odd
        pairs.append(even)
    out[0] = rho - (pairs[0] + pairs[1] + pairs[2]) - (xxyy + xxzz + yyzz)
    return out, (ux, uy, uz)


def corner_pops(side):
    return SHIFT.index((side, 1, 0)), SHIFT.index((side, -1, 0))


def start_kernel(f_hbm, mask_hbm, wet_hbm, wall_hbm, raw_ref, flat_ref, mask_ref, pot_ref, right_ref, left_ref, *scratch):
    mask_in, wet_in, wall_in, f_sems, sems = scratch
    layers, rows = mask_ref.shape[0], mask_ref.shape[1]
    small = [
        pltpu.make_async_copy(source, target, sems.at[i])
        for i, (source, target) in enumerate(
            ((wall_hbm, wall_in), (mask_hbm, mask_in), (wet_hbm, wet_in))
        )
    ]
    large = [pltpu.make_async_copy(f_hbm.at[k], raw_ref.at[k], f_sems.at[k]) for k in range(N)]
    for copy in small + large:
        copy.start()
    for copy in small:
        copy.wait()
    blocks = [slice(i, i + TILE) for i in range(0, layers * rows, TILE)]
    for at in blocks:
        wet = wet_in[at]
        wall = jnp.zeros(wet.shape, jnp.float32)
        for c in range(wall_in.shape[0]):
            wall = jnp.where(wet == c, wall_in[c], wall)
        flat_ref[1, at] = wall
        flat_ref[0, at] = jnp.where(mask_in[at] == 1, 1.0, 0.0)
    density = None
    for k, copy in enumerate(large):
        copy.wait()
        here = [raw_ref[k, at] for at in blocks]
        density = here if density is None else [a + b for a, b in zip(density, here)]
    for at, value in zip(blocks, density):
        flat_ref[1, at] = potential_of(value, flat_ref[0, at] > 0.5, flat_ref[1, at])
    for i in range(layers):
        mask_ref[i] = flat_ref[0, pl.ds(i, rows, stride=layers)]
        pot_ref[i] = flat_ref[1, pl.ds(i, rows, stride=layers)]
    for ref, i in ((right_ref, layers - 1), (left_ref, 0)):
        ref[:rows] = pot_ref[i]
        ref[rows:] = mask_ref[i]


def turn_kernel(raw_ref, f_ref):
    layers, rows = f_ref.shape[1], f_ref.shape[2]
    for k in range(N):
        for i in range(layers):
            f_ref[k, i] = raw_ref[k, pl.ds(i, rows, stride=layers)]


def start_pack_kernel(pot_ref, mask_ref, from_left, from_right, up_ref, down_ref):
    size_x, size_y = mask_ref.shape[0], mask_ref.shape[1]
    for ref, y in ((up_ref, size_y - 1), (down_ref, 0)):
        ref[2 * size_x :] = jnp.zeros((TILE, ref.shape[1]), jnp.float32)
        for x in range(size_x):
            ref[x : x + 1] = pot_ref[x, y : y + 1]
            ref[size_x + x : size_x + x + 1] = mask_ref[x, y : y + 1]
        for i, side in enumerate((from_left, from_right)):
            row = 2 * size_x + i
            ref[row : row + 1] = side[y : y + 1]
            ref[row + 2 : row + 3] = side[size_y + y : size_y + y + 1]


def bits_kernel(mask_ref, x0l, x0r, bits_ref, pad_ref):
    size_x, size_y, size_z = mask_ref.shape
    nothing = jnp.zeros((TILE, size_z), jnp.float32)
    for x in range(size_x + 2):
        pad_ref[x, :TILE] = nothing
        pad_ref[x, TILE + size_y :] = nothing
    for x in range(size_x):
        pad_ref[1 + x, TILE : TILE + size_y] = mask_ref[x]
    for x, side in ((0, x0l), (1 + size_x, x0r)):
        pad_ref[x, TILE : TILE + size_y] = side[size_y:]
    for x in range(size_x):
        for y in range(0, size_y, TILE):
            bits = jnp.zeros((TILE, size_z), jnp.int32)
            for k in range(N):
                ex, ey, ez = SHIFT[k]
                row = TILE + y - ey
                source = roll_z(pad_ref[1 + x - ex, row : row + TILE], ez)
                bits = bits | jnp.where(source > 0.5, 1 << k, 0)
            bits_ref[x, y : y + TILE] = bits


def more_bits_kernel(bits_in, y0d, y0u, bits_ref, pad_ref):
    size_x, size_y, size_z = bits_ref.shape
    row_of = lax.broadcasted_iota(jnp.int32, (TILE, size_z), 0)
    found = []
    for i, (side, ks) in enumerate(((y0d, UP), (y0u, DOWN))):
        pad_ref[i, TILE : TILE + size_x] = side[size_x : 2 * size_x]
        for row, x in ((TILE - 1, 2 * size_x + 2), (TILE + size_x, 2 * size_x + 3)):
            pad_ref[i, row : row + 1] = side[x : x + 1]
        bits = jnp.zeros((size_x, size_z), jnp.int32)
        for k in ks:
            ex, _, ez = SHIFT[k]
            source = roll_z(pad_ref[i, TILE - ex : TILE - ex + size_x], ez)
            bits = bits | jnp.where(source > 0.5, 1 << k, 0)
        found.append(bits)
    for x in range(size_x):
        for y in range(0, size_y, TILE):
            bits = bits_in[x, y : y + TILE]
            for at, more in ((0, found[0]), (size_y - 1, found[1])):
                if y <= at < y + TILE:
                    bits = bits | jnp.where(row_of == at - y, more[x : x + 1], 0)
            bits_ref[x, y : y + TILE] = bits


class Layers:
    def __init__(self, edge_ref, middle_ref, size_x, edge):
        self.where = {}
        middle = [x for x in range(size_x) if x not in edge]
        for ref, xs in ((edge_ref, edge), (middle_ref, middle)):
            for i, x in enumerate(xs):
                self.where[x] = (ref, i)

    def load(self, x, y, k=None):
        ref, i = self.where[x]
        return ref[i, y : y + TILE] if k is None else ref[k, i, y : y + TILE]

    def row(self, x, y, k=None):
        ref, i = self.where[x]
        return ref[i, y : y + 1] if k is None else ref[k, i, y : y + 1]

    def store(self, x, y, value, k=None):
        ref, i = self.where[x]
        if k is None:
            ref[i, y : y + TILE] = value
        else:
            ref[k, i, y : y + TILE] = value


def two_layers(size_x):
    return [0, 1, size_x - 2, size_x - 1]


def one_layer(size_x):
    return [0, size_x - 1]


def fluid_at(bits_ref, x, y):
    return (bits_ref[x, y : y + TILE] & 1) != 0


def clear_outside(post, layers, size_y):
    nothing = jnp.zeros((TILE, post.shape[-1]), jnp.float32)
    for i in range(layers):
        for k in UP:
            post[k, i, :TILE] = nothing
        for k in DOWN:
            post[k, i, TILE + size_y :] = nothing


def collide_layers(xs, rates, f, bits_ref, pot, sides, post, speed):
    size_x, size_y, size_z = bits_ref.shape
    row_of = lax.broadcasted_iota(jnp.int32, (TILE, size_z), 0)
    for x in xs:
        for y in range(0, size_y, TILE):
            near = {
                (i, j): pot[1 + x + i, TILE + y + j : 2 * TILE + y + j]
                for i in (-1, 0, 1)
                for j in (-1, 0, 1)
            }
            scale = near[0, 0] * (STRENGTH / 36.0)
            dx = near[1, 0] - near[-1, 0]
            dy = near[0, 1] - near[0, -1]
            pp, pm, mp, mm = near[1, 1], near[1, -1], near[-1, 1], near[-1, -1]
            both = near[1, 0] + near[-1, 0] + near[0, 1] + near[0, -1] + 2.0 * near[0, 0]
            diag1, diag2 = pp - mm, pm - mp
            force = (
                scale * (2.0 * dy + (diag1 - diag2) + (roll_z(dy, 1) + roll_z(dy, -1))),
                scale * (2.0 * dx + (diag1 + diag2) + (roll_z(dx, 1) + roll_z(dx, -1))),
                scale * (roll_z(both, -1) - roll_z(both, 1)),
            )
            now = [f(k, x, y) for k in range(N)]
            if sides is not None:
                xl, xr, yd, yu = sides
                for at, side, ks in ((0, xl, RIGHT), (size_x - 1, xr, LEFT)):
                    if x == at:
                        for j, k in enumerate(ks):
                            now[k] = now[k] + side[j * size_y + y : j * size_y + y + TILE]
                for at, side, ks in ((0, yd, UP), (size_y - 1, yu, DOWN)):
                    if y <= at < y + TILE:
                        for j, k in enumerate(ks):
                            entering = side[j * size_x + x : j * size_x + x + 1]
                            now[k] = now[k] + jnp.where(row_of == at - y, entering, 0.0)
            fluid = fluid_at(bits_ref, x, y)
            after, at_speed = collide(now, fluid, force, lambda r: rates[r])
            for k in range(N):
                post.store(x, TILE + y, jnp.where(fluid, after[k], 0.0), k)
            if speed is not None:
                for c in range(3):
                    speed.store(x, y, jnp.where(fluid, at_speed[c], 0.0), c)


def stream_layers(xs, bits_ref, post, f, rho):
    size_x, size_y, _ = bits_ref.shape
    for x in xs:
        for y in range(0, size_y, TILE):
            bits = bits_ref[x, y : y + TILE]
            arrived = []
            for k in range(N):
                ex, ey, ez = SHIFT[k]
                value = post.load(x, TILE + y, OPPOSITE[k])
                if k > 0:
                    come = 0.0
                    if 0 <= x - ex < size_x:
                        come = roll_z(post.load(x - ex, TILE + y - ey, k), ez)
                    value = jnp.where((bits & (1 << k)) != 0, come, value)
                f.store(x, y, value, k)
                arrived.append(value)
            if rho is not None:
                rho.store(x, y, total(arrived))


def edge_kernel(first, last, *refs):
    refs = list(refs)
    take = lambda count: [refs.pop(0) for _ in range(count)]
    rates, bits_ref, pot0_ref, x0l, x0r, y0d, y0u = take(7)
    if first:
        f_ref = take(1)[0]
    else:
        f_edge, f_middle, rho_edge, rho_middle, xl, xr, yd, yu = take(8)
        own_right, own_left, own_up, own_down = take(4)
    pot, post_out, f_out, right_ref, left_ref = take(5)
    rest = take(1)[0]
    size_x, size_y, size_z = bits_ref.shape
    edge2, edge1 = two_layers(size_x), one_layer(size_x)
    sides = None
    if first:
        f = lambda k, x, y: f_ref[k, x, y : y + TILE]
    else:
        sides = (xl, xr, yd, yu)
        held = Layers(f_edge, f_middle, size_x, edge1)
        density_of = Layers(rho_edge, rho_middle, size_x, edge1)
        f = lambda k, x, y: held.load(x, y, k)
    clear_outside(post_out, len(edge2), size_y)

    if first:
        for x in range(size_x):
            pot[1 + x, TILE : TILE + size_y] = pot0_ref[x]
        for x, side in ((0, x0l), (1 + size_x, x0r)):
            pot[x, TILE : TILE + size_y] = side[:size_y]
        for y, side in ((TILE - 1, y0d), (TILE + size_y, y0u)):
            for x in range(size_x):
                pot[1 + x, y : y + 1] = side[x : x + 1]
            for x, row in ((0, 2 * size_x), (1 + size_x, 2 * size_x + 1)):
                pot[x, y : y + 1] = side[row : row + 1]
    else:
        end = 6 * size_x
        row_of = lax.broadcasted_iota(jnp.int32, (TILE, size_z), 0)
        entering = {
            at: total([side[j * size_x : (j + 1) * size_x] for j in range(5)])
            for at, side in ((0, yd), (size_y - 1, yu))
        }
        for x in range(size_x):
            for y in range(0, size_y, TILE):
                density = density_of.load(x, y)
                for at, side in ((0, xl), (size_x - 1, xr)):
                    if x == at:
                        density = density + total(
                            [side[j * size_y + y : j * size_y + y + TILE] for j in range(5)]
                        )
                for at, rows in entering.items():
                    if y <= at < y + TILE:
                        density = density + jnp.where(row_of == at - y, rows[x : x + 1], 0.0)
                pot[1 + x, TILE + y : 2 * TILE + y] = potential_of(
                    density, fluid_at(bits_ref, x, y), pot0_ref[x, y : y + TILE]
                )
        for x, side, own, side0, g in (
            (0, xl, own_left, x0l, G_L),
            (1 + size_x, xr, own_right, x0r, G_R),
        ):
            for y in range(0, size_y, TILE):
                density = side[5 * size_y + y : 5 * size_y + y + TILE] + total(
                    [own[j * size_y + y : j * size_y + y + TILE] for j in range(5)]
                )
                for at, row in ((0, yd), (size_y - 1, yu)):
                    if y <= at < y + TILE:
                        more = row[end + g : end + g + 1]
                        density = density + jnp.where(row_of == at - y, more, 0.0)
                pot[x, TILE + y : 2 * TILE + y] = potential_of(
                    density,
                    side0[size_y + y : size_y + y + TILE] > 0.5,
                    side0[y : y + TILE],
                )
        for y, side, own, side0 in (
            (TILE - 1, yd, own_down, y0d),
            (TILE + size_y, yu, own_up, y0u),
        ):
            density = side[5 * size_x : 6 * size_x] + total(
                [own[j * size_x : (j + 1) * size_x] for j in range(5)]
            )
            value = potential_of(density, side0[size_x : 2 * size_x] > 0.5, side0[:size_x])
            for x in range(size_x):
                pot[1 + x, y : y + 1] = value[x : x + 1]
            for x, rc, g, i in ((0, RC_L, G_L, 0), (1 + size_x, RC_R, G_R, 1)):
                density = side[end + rc : end + rc + 1] + own[end + g : end + g + 1]
                row = 2 * size_x + i
                pot[x, y : y + 1] = potential_of(
                    density, side0[row + 2 : row + 3] > 0.5, side0[row : row + 1]
                )

    post = Layers(post_out, None, size_x, edge2)
    speed = Layers(rest, None, size_x, edge2) if last else None
    collide_layers(edge2, rates, f, bits_ref, pot, sides, post, speed)
    rho = None if last else Layers(rest, None, size_x, edge1)
    stream_layers(edge1, bits_ref, post, Layers(f_out, None, size_x, edge1), rho)

    at = (5 if last else 6) * size_y
    for i, (ref, x, ks, dirs) in enumerate(
        ((left_ref, 0, LEFT, corner_pops(-1)), (right_ref, size_x - 1, RIGHT, corner_pops(1)))
    ):
        for j, k in enumerate(ks):
            _, ey, ez = SHIFT[k]
            for y in range(0, size_y, TILE):
                row = j * size_y + y
                ref[row : row + TILE] = roll_z(post.load(x, TILE + y - ey, k), ez)
        ref[at : at + TILE] = jnp.zeros((TILE, size_z), jnp.float32)
        ref[at + C_UP : at + C_UP + 1] = post.row(x, TILE + size_y - 1, dirs[0])
        ref[at + C_DN : at + C_DN + 1] = post.row(x, TILE, dirs[1])
        if not last:
            ref[5 * size_y : 6 * size_y] = rest[i]
            for h, y, leave in ((H_UP, size_y - 1, UP), (H_DN, 0, DOWN)):
                ref[at + h : at + h + 1] = total(
                    [
                        roll_z(post.row(x - SHIFT[k][0], TILE + y, k), SHIFT[k][2])
                        for k in leave
                        if 0 <= x - SHIFT[k][0] < size_x
                    ]
                )


def middle_kernel(first, last, *refs):
    refs = list(refs)
    take = lambda count: [refs.pop(0) for _ in range(count)]
    rates, bits_ref, pot, post_edge, edge_rest = take(5)
    if first:
        f_ref = take(1)[0]
    else:
        f_edge, f_middle, yd, yu = take(4)
    f_out, up_ref, down_ref, rest = take(4)
    post_middle = take(1)[0]
    size_x, size_y, size_z = bits_ref.shape
    edge2, edge1 = two_layers(size_x), one_layer(size_x)
    sides = None
    if first:
        f = lambda k, x, y: f_ref[k, x, y : y + TILE]
    else:
        sides = (None, None, yd, yu)
        held = Layers(f_edge, f_middle, size_x, edge1)
        f = lambda k, x, y: held.load(x, y, k)
    clear_outside(post_middle, size_x - len(edge2), size_y)
    post = Layers(post_edge, post_middle, size_x, edge2)
    speed = None
    if last:
        speed = Layers(None, None, size_x, [])
        speed.store = lambda x, y, value, c: rest.__setitem__((c, turned(x, y, size_x)), value)
        for c in range(3):
            for i, x in enumerate(edge2):
                for y in range(0, size_y, TILE):
                    rest[c, turned(x, y, size_x)] = edge_rest[c, i, y : y + TILE]
    inner = [x for x in range(size_x) if x not in edge2]
    collide_layers(inner, rates, f, bits_ref, pot, sides, post, speed)
    rho = None if last else Layers(edge_rest, rest, size_x, edge1)
    inner = [x for x in range(size_x) if x not in edge1]
    stream_layers(inner, bits_ref, post, Layers(None, f_out, size_x, edge1), rho)
    for ref, y, ks in ((up_ref, size_y - 1, UP), (down_ref, 0, DOWN)):
        for j, k in enumerate(ks):
            ex, _, ez = SHIFT[k]
            for x in range(size_x):
                row = j * size_x + x
                if 0 <= x - ex < size_x:
                    ref[row : row + 1] = post.row(x - ex, TILE + y, k)
                else:
                    ref[row : row + 1] = jnp.zeros((1, size_z), jnp.float32)
            if ez != 0:
                rows = slice(j * size_x, (j + 1) * size_x)
                ref[rows] = roll_z(ref[rows], ez)
        if not last:
            for x in range(size_x):
                ref[5 * size_x + x : 5 * size_x + x + 1] = rho.row(x, y)


def pack_kernel(last, size_x, size_y, *refs):
    up_in, down_in, xl, xr, own_right, own_left, up_ref, down_ref = refs
    parts = 5 if last else 6
    at = parts * size_y
    for ref, source, y, ks, c, h in (
        (up_ref, up_in, size_y - 1, UP, C_UP, H_UP),
        (down_ref, down_in, 0, DOWN, C_DN, H_DN),
    ):
        ref[...] = jnp.zeros(ref.shape, jnp.float32)
        ref[: parts * size_x] = source[: parts * size_x]
        for side, own, x, ex, rc, g in (
            (xl, own_left, 0, 1, RC_L, G_L),
            (xr, own_right, size_x - 1, -1, RC_R, G_R),
        ):
            j = [i for i, k in enumerate(ks) if SHIFT[k][0] == ex][0]
            row = j * size_x + x
            ref[row : row + 1] = side[at + c : at + c + 1]
            if not last:
                row = 5 * size_x + x
                ref[row : row + 1] = source[row : row + 1] + total(
                    [side[i * size_y + y : i * size_y + y + 1] for i in range(5)]
                )
                row = 6 * size_x
                ref[row + rc : row + rc + 1] = side[5 * size_y + y : 5 * size_y + y + 1] + total(
                    [own[i * size_y + y : i * size_y + y + 1] for i in range(5)]
                )
                ref[row + g : row + g + 1] = (
                    side[at + h : at + h + 1] + own[at + c : at + c + 1]
                )


def turned(layer, row, layers):
    return pl.ds(layer + row * layers, TILE, stride=layers)


def write_kernel(f_edge, f_middle, bits_ref, xl, xr, speed_ref, out_hbm, flat_ref, speed_hbm, sems, speed_sem):
    size_x, size_y, _ = bits_ref.shape
    held = Layers(f_edge, f_middle, size_x, one_layer(size_x))
    copies = [pltpu.make_async_copy(speed_ref, speed_hbm, speed_sem)]
    copies[0].start()
    for k in range(N):
        for x in range(size_x):
            for y in range(0, size_y, TILE):
                value = held.load(x, y, k)
                for at, side, ks in ((0, xl, RIGHT), (size_x - 1, xr, LEFT)):
                    if x == at and k in ks:
                        row = ks.index(k) * size_y + y
                        value = value + side[row : row + TILE]
                value = jnp.where(fluid_at(bits_ref, x, y), value, 0.0)
                flat_ref[k, turned(x, y, size_x)] = value
        copies.append(pltpu.make_async_copy(flat_ref.at[k], out_hbm.at[k], sems.at[k]))
        copies[-1].start()
    for copy in copies:
        copy.wait()


def end_kernel(out_in, flat_ref, mask_ref, yd, yu, out_hbm, planes, sems):
    del out_in
    layers = planes.shape[1]
    last = flat_ref.shape[1] - layers
    copies = []
    for at, side, ks in ((0, yd, UP), (last, yu, DOWN)):
        for j, k in enumerate(ks):
            i = len(copies)
            entering = side[j * layers : (j + 1) * layers]
            fluid = mask_ref[0, at : at + layers] > 0.5
            planes[i] = jnp.where(fluid, flat_ref[k, at : at + layers] + entering, 0.0)
            target = out_hbm.at[k, pl.ds(at, layers)]
            copies.append(pltpu.make_async_copy(planes.at[i], target, sems.at[i]))
            copies[-1].start()
    for copy in copies:
        copy.wait()


VMEM = pl.BlockSpec(memory_space=pltpu.VMEM)
HBM = pl.BlockSpec(memory_space=pltpu.HBM)


def call(kernel, outs, args, special=None, special_out=None, scratch=(), cost=None, **kwargs):
    special, special_out = special or {}, special_out or {}
    return pl.pallas_call(
        kernel,
        out_shape=[jax.ShapeDtypeStruct(shape, dtype) for shape, dtype in outs],
        in_specs=[special.get(i, VMEM) for i in range(len(args))],
        out_specs=[special_out.get(i, VMEM) for i in range(len(outs))],
        scratch_shapes=[
            pltpu.VMEM(item, jnp.float32) if isinstance(item, tuple) else item for item in scratch
        ],
        compiler_params=pltpu.CompilerParams(vmem_limit_bytes=16 * 2**20),
        cost_estimate=cost,
        **kwargs,
    )(*args)


def shift(forward, backward, axis):
    count = lax.axis_size(axis)
    ahead = [(i, (i + 1) % count) for i in range(count)]
    return (
        lax.ppermute(forward, axis, ahead),
        lax.ppermute(backward, axis, [(b, a) for a, b in ahead]),
    )


def per_device(populations, fluid_mask, wet_class, wall_potential, relax_rates):
    rows_x, rows_y, size_z = fluid_mask.shape
    size_x, size_y = rows_y, rows_x
    cells = size_x * size_y
    f32, i32 = jnp.float32, jnp.int32
    whole = ((size_x, size_y, size_z), f32)
    rows = lambda count: ((count, size_z), f32)
    fields = lambda count: ((N, count, size_y, size_z), f32)
    flat = lambda count: ((count, cells, size_z), f32)
    padded = (size_x + 2, size_y + PAD, size_z)
    operations = 400 * cells * size_z
    cost = pl.CostEstimate(flops=operations, bytes_accessed=4 * operations // 20, transcendentals=0)

    operands = [
        pltpu.with_memory_space_constraint(item, pltpu.HBM)
        for item in (
            populations.reshape(N, cells, size_z),
            fluid_mask.reshape(cells, size_z),
            wet_class.reshape(cells, size_z),
            wall_potential,
        )
    ]
    raw, flat_mask, mask, pot0, right, left = call(
        start_kernel,
        [flat(N), flat(2), whole, whole, rows(2 * size_y), rows(2 * size_y)],
        operands,
        special={i: HBM for i in range(4)},
        scratch=[
            pltpu.VMEM((cells, size_z), i32),
            pltpu.VMEM((cells, size_z), i32),
            pltpu.SMEM(wall_potential.shape, f32),
            pltpu.SemaphoreType.DMA((N,)),
            pltpu.SemaphoreType.DMA((3,)),
        ],
    )
    x0l, x0r = shift(right, left, "gy")
    (f,) = call(turn_kernel, [fields(size_x)], (raw,), cost=cost)
    rates = jnp.broadcast_to(relax_rates[:, None, None], (N, TILE, size_z))
    up, down = call(start_pack_kernel, [rows(2 * size_x + TILE)] * 2, (pot0, mask, x0l, x0r))
    y0d, y0u = shift(up, down, "gx")
    whole_bits = [((size_x, size_y, size_z), i32)]
    (bits,) = call(bits_kernel, whole_bits, (mask, x0l, x0r), scratch=[padded], cost=cost)
    (bits,) = call(
        more_bits_kernel, whole_bits, (bits, y0d, y0u), scratch=[(2, size_x + PAD, size_z)]
    )
    edge2, edge1 = len(two_layers(size_x)), len(one_layer(size_x))
    held, sent = (f,), ()
    for step in range(STEPS):
        first, last = step == 0, step == STEPS - 1
        parts = 5 if last else 6
        x_rows, y_rows = rows(parts * size_y + TILE), rows(parts * size_x + (0 if last else TILE))
        pot, post, f_edge, right, left, rest = call(
            functools.partial(edge_kernel, first, last),
            [
                (padded, f32),
                ((N, edge2, size_y + PAD, size_z), f32),
                fields(edge1),
                x_rows,
                x_rows,
                ((3, edge2, size_y, size_z) if last else (edge1, size_y, size_z), f32),
            ],
            (rates, bits, pot0, x0l, x0r, y0d, y0u, *held, *sent),
            cost=cost,
        )
        xl, xr = shift(right, left, "gy")
        f_middle, up, down, more = call(
            functools.partial(middle_kernel, first, last),
            [
                fields(size_x - edge1),
                y_rows,
                y_rows,
                flat(3) if last else ((size_x - edge1, size_y, size_z), f32),
            ],
            (rates, bits, pot, post, rest, *held[:2], *sent[2:4]),
            scratch=[(N, size_x - edge2, size_y + PAD, size_z)],
            cost=cost,
        )
        up, down = call(
            functools.partial(pack_kernel, last, size_x, size_y),
            [y_rows, y_rows],
            (up, down, xl, xr, right, left),
        )
        yd, yu = shift(up, down, "gx")
        held = (f_edge, f_middle, rest, more)
        sent = (xl, xr, yd, yu, right, left, up, down)
    out, flat_f, speed = call(
        write_kernel,
        [flat(N), flat(N), flat(3)],
        (f_edge, f_middle, bits, xl, xr, more),
        special_out={0: HBM, 2: HBM},
        scratch=[pltpu.SemaphoreType.DMA((N,)), pltpu.SemaphoreType.DMA(())],
        cost=cost,
    )
    (out,) = call(
        end_kernel,
        [flat(N)],
        (out, flat_f, flat_mask, yd, yu),
        special={0: HBM},
        special_out={0: HBM},
        scratch=[(10, size_x, size_z), pltpu.SemaphoreType.DMA((10,))],
        input_output_aliases={0: 0},
    )
    shape = (rows_x, rows_y, size_z)
    return out.reshape(N, *shape), speed.reshape(3, *shape)


def solution(mesh):
    return jax.shard_map(
        per_device,
        mesh=mesh,
        in_specs=(
            P(None, ("groups", "gx"), "gy", None),
            P(("groups", "gx"), "gy", None),
            P(("groups", "gx"), "gy", None),
            P("groups"),
            P(),
        ),
        out_specs=(P(None, ("groups", "gx"), "gy", None), P(None, ("groups", "gx"), "gy", None)),
        check_vma=False,
    )
```

```python
import functools

import jax
import jax.numpy as jnp
from jax import lax
from jax.experimental import pallas as pl
from jax.experimental.pallas import tpu as pltpu
from jax.sharding import PartitionSpec as P

STEPS = 4
STRENGTH = 2.5
VELOCITY = (
    (0, 0, 0),
    (1, 0, 0),
    (-1, 0, 0),
    (0, 1, 0),
    (0, -1, 0),
    (0, 0, 1),
    (0, 0, -1),
    (1, 1, 0),
    (-1, -1, 0),
    (1, -1, 0),
    (-1, 1, 0),
    (1, 0, 1),
    (-1, 0, -1),
    (1, 0, -1),
    (-1, 0, 1),
    (0, 1, 1),
    (0, -1, -1),
    (0, 1, -1),
    (0, -1, 1),
)
N = len(VELOCITY)
OPPOSITE = [0] + [k + 1 if k % 2 == 1 else k - 1 for k in range(1, N)]
SHIFT = [(y, x, z) for x, y, z in VELOCITY]
RIGHT = [k for k in range(N) if SHIFT[k][0] == 1]
LEFT = [k for k in range(N) if SHIFT[k][0] == -1]
UP = [k for k in range(N) if SHIFT[k][1] == 1]
DOWN = [k for k in range(N) if SHIFT[k][1] == -1]
TILE = 8
PAD = 2 * TILE

C_UP, C_DN, H_UP, H_DN = 0, 1, 2, 3
RC_L, RC_R, G_L, G_R = 0, 1, 2, 3


def roll_z(value, step):
    if step == 0:
        return value
    return pltpu.roll(value, step % value.shape[-1], value.ndim - 1)


def total(values):
    values = list(values)
    while len(values) > 1:
        values = [
            values[i] + values[i + 1] if i + 1 < len(values) else values[i]
            for i in range(0, len(values), 2)
        ]
    return values[0]


def potential_of(density, fluid, solid_value):
    return jnp.where(fluid, 1.0 - jnp.exp(-density), solid_value)


def collide(f, fluid, force, rate):
    fx, fy, fz = force
    s = {k: f[k] + f[k + 1] for k in range(1, N, 2)}
    d = {k: f[k] - f[k + 1] for k in range(1, N, 2)}
    xxyy, xxzz, yyzz = s[7] + s[9], s[11] + s[13], s[15] + s[17]
    xy, xz, yz = s[7] - s[9], s[11] - s[13], s[15] - s[17]
    xyy, yxx = d[7] + d[9], d[7] - d[9]
    xzz, zxx = d[11] + d[13], d[11] - d[13]
    yzz, zyy = d[15] + d[17], d[15] - d[17]
    jx, jy, jz = d[1] + (xyy + xzz), d[3] + (yxx + yzz), d[5] + (zxx + zyy)
    xx, yy, zz = s[1] + (xxyy + xxzz), s[3] + (xxyy + yyzz), s[5] + (xxzz + yyzz)
    rho = (f[0] + s[1]) + (s[3] + s[5]) + (xxyy + (xxzz + yyzz))
    safe = jnp.where(fluid, rho, 1.0)
    inverse = 1.0 / safe
    hx, hy, hz = 0.5 * fx, 0.5 * fy, 0.5 * fz
    gx, gy, gz = jx + hx, jy + hy, jz + hz
    ux, uy, uz = gx * inverse, gy * inverse, gz * inverse
    third = safe * (1.0 / 3.0)
    ninth = safe * (1.0 / 9.0)
    px, py, pz = gx - fx, gy - fy, gz - fz
    txx, tyy, tzz = ux * px, uy * py, uz * pz
    sx, sy, sz = ux * fx, uy * fy, uz * fz
    pxy = ux * fy + uy * fx
    pxz = ux * fz + uz * fx
    pyz = uy * fz + uz * fy
    t3, s3 = (txx + tyy + tzz) * (1.0 / 3.0), (sx + sy + sz) * (2.0 / 3.0)
    rho = rho - rate(0) * (rho - safe)
    nx = jx + fx - rate(1) * (jx - safe * ux + hx)
    ny = jy + fy - rate(2) * (jy - safe * uy + hy)
    nz = jz + fz - rate(3) * (jz - safe * uz + hz)
    xy = xy + rate(4) * (gx * uy - 0.5 * pxy - xy) + pxy
    xz = xz + rate(5) * (gx * uz - 0.5 * pxz - xz) + pxz
    yz = yz + rate(6) * (gy * uz - 0.5 * pyz - yz) + pyz
    xx = xx + rate(7) * (third + txx - xx) + 2.0 * sx
    yy = yy + rate(8) * (third + tyy - yy) + 2.0 * sy
    zz = zz + rate(9) * (third + tzz - zz) + 2.0 * sz
    ex, ey, ez = jx * (1.0 / 3.0), jy * (1.0 / 3.0), jz * (1.0 / 3.0)
    qx, qy, qz = fx * (1.0 / 3.0), fy * (1.0 / 3.0), fz * (1.0 / 3.0)
    xyy = xyy + rate(10) * (ex - xyy) + qx
    xzz = xzz + rate(11) * (ex - xzz) + qx
    yxx = yxx + rate(12) * (ey - yxx) + qy
    yzz = yzz + rate(13) * (ey - yzz) + qy
    zxx = zxx + rate(14) * (ez - zxx) + qz
    zyy = zyy + rate(15) * (ez - zyy) + qz
    base = ninth + t3
    xxyy = xxyy + rate(16) * (base - 0.5 * tzz - xxyy) + (s3 - sz)
    xxzz = xxzz + rate(17) * (base - 0.5 * tyy - xxzz) + (s3 - sy)
    yyzz = yyzz + rate(18) * (base - 0.5 * txx - yyzz) + (s3 - sx)
    out = [None] * N
    for first, even, cross, odd1, odd2 in (
        (7, xxyy, xy, xyy, yxx),
        (11, xxzz, xz, xzz, zxx),
        (15, yyzz, yz, yzz, zyy),
    ):
        even, cross, odd1, odd2 = 0.25 * even, 0.25 * cross, 0.25 * odd1, 0.25 * odd2
        plus, minus = even + cross, even - cross
        both, diff = odd1 + odd2, odd1 - odd2
        out[first], out[first + 1] = plus + both, plus - both
        out[first + 2], out[first + 3] = minus + diff, minus - diff
    pairs = []
    for first, even, odd in (
        (1, xx - (xxyy + xxzz), nx - (xyy + xzz)),
        (3, yy - (xxyy + yyzz), ny - (yxx + yzz)),
        (5, zz - (xxzz + yyzz), nz - (zxx + zyy)),
    ):
        half_even, half_odd = 0.5 * even, 0.5 * odd
        out[first], out[first + 1] = half_even + half_odd, half_even - half_odd
        pairs.append(even)
    out[0] = rho - (pairs[0] + pairs[1] + pairs[2]) - (xxyy + xxzz + yyzz)
    return out, (ux, uy, uz)


def corner_pops(side):
    return SHIFT.index((side, 1, 0)), SHIFT.index((side, -1, 0))


def in_swap_order(pairs, right, left):
    if not pairs:
        return right, left
    odd = lax.axis_index("gy") % 2 == 1
    return jnp.where(odd, left, right), jnp.where(odd, right, left)


def sort_received(pairs, a_ref, b_ref, xl_ref, xr_ref):
    if pairs:
        xr_ref[...], xl_ref[...] = in_swap_order(pairs, a_ref[...], b_ref[...])
    else:
        xl_ref[...], xr_ref[...] = a_ref[...], b_ref[...]


def start_kernel(pairs, f_hbm, mask_hbm, wet_hbm, wall_hbm, raw_ref, flat_ref, mask_ref, pot_ref, a_ref, b_ref, *scratch):
    mask_in, wet_in, wall_in, f_sems, sems = scratch
    layers, rows = mask_ref.shape[0], mask_ref.shape[1]
    small = [
        pltpu.make_async_copy(source, target, sems.at[i])
        for i, (source, target) in enumerate(
            ((wall_hbm, wall_in), (mask_hbm, mask_in), (wet_hbm, wet_in))
        )
    ]
    large = [pltpu.make_async_copy(f_hbm.at[k], raw_ref.at[k], f_sems.at[k]) for k in range(N)]
    for copy in small + large:
        copy.start()
    for copy in small:
        copy.wait()
    blocks = [slice(i, i + TILE) for i in range(0, layers * rows, TILE)]
    for at in blocks:
        wet = wet_in[at]
        wall = jnp.zeros(wet.shape, jnp.float32)
        for c in range(wall_in.shape[0]):
            wall = jnp.where(wet == c, wall_in[c], wall)
        flat_ref[1, at] = wall
        flat_ref[0, at] = jnp.where(mask_in[at] == 1, 1.0, 0.0)
    density = None
    for k, copy in enumerate(large):
        copy.wait()
        here = [raw_ref[k, at] for at in blocks]
        density = here if density is None else [a + b for a, b in zip(density, here)]
    for at, value in zip(blocks, density):
        flat_ref[1, at] = potential_of(value, flat_ref[0, at] > 0.5, flat_ref[1, at])
    for i in range(layers):
        mask_ref[i] = flat_ref[0, pl.ds(i, rows, stride=layers)]
        pot_ref[i] = flat_ref[1, pl.ds(i, rows, stride=layers)]
    for ref in (pot_ref, mask_ref):
        at = slice(0, rows) if ref is pot_ref else slice(rows, 2 * rows)
        a_ref[at], b_ref[at] = in_swap_order(pairs, ref[layers - 1], ref[0])


def turn_kernel(raw_ref, f_ref):
    layers, rows = f_ref.shape[1], f_ref.shape[2]
    for k in range(N):
        for i in range(layers):
            f_ref[k, i] = raw_ref[k, pl.ds(i, rows, stride=layers)]


def start_pack_kernel(pairs, pot_ref, mask_ref, a_ref, b_ref, up_ref, down_ref, from_left, from_right):
    size_x, size_y = mask_ref.shape[0], mask_ref.shape[1]
    sort_received(pairs, a_ref, b_ref, from_left, from_right)
    for ref, y in ((up_ref, size_y - 1), (down_ref, 0)):
        ref[2 * size_x :] = jnp.zeros((TILE, ref.shape[1]), jnp.float32)
        for x in range(size_x):
            ref[x : x + 1] = pot_ref[x, y : y + 1]
            ref[size_x + x : size_x + x + 1] = mask_ref[x, y : y + 1]
        for i, side in enumerate((from_left, from_right)):
            row = 2 * size_x + i
            ref[row : row + 1] = side[y : y + 1]
            ref[row + 2 : row + 3] = side[size_y + y : size_y + y + 1]


def bits_kernel(mask_ref, x0l, x0r, bits_ref, pad_ref):
    size_x, size_y, size_z = mask_ref.shape
    nothing = jnp.zeros((TILE, size_z), jnp.float32)
    for x in range(size_x + 2):
        pad_ref[x, :TILE] = nothing
        pad_ref[x, TILE + size_y :] = nothing
    for x in range(size_x):
        pad_ref[1 + x, TILE : TILE + size_y] = mask_ref[x]
    for x, side in ((0, x0l), (1 + size_x, x0r)):
        pad_ref[x, TILE : TILE + size_y] = side[size_y:]
    for x in range(size_x):
        for y in range(0, size_y, TILE):
            bits = jnp.zeros((TILE, size_z), jnp.int32)
            for k in range(N):
                ex, ey, ez = SHIFT[k]
                row = TILE + y - ey
                source = roll_z(pad_ref[1 + x - ex, row : row + TILE], ez)
                bits = bits | jnp.where(source > 0.5, 1 << k, 0)
            bits_ref[x, y : y + TILE] = bits


def more_bits_kernel(bits_in, y0d, y0u, bits_ref, pad_ref):
    size_x, size_y, size_z = bits_ref.shape
    row_of = lax.broadcasted_iota(jnp.int32, (TILE, size_z), 0)
    found = []
    for i, (side, ks) in enumerate(((y0d, UP), (y0u, DOWN))):
        pad_ref[i, TILE : TILE + size_x] = side[size_x : 2 * size_x]
        for row, x in ((TILE - 1, 2 * size_x + 2), (TILE + size_x, 2 * size_x + 3)):
            pad_ref[i, row : row + 1] = side[x : x + 1]
        bits = jnp.zeros((size_x, size_z), jnp.int32)
        for k in ks:
            ex, _, ez = SHIFT[k]
            source = roll_z(pad_ref[i, TILE - ex : TILE - ex + size_x], ez)
            bits = bits | jnp.where(source > 0.5, 1 << k, 0)
        found.append(bits)
    for x in range(size_x):
        for y in range(0, size_y, TILE):
            bits = bits_in[x, y : y + TILE]
            for at, more in ((0, found[0]), (size_y - 1, found[1])):
                if y <= at < y + TILE:
                    bits = bits | jnp.where(row_of == at - y, more[x : x + 1], 0)
            bits_ref[x, y : y + TILE] = bits


class Layers:
    def __init__(self, edge_ref, middle_ref, size_x, edge):
        self.where = {}
        middle = [x for x in range(size_x) if x not in edge]
        for ref, xs in ((edge_ref, edge), (middle_ref, middle)):
            for i, x in enumerate(xs):
                self.where[x] = (ref, i)

    def load(self, x, y, k=None):
        ref, i = self.where[x]
        return ref[i, y : y + TILE] if k is None else ref[k, i, y : y + TILE]

    def row(self, x, y, k=None):
        ref, i = self.where[x]
        return ref[i, y : y + 1] if k is None else ref[k, i, y : y + 1]

    def store(self, x, y, value, k=None):
        ref, i = self.where[x]
        if k is None:
            ref[i, y : y + TILE] = value
        else:
            ref[k, i, y : y + TILE] = value


def two_layers(size_x):
    return [0, 1, size_x - 2, size_x - 1]


def one_layer(size_x):
    return [0, size_x - 1]


def fluid_at(bits_ref, x, y):
    return (bits_ref[x, y : y + TILE] & 1) != 0


def clear_outside(post, layers, size_y):
    nothing = jnp.zeros((TILE, post.shape[-1]), jnp.float32)
    for i in range(layers):
        for k in UP:
            post[k, i, :TILE] = nothing
        for k in DOWN:
            post[k, i, TILE + size_y :] = nothing


def collide_layers(xs, rates, f, bits_ref, pot, sides, post, speed):
    size_x, size_y, size_z = bits_ref.shape
    row_of = lax.broadcasted_iota(jnp.int32, (TILE, size_z), 0)
    for x in xs:
        for y in range(0, size_y, TILE):
            near = {
                (i, j): pot[1 + x + i, TILE + y + j : 2 * TILE + y + j]
                for i in (-1, 0, 1)
                for j in (-1, 0, 1)
            }
            scale = near[0, 0] * (STRENGTH / 36.0)
            dx = near[1, 0] - near[-1, 0]
            dy = near[0, 1] - near[0, -1]
            pp, pm, mp, mm = near[1, 1], near[1, -1], near[-1, 1], near[-1, -1]
            both = near[1, 0] + near[-1, 0] + near[0, 1] + near[0, -1] + 2.0 * near[0, 0]
            diag1, diag2 = pp - mm, pm - mp
            force = (
                scale * (2.0 * dy + (diag1 - diag2) + (roll_z(dy, 1) + roll_z(dy, -1))),
                scale * (2.0 * dx + (diag1 + diag2) + (roll_z(dx, 1) + roll_z(dx, -1))),
                scale * (roll_z(both, -1) - roll_z(both, 1)),
            )
            now = [f(k, x, y) for k in range(N)]
            if sides is not None:
                xl, xr, yd, yu = sides
                for at, side, ks in ((0, xl, RIGHT), (size_x - 1, xr, LEFT)):
                    if x == at:
                        for j, k in enumerate(ks):
                            now[k] = now[k] + side[j * size_y + y : j * size_y + y + TILE]
                for at, side, ks in ((0, yd, UP), (size_y - 1, yu, DOWN)):
                    if y <= at < y + TILE:
                        for j, k in enumerate(ks):
                            entering = side[j * size_x + x : j * size_x + x + 1]
                            now[k] = now[k] + jnp.where(row_of == at - y, entering, 0.0)
            fluid = fluid_at(bits_ref, x, y)
            after, at_speed = collide(now, fluid, force, lambda r: rates[r])
            for k in range(N):
                post.store(x, TILE + y, jnp.where(fluid, after[k], 0.0), k)
            if speed is not None:
                for c in range(3):
                    speed.store(x, y, jnp.where(fluid, at_speed[c], 0.0), c)


def stream_layers(xs, bits_ref, post, f, rho):
    size_x, size_y, _ = bits_ref.shape
    for x in xs:
        for y in range(0, size_y, TILE):
            bits = bits_ref[x, y : y + TILE]
            arrived = []
            for k in range(N):
                ex, ey, ez = SHIFT[k]
                value = post.load(x, TILE + y, OPPOSITE[k])
                if k > 0:
                    come = 0.0
                    if 0 <= x - ex < size_x:
                        come = roll_z(post.load(x - ex, TILE + y - ey, k), ez)
                    value = jnp.where((bits & (1 << k)) != 0, come, value)
                f.store(x, y, value, k)
                arrived.append(value)
            if rho is not None:
                rho.store(x, y, total(arrived))


def edge_kernel(first, last, pairs, *refs):
    refs = list(refs)
    take = lambda count: [refs.pop(0) for _ in range(count)]
    rates, bits_ref, pot0_ref, x0l, x0r, y0d, y0u = take(7)
    if first:
        f_ref = take(1)[0]
    else:
        f_edge, f_middle, rho_edge, rho_middle, xl, xr, yd, yu = take(8)
        own_right, own_left, own_up, own_down = take(4)
    pot, post_out, f_out, right_ref, left_ref, a_ref, b_ref, rest = take(8)
    size_x, size_y, size_z = bits_ref.shape
    edge2, edge1 = two_layers(size_x), one_layer(size_x)
    sides = None
    if first:
        f = lambda k, x, y: f_ref[k, x, y : y + TILE]
    else:
        sides = (xl, xr, yd, yu)
        held = Layers(f_edge, f_middle, size_x, edge1)
        density_of = Layers(rho_edge, rho_middle, size_x, edge1)
        f = lambda k, x, y: held.load(x, y, k)
    clear_outside(post_out, len(edge2), size_y)

    if first:
        for x in range(size_x):
            pot[1 + x, TILE : TILE + size_y] = pot0_ref[x]
        for x, side in ((0, x0l), (1 + size_x, x0r)):
            pot[x, TILE : TILE + size_y] = side[:size_y]
        for y, side in ((TILE - 1, y0d), (TILE + size_y, y0u)):
            for x in range(size_x):
                pot[1 + x, y : y + 1] = side[x : x + 1]
            for x, row in ((0, 2 * size_x), (1 + size_x, 2 * size_x + 1)):
                pot[x, y : y + 1] = side[row : row + 1]
    else:
        end = 6 * size_x
        row_of = lax.broadcasted_iota(jnp.int32, (TILE, size_z), 0)
        entering = {
            at: total([side[j * size_x : (j + 1) * size_x] for j in range(5)])
            for at, side in ((0, yd), (size_y - 1, yu))
        }
        for x in range(size_x):
            for y in range(0, size_y, TILE):
                density = density_of.load(x, y)
                for at, side in ((0, xl), (size_x - 1, xr)):
                    if x == at:
                        density = density + total(
                            [side[j * size_y + y : j * size_y + y + TILE] for j in range(5)]
                        )
                for at, rows in entering.items():
                    if y <= at < y + TILE:
                        density = density + jnp.where(row_of == at - y, rows[x : x + 1], 0.0)
                pot[1 + x, TILE + y : 2 * TILE + y] = potential_of(
                    density, fluid_at(bits_ref, x, y), pot0_ref[x, y : y + TILE]
                )
        for x, side, own, side0, g in (
            (0, xl, own_left, x0l, G_L),
            (1 + size_x, xr, own_right, x0r, G_R),
        ):
            for y in range(0, size_y, TILE):
                density = side[5 * size_y + y : 5 * size_y + y + TILE] + total(
                    [own[j * size_y + y : j * size_y + y + TILE] for j in range(5)]
                )
                for at, row in ((0, yd), (size_y - 1, yu)):
                    if y <= at < y + TILE:
                        more = row[end + g : end + g + 1]
                        density = density + jnp.where(row_of == at - y, more, 0.0)
                pot[x, TILE + y : 2 * TILE + y] = potential_of(
                    density,
                    side0[size_y + y : size_y + y + TILE] > 0.5,
                    side0[y : y + TILE],
                )
        for y, side, own, side0 in (
            (TILE - 1, yd, own_down, y0d),
            (TILE + size_y, yu, own_up, y0u),
        ):
            density = side[5 * size_x : 6 * size_x] + total(
                [own[j * size_x : (j + 1) * size_x] for j in range(5)]
            )
            value = potential_of(density, side0[size_x : 2 * size_x] > 0.5, side0[:size_x])
            for x in range(size_x):
                pot[1 + x, y : y + 1] = value[x : x + 1]
            for x, rc, g, i in ((0, RC_L, G_L, 0), (1 + size_x, RC_R, G_R, 1)):
                density = side[end + rc : end + rc + 1] + own[end + g : end + g + 1]
                row = 2 * size_x + i
                pot[x, y : y + 1] = potential_of(
                    density, side0[row + 2 : row + 3] > 0.5, side0[row : row + 1]
                )

    post = Layers(post_out, None, size_x, edge2)
    speed = Layers(rest, None, size_x, edge2) if last else None
    collide_layers(edge2, rates, f, bits_ref, pot, sides, post, speed)
    rho = None if last else Layers(rest, None, size_x, edge1)
    stream_layers(edge1, bits_ref, post, Layers(f_out, None, size_x, edge1), rho)

    at = (5 if last else 6) * size_y
    for i, (ref, x, ks, dirs) in enumerate(
        ((left_ref, 0, LEFT, corner_pops(-1)), (right_ref, size_x - 1, RIGHT, corner_pops(1)))
    ):
        for j, k in enumerate(ks):
            _, ey, ez = SHIFT[k]
            for y in range(0, size_y, TILE):
                row = j * size_y + y
                ref[row : row + TILE] = roll_z(post.load(x, TILE + y - ey, k), ez)
        ref[at : at + TILE] = jnp.zeros((TILE, size_z), jnp.float32)
        ref[at + C_UP : at + C_UP + 1] = post.row(x, TILE + size_y - 1, dirs[0])
        ref[at + C_DN : at + C_DN + 1] = post.row(x, TILE, dirs[1])
        if not last:
            ref[5 * size_y : 6 * size_y] = rest[i]
            for h, y, leave in ((H_UP, size_y - 1, UP), (H_DN, 0, DOWN)):
                ref[at + h : at + h + 1] = total(
                    [
                        roll_z(post.row(x - SHIFT[k][0], TILE + y, k), SHIFT[k][2])
                        for k in leave
                        if 0 <= x - SHIFT[k][0] < size_x
                    ]
                )
    a_ref[...], b_ref[...] = in_swap_order(pairs, right_ref[...], left_ref[...])


def middle_kernel(first, last, *refs):
    refs = list(refs)
    take = lambda count: [refs.pop(0) for _ in range(count)]
    rates, bits_ref, pot, post_edge, edge_rest = take(5)
    if first:
        f_ref = take(1)[0]
    else:
        f_edge, f_middle, yd, yu = take(4)
    f_out, up_ref, down_ref, rest = take(4)
    post_middle = take(1)[0]
    size_x, size_y, size_z = bits_ref.shape
    edge2, edge1 = two_layers(size_x), one_layer(size_x)
    sides = None
    if first:
        f = lambda k, x, y: f_ref[k, x, y : y + TILE]
    else:
        sides = (None, None, yd, yu)
        held = Layers(f_edge, f_middle, size_x, edge1)
        f = lambda k, x, y: held.load(x, y, k)
    clear_outside(post_middle, size_x - len(edge2), size_y)
    post = Layers(post_edge, post_middle, size_x, edge2)
    speed = None
    if last:
        speed = Layers(None, None, size_x, [])
        speed.store = lambda x, y, value, c: rest.__setitem__((c, turned(x, y, size_x)), value)
        for c in range(3):
            for i, x in enumerate(edge2):
                for y in range(0, size_y, TILE):
                    rest[c, turned(x, y, size_x)] = edge_rest[c, i, y : y + TILE]
    inner = [x for x in range(size_x) if x not in edge2]
    collide_layers(inner, rates, f, bits_ref, pot, sides, post, speed)
    rho = None if last else Layers(edge_rest, rest, size_x, edge1)
    inner = [x for x in range(size_x) if x not in edge1]
    stream_layers(inner, bits_ref, post, Layers(None, f_out, size_x, edge1), rho)
    for ref, y, ks in ((up_ref, size_y - 1, UP), (down_ref, 0, DOWN)):
        for j, k in enumerate(ks):
            ex, _, ez = SHIFT[k]
            for x in range(size_x):
                row = j * size_x + x
                if 0 <= x - ex < size_x:
                    ref[row : row + 1] = post.row(x - ex, TILE + y, k)
                else:
                    ref[row : row + 1] = jnp.zeros((1, size_z), jnp.float32)
            if ez != 0:
                rows = slice(j * size_x, (j + 1) * size_x)
                ref[rows] = roll_z(ref[rows], ez)
        if not last:
            for x in range(size_x):
                ref[5 * size_x + x : 5 * size_x + x + 1] = rho.row(x, y)


def pack_kernel(last, pairs, size_x, size_y, *refs):
    up_in, down_in, a_ref, b_ref, own_right, own_left, up_ref, down_ref, xl, xr = refs
    sort_received(pairs, a_ref, b_ref, xl, xr)
    parts = 5 if last else 6
    at = parts * size_y
    for ref, source, y, ks, c, h in (
        (up_ref, up_in, size_y - 1, UP, C_UP, H_UP),
        (down_ref, down_in, 0, DOWN, C_DN, H_DN),
    ):
        ref[...] = jnp.zeros(ref.shape, jnp.float32)
        ref[: parts * size_x] = source[: parts * size_x]
        for side, own, x, ex, rc, g in (
            (xl, own_left, 0, 1, RC_L, G_L),
            (xr, own_right, size_x - 1, -1, RC_R, G_R),
        ):
            j = [i for i, k in enumerate(ks) if SHIFT[k][0] == ex][0]
            row = j * size_x + x
            ref[row : row + 1] = side[at + c : at + c + 1]
            if not last:
                row = 5 * size_x + x
                ref[row : row + 1] = source[row : row + 1] + total(
                    [side[i * size_y + y : i * size_y + y + 1] for i in range(5)]
                )
                row = 6 * size_x
                ref[row + rc : row + rc + 1] = side[5 * size_y + y : 5 * size_y + y + 1] + total(
                    [own[i * size_y + y : i * size_y + y + 1] for i in range(5)]
                )
                ref[row + g : row + g + 1] = (
                    side[at + h : at + h + 1] + own[at + c : at + c + 1]
                )


def turned(layer, row, layers):
    return pl.ds(layer + row * layers, TILE, stride=layers)


def write_kernel(f_edge, f_middle, bits_ref, xl, xr, speed_ref, out_hbm, flat_ref, speed_hbm, sems, speed_sem):
    size_x, size_y, _ = bits_ref.shape
    held = Layers(f_edge, f_middle, size_x, one_layer(size_x))
    copies = [pltpu.make_async_copy(speed_ref, speed_hbm, speed_sem)]
    copies[0].start()
    for k in range(N):
        for x in range(size_x):
            for y in range(0, size_y, TILE):
                value = held.load(x, y, k)
                for at, side, ks in ((0, xl, RIGHT), (size_x - 1, xr, LEFT)):
                    if x == at and k in ks:
                        row = ks.index(k) * size_y + y
                        value = value + side[row : row + TILE]
                value = jnp.where(fluid_at(bits_ref, x, y), value, 0.0)
                flat_ref[k, turned(x, y, size_x)] = value
        copies.append(pltpu.make_async_copy(flat_ref.at[k], out_hbm.at[k], sems.at[k]))
        copies[-1].start()
    for copy in copies:
        copy.wait()


def end_kernel(out_in, flat_ref, mask_ref, yd, yu, out_hbm, planes, sems):
    del out_in
    layers = planes.shape[1]
    last = flat_ref.shape[1] - layers
    copies = []
    for at, side, ks in ((0, yd, UP), (last, yu, DOWN)):
        for j, k in enumerate(ks):
            i = len(copies)
            entering = side[j * layers : (j + 1) * layers]
            fluid = mask_ref[0, at : at + layers] > 0.5
            planes[i] = jnp.where(fluid, flat_ref[k, at : at + layers] + entering, 0.0)
            target = out_hbm.at[k, pl.ds(at, layers)]
            copies.append(pltpu.make_async_copy(planes.at[i], target, sems.at[i]))
            copies[-1].start()
    for copy in copies:
        copy.wait()


VMEM = pl.BlockSpec(memory_space=pltpu.VMEM)
HBM = pl.BlockSpec(memory_space=pltpu.HBM)


def call(kernel, outs, args, special=None, special_out=None, scratch=(), cost=None, **kwargs):
    special, special_out = special or {}, special_out or {}
    return pl.pallas_call(
        kernel,
        out_shape=[jax.ShapeDtypeStruct(shape, dtype) for shape, dtype in outs],
        in_specs=[special.get(i, VMEM) for i in range(len(args))],
        out_specs=[special_out.get(i, VMEM) for i in range(len(outs))],
        scratch_shapes=[
            pltpu.VMEM(item, jnp.float32) if isinstance(item, tuple) else item for item in scratch
        ],
        compiler_params=pltpu.CompilerParams(vmem_limit_bytes=16 * 2**20),
        cost_estimate=cost,
        **kwargs,
    )(*args)


def shift(forward, backward, axis):
    count = lax.axis_size(axis)
    ahead = [(i, (i + 1) % count) for i in range(count)]
    return (
        lax.ppermute(forward, axis, ahead),
        lax.ppermute(backward, axis, [(b, a) for a, b in ahead]),
    )


def swap(a, b, axis):
    count = lax.axis_size(axis)
    partners = [
        [(i, (i + (1 if i % 2 == parity else -1)) % count) for i in range(count)]
        for parity in range(2)
    ]
    b = lax.ppermute(b, axis, partners[1])
    return lax.ppermute(a, axis, partners[0]), b


def per_device(populations, fluid_mask, wet_class, wall_potential, relax_rates):
    rows_x, rows_y, size_z = fluid_mask.shape
    pairs = lax.axis_size("gy") % 2 == 0
    exchange = swap if pairs else shift
    size_x, size_y = rows_y, rows_x
    cells = size_x * size_y
    f32, i32 = jnp.float32, jnp.int32
    whole = ((size_x, size_y, size_z), f32)
    rows = lambda count: ((count, size_z), f32)
    fields = lambda count: ((N, count, size_y, size_z), f32)
    flat = lambda count: ((count, cells, size_z), f32)
    padded = (size_x + 2, size_y + PAD, size_z)
    operations = 400 * cells * size_z
    cost = pl.CostEstimate(flops=operations, bytes_accessed=4 * operations // 20, transcendentals=0)

    operands = [
        pltpu.with_memory_space_constraint(item, pltpu.HBM)
        for item in (
            populations.reshape(N, cells, size_z),
            fluid_mask.reshape(cells, size_z),
            wet_class.reshape(cells, size_z),
            wall_potential,
        )
    ]
    raw, flat_mask, mask, pot0, a, b = call(
        functools.partial(start_kernel, pairs),
        [flat(N), flat(2), whole, whole, rows(2 * size_y), rows(2 * size_y)],
        operands,
        special={i: HBM for i in range(4)},
        scratch=[
            pltpu.VMEM((cells, size_z), i32),
            pltpu.VMEM((cells, size_z), i32),
            pltpu.SMEM(wall_potential.shape, f32),
            pltpu.SemaphoreType.DMA((N,)),
            pltpu.SemaphoreType.DMA((3,)),
        ],
    )
    a, b = exchange(a, b, "gy")
    (f,) = call(turn_kernel, [fields(size_x)], (raw,), cost=cost)
    rates = jnp.broadcast_to(relax_rates[:, None, None], (N, TILE, size_z))
    up, down, x0l, x0r = call(
        functools.partial(start_pack_kernel, pairs),
        [rows(2 * size_x + TILE)] * 2 + [rows(2 * size_y)] * 2,
        (pot0, mask, a, b),
    )
    y0d, y0u = shift(up, down, "gx")
    whole_bits = [((size_x, size_y, size_z), i32)]
    (bits,) = call(bits_kernel, whole_bits, (mask, x0l, x0r), scratch=[padded], cost=cost)
    (bits,) = call(
        more_bits_kernel, whole_bits, (bits, y0d, y0u), scratch=[(2, size_x + PAD, size_z)]
    )
    edge2, edge1 = len(two_layers(size_x)), len(one_layer(size_x))
    held, sent = (f,), ()
    for step in range(STEPS):
        first, last = step == 0, step == STEPS - 1
        parts = 5 if last else 6
        x_rows, y_rows = rows(parts * size_y + TILE), rows(parts * size_x + (0 if last else TILE))
        pot, post, f_edge, right, left, a, b, rest = call(
            functools.partial(edge_kernel, first, last, pairs),
            [
                (padded, f32),
                ((N, edge2, size_y + PAD, size_z), f32),
                fields(edge1),
                x_rows,
                x_rows,
                x_rows,
                x_rows,
                ((3, edge2, size_y, size_z) if last else (edge1, size_y, size_z), f32),
            ],
            (rates, bits, pot0, x0l, x0r, y0d, y0u, *held, *sent),
            cost=cost,
        )
        a, b = exchange(a, b, "gy")
        f_middle, up, down, more = call(
            functools.partial(middle_kernel, first, last),
            [
                fields(size_x - edge1),
                y_rows,
                y_rows,
                flat(3) if last else ((size_x - edge1, size_y, size_z), f32),
            ],
            (rates, bits, pot, post, rest, *held[:2], *sent[2:4]),
            scratch=[(N, size_x - edge2, size_y + PAD, size_z)],
            cost=cost,
        )
        up, down, xl, xr = call(
            functools.partial(pack_kernel, last, pairs, size_x, size_y),
            [y_rows, y_rows, x_rows, x_rows],
            (up, down, a, b, right, left),
        )
        yd, yu = shift(up, down, "gx")
        held = (f_edge, f_middle, rest, more)
        sent = (xl, xr, yd, yu, right, left, up, down)
    out, flat_f, speed = call(
        write_kernel,
        [flat(N), flat(N), flat(3)],
        (f_edge, f_middle, bits, xl, xr, more),
        special_out={0: HBM, 2: HBM},
        scratch=[pltpu.SemaphoreType.DMA((N,)), pltpu.SemaphoreType.DMA(())],
        cost=cost,
    )
    (out,) = call(
        end_kernel,
        [flat(N)],
        (out, flat_f, flat_mask, yd, yu),
        special={0: HBM},
        special_out={0: HBM},
        scratch=[(10, size_x, size_z), pltpu.SemaphoreType.DMA((10,))],
        input_output_aliases={0: 0},
    )
    shape = (rows_x, rows_y, size_z)
    return out.reshape(N, *shape), speed.reshape(3, *shape)


def solution(mesh):
    return jax.shard_map(
        per_device,
        mesh=mesh,
        in_specs=(
            P(None, ("groups", "gx"), "gy", None),
            P(("groups", "gx"), "gy", None),
            P(("groups", "gx"), "gy", None),
            P("groups"),
            P(),
        ),
        out_specs=(P(None, ("groups", "gx"), "gy", None), P(None, ("groups", "gx"), "gy", None)),
        check_vma=False,
    )
```

```python
import functools

import jax
import jax.numpy as jnp
from jax import lax
from jax.experimental import pallas as pl
from jax.experimental.pallas import tpu as pltpu
from jax.sharding import PartitionSpec as P

STEPS = 4
STRENGTH = 2.5
VELOCITY = (
    (0, 0, 0),
    (1, 0, 0),
    (-1, 0, 0),
    (0, 1, 0),
    (0, -1, 0),
    (0, 0, 1),
    (0, 0, -1),
    (1, 1, 0),
    (-1, -1, 0),
    (1, -1, 0),
    (-1, 1, 0),
    (1, 0, 1),
    (-1, 0, -1),
    (1, 0, -1),
    (-1, 0, 1),
    (0, 1, 1),
    (0, -1, -1),
    (0, 1, -1),
    (0, -1, 1),
)
N = len(VELOCITY)
OPPOSITE = [0] + [k + 1 if k % 2 == 1 else k - 1 for k in range(1, N)]
SHIFT = [(y, x, z) for x, y, z in VELOCITY]
RIGHT = [k for k in range(N) if SHIFT[k][0] == 1]
LEFT = [k for k in range(N) if SHIFT[k][0] == -1]
UP = [k for k in range(N) if SHIFT[k][1] == 1]
DOWN = [k for k in range(N) if SHIFT[k][1] == -1]
TILE = 8
PAD = 2 * TILE

C_UP, C_DN, H_UP, H_DN = 0, 1, 2, 3
RC_L, RC_R, G_L, G_R = 0, 1, 2, 3


def roll_z(value, step):
    if step == 0:
        return value
    return pltpu.roll(value, step % value.shape[-1], value.ndim - 1)


def total(values):
    values = list(values)
    while len(values) > 1:
        values = [
            values[i] + values[i + 1] if i + 1 < len(values) else values[i]
            for i in range(0, len(values), 2)
        ]
    return values[0]


def potential_of(density, fluid, solid_value):
    return jnp.where(fluid, 1.0 - jnp.exp(-density), solid_value)


def collide(f, fluid, force, rate):
    fx, fy, fz = force
    s = {k: f[k] + f[k + 1] for k in range(1, N, 2)}
    d = {k: f[k] - f[k + 1] for k in range(1, N, 2)}
    xxyy, xxzz, yyzz = s[7] + s[9], s[11] + s[13], s[15] + s[17]
    xy, xz, yz = s[7] - s[9], s[11] - s[13], s[15] - s[17]
    xyy, yxx = d[7] + d[9], d[7] - d[9]
    xzz, zxx = d[11] + d[13], d[11] - d[13]
    yzz, zyy = d[15] + d[17], d[15] - d[17]
    jx, jy, jz = d[1] + (xyy + xzz), d[3] + (yxx + yzz), d[5] + (zxx + zyy)
    xx, yy, zz = s[1] + (xxyy + xxzz), s[3] + (xxyy + yyzz), s[5] + (xxzz + yyzz)
    rho = (f[0] + s[1]) + (s[3] + s[5]) + (xxyy + (xxzz + yyzz))
    safe = jnp.where(fluid, rho, 1.0)
    inverse = 1.0 / safe
    hx, hy, hz = 0.5 * fx, 0.5 * fy, 0.5 * fz
    gx, gy, gz = jx + hx, jy + hy, jz + hz
    ux, uy, uz = gx * inverse, gy * inverse, gz * inverse
    third = safe * (1.0 / 3.0)
    ninth = safe * (1.0 / 9.0)
    px, py, pz = gx - fx, gy - fy, gz - fz
    txx, tyy, tzz = ux * px, uy * py, uz * pz
    sx, sy, sz = ux * fx, uy * fy, uz * fz
    pxy = ux * fy + uy * fx
    pxz = ux * fz + uz * fx
    pyz = uy * fz + uz * fy
    t3, s3 = (txx + tyy + tzz) * (1.0 / 3.0), (sx + sy + sz) * (2.0 / 3.0)
    rho = rho - rate(0) * (rho - safe)
    nx = jx + fx - rate(1) * (jx - safe * ux + hx)
    ny = jy + fy - rate(2) * (jy - safe * uy + hy)
    nz = jz + fz - rate(3) * (jz - safe * uz + hz)
    xy = xy + rate(4) * (gx * uy - 0.5 * pxy - xy) + pxy
    xz = xz + rate(5) * (gx * uz - 0.5 * pxz - xz) + pxz
    yz = yz + rate(6) * (gy * uz - 0.5 * pyz - yz) + pyz
    xx = xx + rate(7) * (third + txx - xx) + 2.0 * sx
    yy = yy + rate(8) * (third + tyy - yy) + 2.0 * sy
    zz = zz + rate(9) * (third + tzz - zz) + 2.0 * sz
    ex, ey, ez = jx * (1.0 / 3.0), jy * (1.0 / 3.0), jz * (1.0 / 3.0)
    qx, qy, qz = fx * (1.0 / 3.0), fy * (1.0 / 3.0), fz * (1.0 / 3.0)
    xyy = xyy + rate(10) * (ex - xyy) + qx
    xzz = xzz + rate(11) * (ex - xzz) + qx
    yxx = yxx + rate(12) * (ey - yxx) + qy
    yzz = yzz + rate(13) * (ey - yzz) + qy
    zxx = zxx + rate(14) * (ez - zxx) + qz
    zyy = zyy + rate(15) * (ez - zyy) + qz
    base = ninth + t3
    xxyy = xxyy + rate(16) * (base - 0.5 * tzz - xxyy) + (s3 - sz)
    xxzz = xxzz + rate(17) * (base - 0.5 * tyy - xxzz) + (s3 - sy)
    yyzz = yyzz + rate(18) * (base - 0.5 * txx - yyzz) + (s3 - sx)
    out = [None] * N
    for first, even, cross, odd1, odd2 in (
        (7, xxyy, xy, xyy, yxx),
        (11, xxzz, xz, xzz, zxx),
        (15, yyzz, yz, yzz, zyy),
    ):
        even, cross, odd1, odd2 = 0.25 * even, 0.25 * cross, 0.25 * odd1, 0.25 * odd2
        plus, minus = even + cross, even - cross
        both, diff = odd1 + odd2, odd1 - odd2
        out[first], out[first + 1] = plus + both, plus - both
        out[first + 2], out[first + 3] = minus + diff, minus - diff
    pairs = []
    for first, even, odd in (
        (1, xx - (xxyy + xxzz), nx - (xyy + xzz)),
        (3, yy - (xxyy + yyzz), ny - (yxx + yzz)),
        (5, zz - (xxzz + yyzz), nz - (zxx + zyy)),
    ):
        half_even, half_odd = 0.5 * even, 0.5 * odd
        out[first], out[first + 1] = half_even + half_odd, half_even - half_odd
        pairs.append(even)
    out[0] = rho - (pairs[0] + pairs[1] + pairs[2]) - (xxyy + xxzz + yyzz)
    return out, (ux, uy, uz)


def corner_pops(side):
    return SHIFT.index((side, 1, 0)), SHIFT.index((side, -1, 0))


def in_swap_order(pairs, right, left):
    if not pairs:
        return right, left
    odd = lax.axis_index("gy") % 2 == 1
    return jnp.where(odd, left, right), jnp.where(odd, right, left)


def sort_received(pairs, a_ref, b_ref, xl_ref, xr_ref):
    if pairs:
        xr_ref[...], xl_ref[...] = in_swap_order(pairs, a_ref[...], b_ref[...])
    else:
        xl_ref[...], xr_ref[...] = a_ref[...], b_ref[...]


def wall_of(wet, wall_ref):
    wall = jnp.zeros(wet.shape, jnp.float32)
    for c in range(wall_ref.shape[0]):
        wall = jnp.where(wet == c, wall_ref[c], wall)
    return wall


def face_kernel(pairs, f_hbm, mask_hbm, wet_hbm, wall_hbm, a_ref, b_ref, rows_ref, *scratch):
    layer_in, row_in, mask_in, wet_in, wall_in, layer_sems, row_sems, sems = scratch
    layers, rows = row_in.shape[2], layer_in.shape[2]
    small = [
        pltpu.make_async_copy(source, target, sems.at[i])
        for i, (source, target) in enumerate(
            ((wall_hbm, wall_in), (mask_hbm, mask_in), (wet_hbm, wet_in))
        )
    ]
    large = []
    for s, layer in enumerate((0, layers - 1)):
        for row in range(rows):
            source = f_hbm.at[:, pl.ds(row * layers + layer, 1)]
            target = layer_in.at[s, :, pl.ds(row, 1)]
            large.append(pltpu.make_async_copy(source, target, layer_sems.at[s, row]))
    for s, row in enumerate((0, rows - 1)):
        source = f_hbm.at[:, pl.ds(row * layers, layers)]
        large.append(pltpu.make_async_copy(source, row_in.at[s], row_sems.at[s]))
    for copy in small + large:
        copy.start()
    for copy in small + large:
        copy.wait()
    faces = []
    for s, layer in enumerate((0, layers - 1)):
        at = pl.ds(layer, rows, stride=layers)
        pore = mask_in[at] == 1
        density = total([layer_in[s, k] for k in range(N)])
        pot = potential_of(density, pore, wall_of(wet_in[at], wall_in))
        faces.append((pot, jnp.where(pore, 1.0, 0.0)))
    for i in range(2):
        at = slice(i * rows, (i + 1) * rows)
        a_ref[at], b_ref[at] = in_swap_order(pairs, faces[1][i], faces[0][i])
    for s, row in enumerate((0, rows - 1)):
        at = slice(row * layers, (row + 1) * layers)
        pore = mask_in[at] == 1
        density = total([row_in[s, k] for k in range(N)])
        rows_ref[s, :layers] = potential_of(density, pore, wall_of(wet_in[at], wall_in))
        rows_ref[s, layers:] = jnp.where(pore, 1.0, 0.0)


def turn_kernel(raw_ref, mask_in, wet_in, wall_ref, rate_ref, f_ref, rates_ref, flat_ref, mask_ref, pot_ref):
    layers, rows = f_ref.shape[1], f_ref.shape[2]
    for k in range(N):
        rates_ref[k] = jnp.full(rates_ref.shape[1:], rate_ref[k], jnp.float32)
    for i in range(0, layers * rows, TILE):
        at = slice(i, i + TILE)
        pore = mask_in[at] == 1
        density = total([raw_ref[k, at] for k in range(N)])
        flat_ref[0, at] = jnp.where(pore, 1.0, 0.0)
        flat_ref[1, at] = potential_of(density, pore, wall_of(wet_in[at], wall_ref))
    for i in range(layers):
        mask_ref[i] = flat_ref[0, pl.ds(i, rows, stride=layers)]
        pot_ref[i] = flat_ref[1, pl.ds(i, rows, stride=layers)]
    for k in range(N):
        for i in range(layers):
            f_ref[k, i] = raw_ref[k, pl.ds(i, rows, stride=layers)]


def start_pack_kernel(pairs, rows_ref, a_ref, b_ref, up_ref, down_ref, from_left, from_right):
    size_x = rows_ref.shape[1] // 2
    size_y = a_ref.shape[0] // 2
    sort_received(pairs, a_ref, b_ref, from_left, from_right)
    for s, ref, y in ((1, up_ref, size_y - 1), (0, down_ref, 0)):
        ref[: 2 * size_x] = rows_ref[s]
        ref[2 * size_x :] = jnp.zeros((TILE, ref.shape[1]), jnp.float32)
        for i, side in enumerate((from_left, from_right)):
            row = 2 * size_x + i
            ref[row : row + 1] = side[y : y + 1]
            ref[row + 2 : row + 3] = side[size_y + y : size_y + y + 1]


def bits_kernel(mask_ref, x0l, x0r, bits_ref, pad_ref):
    size_x, size_y, size_z = mask_ref.shape
    nothing = jnp.zeros((TILE, size_z), jnp.float32)
    for x in range(size_x + 2):
        pad_ref[x, :TILE] = nothing
        pad_ref[x, TILE + size_y :] = nothing
    for x in range(size_x):
        pad_ref[1 + x, TILE : TILE + size_y] = mask_ref[x]
    for x, side in ((0, x0l), (1 + size_x, x0r)):
        pad_ref[x, TILE : TILE + size_y] = side[size_y:]
    for x in range(size_x):
        for y in range(0, size_y, TILE):
            bits = jnp.zeros((TILE, size_z), jnp.int32)
            for k in range(N):
                ex, ey, ez = SHIFT[k]
                row = TILE + y - ey
                source = roll_z(pad_ref[1 + x - ex, row : row + TILE], ez)
                bits = bits | jnp.where(source > 0.5, 1 << k, 0)
            bits_ref[x, y : y + TILE] = bits


def more_bits_kernel(bits_in, y0d, y0u, bits_ref, pad_ref):
    size_x, size_y, size_z = bits_ref.shape
    row_of = lax.broadcasted_iota(jnp.int32, (TILE, size_z), 0)
    found = []
    for i, (side, ks) in enumerate(((y0d, UP), (y0u, DOWN))):
        pad_ref[i, TILE : TILE + size_x] = side[size_x : 2 * size_x]
        for row, x in ((TILE - 1, 2 * size_x + 2), (TILE + size_x, 2 * size_x + 3)):
            pad_ref[i, row : row + 1] = side[x : x + 1]
        bits = jnp.zeros((size_x, size_z), jnp.int32)
        for k in ks:
            ex, _, ez = SHIFT[k]
            source = roll_z(pad_ref[i, TILE - ex : TILE - ex + size_x], ez)
            bits = bits | jnp.where(source > 0.5, 1 << k, 0)
        found.append(bits)
    for x in range(size_x):
        for y in range(0, size_y, TILE):
            bits = bits_in[x, y : y + TILE]
            for at, more in ((0, found[0]), (size_y - 1, found[1])):
                if y <= at < y + TILE:
                    bits = bits | jnp.where(row_of == at - y, more[x : x + 1], 0)
            bits_ref[x, y : y + TILE] = bits


class Layers:
    def __init__(self, edge_ref, middle_ref, size_x, edge):
        self.where = {}
        middle = [x for x in range(size_x) if x not in edge]
        for ref, xs in ((edge_ref, edge), (middle_ref, middle)):
            for i, x in enumerate(xs):
                self.where[x] = (ref, i)

    def load(self, x, y, k=None):
        ref, i = self.where[x]
        return ref[i, y : y + TILE] if k is None else ref[k, i, y : y + TILE]

    def row(self, x, y, k=None):
        ref, i = self.where[x]
        return ref[i, y : y + 1] if k is None else ref[k, i, y : y + 1]

    def store(self, x, y, value, k=None):
        ref, i = self.where[x]
        if k is None:
            ref[i, y : y + TILE] = value
        else:
            ref[k, i, y : y + TILE] = value


def two_layers(size_x):
    return [0, 1, size_x - 2, size_x - 1]


def one_layer(size_x):
    return [0, size_x - 1]


def fluid_at(bits_ref, x, y):
    return (bits_ref[x, y : y + TILE] & 1) != 0


def clear_outside(post, layers, size_y):
    nothing = jnp.zeros((TILE, post.shape[-1]), jnp.float32)
    for i in range(layers):
        for k in UP:
            post[k, i, :TILE] = nothing
        for k in DOWN:
            post[k, i, TILE + size_y :] = nothing


def collide_layers(xs, rates, f, bits_ref, pot, sides, post, speed):
    size_x, size_y, size_z = bits_ref.shape
    row_of = lax.broadcasted_iota(jnp.int32, (TILE, size_z), 0)
    for x in xs:
        for y in range(0, size_y, TILE):
            near = {
                (i, j): pot[1 + x + i, TILE + y + j : 2 * TILE + y + j]
                for i in (-1, 0, 1)
                for j in (-1, 0, 1)
            }
            scale = near[0, 0] * (STRENGTH / 36.0)
            dx = near[1, 0] - near[-1, 0]
            dy = near[0, 1] - near[0, -1]
            pp, pm, mp, mm = near[1, 1], near[1, -1], near[-1, 1], near[-1, -1]
            both = near[1, 0] + near[-1, 0] + near[0, 1] + near[0, -1] + 2.0 * near[0, 0]
            diag1, diag2 = pp - mm, pm - mp
            force = (
                scale * (2.0 * dy + (diag1 - diag2) + (roll_z(dy, 1) + roll_z(dy, -1))),
                scale * (2.0 * dx + (diag1 + diag2) + (roll_z(dx, 1) + roll_z(dx, -1))),
                scale * (roll_z(both, -1) - roll_z(both, 1)),
            )
            now = [f(k, x, y) for k in range(N)]
            if sides is not None:
                xl, xr, yd, yu = sides
                for at, side, ks in ((0, xl, RIGHT), (size_x - 1, xr, LEFT)):
                    if x == at:
                        for j, k in enumerate(ks):
                            now[k] = now[k] + side[j * size_y + y : j * size_y + y + TILE]
                for at, side, ks in ((0, yd, UP), (size_y - 1, yu, DOWN)):
                    if y <= at < y + TILE:
                        for j, k in enumerate(ks):
                            entering = side[j * size_x + x : j * size_x + x + 1]
                            now[k] = now[k] + jnp.where(row_of == at - y, entering, 0.0)
            fluid = fluid_at(bits_ref, x, y)
            after, at_speed = collide(now, fluid, force, lambda r: rates[r])
            for k in range(N):
                post.store(x, TILE + y, jnp.where(fluid, after[k], 0.0), k)
            if speed is not None:
                for c in range(3):
                    speed.store(x, y, jnp.where(fluid, at_speed[c], 0.0), c)


def stream_layers(xs, bits_ref, post, f, rho):
    size_x, size_y, _ = bits_ref.shape
    for x in xs:
        for y in range(0, size_y, TILE):
            bits = bits_ref[x, y : y + TILE]
            arrived = []
            for k in range(N):
                ex, ey, ez = SHIFT[k]
                value = post.load(x, TILE + y, OPPOSITE[k])
                if k > 0:
                    come = 0.0
                    if 0 <= x - ex < size_x:
                        come = roll_z(post.load(x - ex, TILE + y - ey, k), ez)
                    value = jnp.where((bits & (1 << k)) != 0, come, value)
                f.store(x, y, value, k)
                arrived.append(value)
            if rho is not None:
                rho.store(x, y, total(arrived))


def edge_kernel(first, last, pairs, *refs):
    refs = list(refs)
    take = lambda count: [refs.pop(0) for _ in range(count)]
    rates, bits_ref, pot0_ref, x0l, x0r, y0d, y0u = take(7)
    if first:
        f_ref = take(1)[0]
    else:
        f_edge, f_middle, rho_edge, rho_middle, xl, xr, yd, yu = take(8)
        own_right, own_left, own_up, own_down = take(4)
    pot, post_out, f_out, right_ref, left_ref, a_ref, b_ref, rest = take(8)
    size_x, size_y, size_z = bits_ref.shape
    edge2, edge1 = two_layers(size_x), one_layer(size_x)
    sides = None
    if first:
        f = lambda k, x, y: f_ref[k, x, y : y + TILE]
    else:
        sides = (xl, xr, yd, yu)
        held = Layers(f_edge, f_middle, size_x, edge1)
        density_of = Layers(rho_edge, rho_middle, size_x, edge1)
        f = lambda k, x, y: held.load(x, y, k)
    clear_outside(post_out, len(edge2), size_y)

    if first:
        for x in range(size_x):
            pot[1 + x, TILE : TILE + size_y] = pot0_ref[x]
        for x, side in ((0, x0l), (1 + size_x, x0r)):
            pot[x, TILE : TILE + size_y] = side[:size_y]
        for y, side in ((TILE - 1, y0d), (TILE + size_y, y0u)):
            for x in range(size_x):
                pot[1 + x, y : y + 1] = side[x : x + 1]
            for x, row in ((0, 2 * size_x), (1 + size_x, 2 * size_x + 1)):
                pot[x, y : y + 1] = side[row : row + 1]
    else:
        end = 6 * size_x
        row_of = lax.broadcasted_iota(jnp.int32, (TILE, size_z), 0)
        entering = {
            at: total([side[j * size_x : (j + 1) * size_x] for j in range(5)])
            for at, side in ((0, yd), (size_y - 1, yu))
        }
        for x in range(size_x):
            for y in range(0, size_y, TILE):
                density = density_of.load(x, y)
                for at, side in ((0, xl), (size_x - 1, xr)):
                    if x == at:
                        density = density + total(
                            [side[j * size_y + y : j * size_y + y + TILE] for j in range(5)]
                        )
                for at, rows in entering.items():
                    if y <= at < y + TILE:
                        density = density + jnp.where(row_of == at - y, rows[x : x + 1], 0.0)
                pot[1 + x, TILE + y : 2 * TILE + y] = potential_of(
                    density, fluid_at(bits_ref, x, y), pot0_ref[x, y : y + TILE]
                )
        for x, side, own, side0, g in (
            (0, xl, own_left, x0l, G_L),
            (1 + size_x, xr, own_right, x0r, G_R),
        ):
            for y in range(0, size_y, TILE):
                density = side[5 * size_y + y : 5 * size_y + y + TILE] + total(
                    [own[j * size_y + y : j * size_y + y + TILE] for j in range(5)]
                )
                for at, row in ((0, yd), (size_y - 1, yu)):
                    if y <= at < y + TILE:
                        more = row[end + g : end + g + 1]
                        density = density + jnp.where(row_of == at - y, more, 0.0)
                pot[x, TILE + y : 2 * TILE + y] = potential_of(
                    density,
                    side0[size_y + y : size_y + y + TILE] > 0.5,
                    side0[y : y + TILE],
                )
        for y, side, own, side0 in (
            (TILE - 1, yd, own_down, y0d),
            (TILE + size_y, yu, own_up, y0u),
        ):
            density = side[5 * size_x : 6 * size_x] + total(
                [own[j * size_x : (j + 1) * size_x] for j in range(5)]
            )
            value = potential_of(density, side0[size_x : 2 * size_x] > 0.5, side0[:size_x])
            for x in range(size_x):
                pot[1 + x, y : y + 1] = value[x : x + 1]
            for x, rc, g, i in ((0, RC_L, G_L, 0), (1 + size_x, RC_R, G_R, 1)):
                density = side[end + rc : end + rc + 1] + own[end + g : end + g + 1]
                row = 2 * size_x + i
                pot[x, y : y + 1] = potential_of(
                    density, side0[row + 2 : row + 3] > 0.5, side0[row : row + 1]
                )

    post = Layers(post_out, None, size_x, edge2)
    speed = Layers(rest, None, size_x, edge2) if last else None
    collide_layers(edge2, rates, f, bits_ref, pot, sides, post, speed)
    rho = None if last else Layers(rest, None, size_x, edge1)
    stream_layers(edge1, bits_ref, post, Layers(f_out, None, size_x, edge1), rho)

    at = (5 if last else 6) * size_y
    for i, (ref, x, ks, dirs) in enumerate(
        ((left_ref, 0, LEFT, corner_pops(-1)), (right_ref, size_x - 1, RIGHT, corner_pops(1)))
    ):
        for j, k in enumerate(ks):
            _, ey, ez = SHIFT[k]
            for y in range(0, size_y, TILE):
                row = j * size_y + y
                ref[row : row + TILE] = roll_z(post.load(x, TILE + y - ey, k), ez)
        ref[at : at + TILE] = jnp.zeros((TILE, size_z), jnp.float32)
        ref[at + C_UP : at + C_UP + 1] = post.row(x, TILE + size_y - 1, dirs[0])
        ref[at + C_DN : at + C_DN + 1] = post.row(x, TILE, dirs[1])
        if not last:
            ref[5 * size_y : 6 * size_y] = rest[i]
            for h, y, leave in ((H_UP, size_y - 1, UP), (H_DN, 0, DOWN)):
                ref[at + h : at + h + 1] = total(
                    [
                        roll_z(post.row(x - SHIFT[k][0], TILE + y, k), SHIFT[k][2])
                        for k in leave
                        if 0 <= x - SHIFT[k][0] < size_x
                    ]
                )
    a_ref[...], b_ref[...] = in_swap_order(pairs, right_ref[...], left_ref[...])


def middle_kernel(first, last, *refs):
    refs = list(refs)
    take = lambda count: [refs.pop(0) for _ in range(count)]
    rates, bits_ref, pot, post_edge, edge_rest = take(5)
    if first:
        f_ref = take(1)[0]
    else:
        f_edge, f_middle, yd, yu = take(4)
    f_out, up_ref, down_ref, rest = take(4)
    post_middle = take(1)[0]
    size_x, size_y, size_z = bits_ref.shape
    edge2, edge1 = two_layers(size_x), one_layer(size_x)
    sides = None
    if first:
        f = lambda k, x, y: f_ref[k, x, y : y + TILE]
    else:
        sides = (None, None, yd, yu)
        held = Layers(f_edge, f_middle, size_x, edge1)
        f = lambda k, x, y: held.load(x, y, k)
    clear_outside(post_middle, size_x - len(edge2), size_y)
    post = Layers(post_edge, post_middle, size_x, edge2)
    speed = None
    if last:
        speed = Layers(None, None, size_x, [])
        speed.store = lambda x, y, value, c: rest.__setitem__((c, turned(x, y, size_x)), value)
        for c in range(3):
            for i, x in enumerate(edge2):
                for y in range(0, size_y, TILE):
                    rest[c, turned(x, y, size_x)] = edge_rest[c, i, y : y + TILE]
    inner = [x for x in range(size_x) if x not in edge2]
    collide_layers(inner, rates, f, bits_ref, pot, sides, post, speed)
    rho = None if last else Layers(edge_rest, rest, size_x, edge1)
    inner = [x for x in range(size_x) if x not in edge1]
    stream_layers(inner, bits_ref, post, Layers(None, f_out, size_x, edge1), rho)
    for ref, y, ks in ((up_ref, size_y - 1, UP), (down_ref, 0, DOWN)):
        for j, k in enumerate(ks):
            ex, _, ez = SHIFT[k]
            for x in range(size_x):
                row = j * size_x + x
                if 0 <= x - ex < size_x:
                    ref[row : row + 1] = post.row(x - ex, TILE + y, k)
                else:
                    ref[row : row + 1] = jnp.zeros((1, size_z), jnp.float32)
            if ez != 0:
                rows = slice(j * size_x, (j + 1) * size_x)
                ref[rows] = roll_z(ref[rows], ez)
        if not last:
            for x in range(size_x):
                ref[5 * size_x + x : 5 * size_x + x + 1] = rho.row(x, y)


def pack_kernel(last, pairs, size_x, size_y, *refs):
    up_in, down_in, a_ref, b_ref, own_right, own_left, up_ref, down_ref, xl, xr = refs
    sort_received(pairs, a_ref, b_ref, xl, xr)
    parts = 5 if last else 6
    at = parts * size_y
    for ref, source, y, ks, c, h in (
        (up_ref, up_in, size_y - 1, UP, C_UP, H_UP),
        (down_ref, down_in, 0, DOWN, C_DN, H_DN),
    ):
        ref[...] = jnp.zeros(ref.shape, jnp.float32)
        ref[: parts * size_x] = source[: parts * size_x]
        for side, own, x, ex, rc, g in (
            (xl, own_left, 0, 1, RC_L, G_L),
            (xr, own_right, size_x - 1, -1, RC_R, G_R),
        ):
            j = [i for i, k in enumerate(ks) if SHIFT[k][0] == ex][0]
            row = j * size_x + x
            ref[row : row + 1] = side[at + c : at + c + 1]
            if not last:
                row = 5 * size_x + x
                ref[row : row + 1] = source[row : row + 1] + total(
                    [side[i * size_y + y : i * size_y + y + 1] for i in range(5)]
                )
                row = 6 * size_x
                ref[row + rc : row + rc + 1] = side[5 * size_y + y : 5 * size_y + y + 1] + total(
                    [own[i * size_y + y : i * size_y + y + 1] for i in range(5)]
                )
                ref[row + g : row + g + 1] = (
                    side[at + h : at + h + 1] + own[at + c : at + c + 1]
                )


def turned(layer, row, layers):
    return pl.ds(layer + row * layers, TILE, stride=layers)


def write_kernel(f_edge, f_middle, bits_ref, xl, xr, speed_ref, out_hbm, flat_ref, speed_hbm, sems, speed_sem):
    size_x, size_y, _ = bits_ref.shape
    held = Layers(f_edge, f_middle, size_x, one_layer(size_x))
    copies = [pltpu.make_async_copy(speed_ref, speed_hbm, speed_sem)]
    copies[0].start()
    for k in range(N):
        for x in range(size_x):
            for y in range(0, size_y, TILE):
                value = held.load(x, y, k)
                for at, side, ks in ((0, xl, RIGHT), (size_x - 1, xr, LEFT)):
                    if x == at and k in ks:
                        row = ks.index(k) * size_y + y
                        value = value + side[row : row + TILE]
                value = jnp.where(fluid_at(bits_ref, x, y), value, 0.0)
                flat_ref[k, turned(x, y, size_x)] = value
        copies.append(pltpu.make_async_copy(flat_ref.at[k], out_hbm.at[k], sems.at[k]))
        copies[-1].start()
    for copy in copies:
        copy.wait()


def end_kernel(out_in, flat_ref, mask_ref, yd, yu, out_hbm, planes, sems):
    del out_in
    layers = planes.shape[1]
    last = flat_ref.shape[1] - layers
    copies = []
    for at, side, ks in ((0, yd, UP), (last, yu, DOWN)):
        for j, k in enumerate(ks):
            i = len(copies)
            entering = side[j * layers : (j + 1) * layers]
            fluid = mask_ref[0, at : at + layers] > 0.5
            planes[i] = jnp.where(fluid, flat_ref[k, at : at + layers] + entering, 0.0)
            target = out_hbm.at[k, pl.ds(at, layers)]
            copies.append(pltpu.make_async_copy(planes.at[i], target, sems.at[i]))
            copies[-1].start()
    for copy in copies:
        copy.wait()


VMEM = pl.BlockSpec(memory_space=pltpu.VMEM)
SMEM = pl.BlockSpec(memory_space=pltpu.SMEM)
HBM = pl.BlockSpec(memory_space=pltpu.HBM)


def call(kernel, outs, args, special=None, special_out=None, scratch=(), cost=None, **kwargs):
    special, special_out = special or {}, special_out or {}
    return pl.pallas_call(
        kernel,
        out_shape=[jax.ShapeDtypeStruct(shape, dtype) for shape, dtype in outs],
        in_specs=[special.get(i, VMEM) for i in range(len(args))],
        out_specs=[special_out.get(i, VMEM) for i in range(len(outs))],
        scratch_shapes=[
            pltpu.VMEM(item, jnp.float32) if isinstance(item, tuple) else item for item in scratch
        ],
        compiler_params=pltpu.CompilerParams(vmem_limit_bytes=16 * 2**20),
        cost_estimate=cost,
        **kwargs,
    )(*args)


def shift(forward, backward, axis):
    count = lax.axis_size(axis)
    ahead = [(i, (i + 1) % count) for i in range(count)]
    return (
        lax.ppermute(forward, axis, ahead),
        lax.ppermute(backward, axis, [(b, a) for a, b in ahead]),
    )


def swap(a, b, axis):
    count = lax.axis_size(axis)
    partners = [
        [(i, (i + (1 if i % 2 == parity else -1)) % count) for i in range(count)]
        for parity in range(2)
    ]
    b = lax.ppermute(b, axis, partners[1])
    return lax.ppermute(a, axis, partners[0]), b


def per_device(populations, fluid_mask, wet_class, wall_potential, relax_rates):
    rows_x, rows_y, size_z = fluid_mask.shape
    pairs = lax.axis_size("gy") % 2 == 0
    exchange = swap if pairs else shift
    size_x, size_y = rows_y, rows_x
    cells = size_x * size_y
    f32, i32 = jnp.float32, jnp.int32
    whole = ((size_x, size_y, size_z), f32)
    rows = lambda count: ((count, size_z), f32)
    fields = lambda count: ((N, count, size_y, size_z), f32)
    flat = lambda count: ((count, cells, size_z), f32)
    padded = (size_x + 2, size_y + PAD, size_z)
    operations = 400 * cells * size_z
    cost = pl.CostEstimate(flops=operations, bytes_accessed=4 * operations // 20, transcendentals=0)

    operands = (
        populations.reshape(N, cells, size_z),
        fluid_mask.reshape(cells, size_z),
        wet_class.reshape(cells, size_z),
        wall_potential,
    )
    start_rows = rows(2 * size_x + TILE)
    a, b, row_faces = call(
        functools.partial(face_kernel, pairs),
        [rows(2 * size_y), rows(2 * size_y), ((2, 2 * size_x, size_z), f32)],
        [pltpu.with_memory_space_constraint(item, pltpu.HBM) for item in operands],
        special={i: HBM for i in range(4)},
        scratch=[
            (2, N, size_y, size_z),
            (2, N, size_x, size_z),
            pltpu.VMEM((cells, size_z), i32),
            pltpu.VMEM((cells, size_z), i32),
            pltpu.SMEM(wall_potential.shape, f32),
            pltpu.SemaphoreType.DMA((2, size_y)),
            pltpu.SemaphoreType.DMA((2,)),
            pltpu.SemaphoreType.DMA((3,)),
        ],
    )
    a, b = exchange(a, b, "gy")
    up, down, x0l, x0r = call(
        functools.partial(start_pack_kernel, pairs),
        [start_rows, start_rows, rows(2 * size_y), rows(2 * size_y)],
        (row_faces, a, b),
    )
    f, rates, flat_mask, mask, pot0 = call(
        turn_kernel,
        [fields(size_x), ((N, TILE, size_z), f32), flat(2), whole, whole],
        (*operands, relax_rates),
        special={3: SMEM, 4: SMEM},
        cost=cost,
    )
    y0d, y0u = shift(up, down, "gx")
    whole_bits = [((size_x, size_y, size_z), i32)]
    (bits,) = call(bits_kernel, whole_bits, (mask, x0l, x0r), scratch=[padded], cost=cost)
    (bits,) = call(
        more_bits_kernel, whole_bits, (bits, y0d, y0u), scratch=[(2, size_x + PAD, size_z)]
    )
    edge2, edge1 = len(two_layers(size_x)), len(one_layer(size_x))
    held, sent = (f,), ()
    for step in range(STEPS):
        first, last = step == 0, step == STEPS - 1
        parts = 5 if last else 6
        x_rows, y_rows = rows(parts * size_y + TILE), rows(parts * size_x + (0 if last else TILE))
        pot, post, f_edge, right, left, a, b, rest = call(
            functools.partial(edge_kernel, first, last, pairs),
            [
                (padded, f32),
                ((N, edge2, size_y + PAD, size_z), f32),
                fields(edge1),
                x_rows,
                x_rows,
                x_rows,
                x_rows,
                ((3, edge2, size_y, size_z) if last else (edge1, size_y, size_z), f32),
            ],
            (rates, bits, pot0, x0l, x0r, y0d, y0u, *held, *sent),
            cost=cost,
        )
        a, b = exchange(a, b, "gy")
        f_middle, up, down, more = call(
            functools.partial(middle_kernel, first, last),
            [
                fields(size_x - edge1),
                y_rows,
                y_rows,
                flat(3) if last else ((size_x - edge1, size_y, size_z), f32),
            ],
            (rates, bits, pot, post, rest, *held[:2], *sent[2:4]),
            scratch=[(N, size_x - edge2, size_y + PAD, size_z)],
            cost=cost,
        )
        up, down, xl, xr = call(
            functools.partial(pack_kernel, last, pairs, size_x, size_y),
            [y_rows, y_rows, x_rows, x_rows],
            (up, down, a, b, right, left),
        )
        yd, yu = shift(up, down, "gx")
        held = (f_edge, f_middle, rest, more)
        sent = (xl, xr, yd, yu, right, left, up, down)
    out, flat_f, speed = call(
        write_kernel,
        [flat(N), flat(N), flat(3)],
        (f_edge, f_middle, bits, xl, xr, more),
        special_out={0: HBM, 2: HBM},
        scratch=[pltpu.SemaphoreType.DMA((N,)), pltpu.SemaphoreType.DMA(())],
        cost=cost,
    )
    (out,) = call(
        end_kernel,
        [flat(N)],
        (out, flat_f, flat_mask, yd, yu),
        special={0: HBM},
        special_out={0: HBM},
        scratch=[(10, size_x, size_z), pltpu.SemaphoreType.DMA((10,))],
        input_output_aliases={0: 0},
    )
    shape = (rows_x, rows_y, size_z)
    return out.reshape(N, *shape), speed.reshape(3, *shape)


def solution(mesh):
    return jax.shard_map(
        per_device,
        mesh=mesh,
        in_specs=(
            P(None, ("groups", "gx"), "gy", None),
            P(("groups", "gx"), "gy", None),
            P(("groups", "gx"), "gy", None),
            P("groups"),
            P(),
        ),
        out_specs=(P(None, ("groups", "gx"), "gy", None), P(None, ("groups", "gx"), "gy", None)),
        check_vma=False,
    )
```

```python
import functools

import jax
import jax.numpy as jnp
from jax import lax
from jax.experimental import pallas as pl
from jax.experimental.pallas import tpu as pltpu
from jax.sharding import PartitionSpec as P

STEPS = 4
STRENGTH = 2.5
VELOCITY = (
    (0, 0, 0),
    (1, 0, 0),
    (-1, 0, 0),
    (0, 1, 0),
    (0, -1, 0),
    (0, 0, 1),
    (0, 0, -1),
    (1, 1, 0),
    (-1, -1, 0),
    (1, -1, 0),
    (-1, 1, 0),
    (1, 0, 1),
    (-1, 0, -1),
    (1, 0, -1),
    (-1, 0, 1),
    (0, 1, 1),
    (0, -1, -1),
    (0, 1, -1),
    (0, -1, 1),
)
N = len(VELOCITY)
OPPOSITE = [0] + [k + 1 if k % 2 == 1 else k - 1 for k in range(1, N)]
SHIFT = [(y, x, z) for x, y, z in VELOCITY]
RIGHT = [k for k in range(N) if SHIFT[k][0] == 1]
LEFT = [k for k in range(N) if SHIFT[k][0] == -1]
UP = [k for k in range(N) if SHIFT[k][1] == 1]
DOWN = [k for k in range(N) if SHIFT[k][1] == -1]
TILE = 8
PAD = 2 * TILE

C_UP, C_DN, H_UP, H_DN = 0, 1, 2, 3
RC_L, RC_R, G_L, G_R = 0, 1, 2, 3


def roll_z(value, step):
    if step == 0:
        return value
    return pltpu.roll(value, step % value.shape[-1], value.ndim - 1)


def total(values):
    values = list(values)
    while len(values) > 1:
        values = [
            values[i] + values[i + 1] if i + 1 < len(values) else values[i]
            for i in range(0, len(values), 2)
        ]
    return values[0]


def potential_of(density, fluid, solid_value):
    return jnp.where(fluid, 1.0 - jnp.exp(-density), solid_value)


def collide(f, fluid, force, rate):
    fx, fy, fz = force
    s = {k: f[k] + f[k + 1] for k in range(1, N, 2)}
    d = {k: f[k] - f[k + 1] for k in range(1, N, 2)}
    xxyy, xxzz, yyzz = s[7] + s[9], s[11] + s[13], s[15] + s[17]
    xy, xz, yz = s[7] - s[9], s[11] - s[13], s[15] - s[17]
    xyy, yxx = d[7] + d[9], d[7] - d[9]
    xzz, zxx = d[11] + d[13], d[11] - d[13]
    yzz, zyy = d[15] + d[17], d[15] - d[17]
    jx, jy, jz = d[1] + (xyy + xzz), d[3] + (yxx + yzz), d[5] + (zxx + zyy)
    xx, yy, zz = s[1] + (xxyy + xxzz), s[3] + (xxyy + yyzz), s[5] + (xxzz + yyzz)
    rho = (f[0] + s[1]) + (s[3] + s[5]) + (xxyy + (xxzz + yyzz))
    safe = jnp.where(fluid, rho, 1.0)
    inverse = 1.0 / safe
    hx, hy, hz = 0.5 * fx, 0.5 * fy, 0.5 * fz
    gx, gy, gz = jx + hx, jy + hy, jz + hz
    ux, uy, uz = gx * inverse, gy * inverse, gz * inverse
    third = safe * (1.0 / 3.0)
    ninth = safe * (1.0 / 9.0)
    px, py, pz = gx - fx, gy - fy, gz - fz
    txx, tyy, tzz = ux * px, uy * py, uz * pz
    sx, sy, sz = ux * fx, uy * fy, uz * fz
    pxy = ux * fy + uy * fx
    pxz = ux * fz + uz * fx
    pyz = uy * fz + uz * fy
    t3, s3 = (txx + tyy + tzz) * (1.0 / 3.0), (sx + sy + sz) * (2.0 / 3.0)
    rho = rho - rate(0) * (rho - safe)
    nx = jx + fx - rate(1) * (jx - safe * ux + hx)
    ny = jy + fy - rate(2) * (jy - safe * uy + hy)
    nz = jz + fz - rate(3) * (jz - safe * uz + hz)
    xy = xy + rate(4) * (gx * uy - 0.5 * pxy - xy) + pxy
    xz = xz + rate(5) * (gx * uz - 0.5 * pxz - xz) + pxz
    yz = yz + rate(6) * (gy * uz - 0.5 * pyz - yz) + pyz
    xx = xx + rate(7) * (third + txx - xx) + 2.0 * sx
    yy = yy + rate(8) * (third + tyy - yy) + 2.0 * sy
    zz = zz + rate(9) * (third + tzz - zz) + 2.0 * sz
    ex, ey, ez = jx * (1.0 / 3.0), jy * (1.0 / 3.0), jz * (1.0 / 3.0)
    qx, qy, qz = fx * (1.0 / 3.0), fy * (1.0 / 3.0), fz * (1.0 / 3.0)
    xyy = xyy + rate(10) * (ex - xyy) + qx
    xzz = xzz + rate(11) * (ex - xzz) + qx
    yxx = yxx + rate(12) * (ey - yxx) + qy
    yzz = yzz + rate(13) * (ey - yzz) + qy
    zxx = zxx + rate(14) * (ez - zxx) + qz
    zyy = zyy + rate(15) * (ez - zyy) + qz
    base = ninth + t3
    xxyy = xxyy + rate(16) * (base - 0.5 * tzz - xxyy) + (s3 - sz)
    xxzz = xxzz + rate(17) * (base - 0.5 * tyy - xxzz) + (s3 - sy)
    yyzz = yyzz + rate(18) * (base - 0.5 * txx - yyzz) + (s3 - sx)
    out = [None] * N
    for first, even, cross, odd1, odd2 in (
        (7, xxyy, xy, xyy, yxx),
        (11, xxzz, xz, xzz, zxx),
        (15, yyzz, yz, yzz, zyy),
    ):
        even, cross, odd1, odd2 = 0.25 * even, 0.25 * cross, 0.25 * odd1, 0.25 * odd2
        plus, minus = even + cross, even - cross
        both, diff = odd1 + odd2, odd1 - odd2
        out[first], out[first + 1] = plus + both, plus - both
        out[first + 2], out[first + 3] = minus + diff, minus - diff
    pairs = []
    for first, even, odd in (
        (1, xx - (xxyy + xxzz), nx - (xyy + xzz)),
        (3, yy - (xxyy + yyzz), ny - (yxx + yzz)),
        (5, zz - (xxzz + yyzz), nz - (zxx + zyy)),
    ):
        half_even, half_odd = 0.5 * even, 0.5 * odd
        out[first], out[first + 1] = half_even + half_odd, half_even - half_odd
        pairs.append(even)
    out[0] = rho - (pairs[0] + pairs[1] + pairs[2]) - (xxyy + xxzz + yyzz)
    return out, (ux, uy, uz)


def corner_pops(side):
    return SHIFT.index((side, 1, 0)), SHIFT.index((side, -1, 0))


def in_swap_order(pairs, right, left):
    if not pairs:
        return right, left
    odd = lax.axis_index("gy") % 2 == 1
    return jnp.where(odd, left, right), jnp.where(odd, right, left)


def sort_received(pairs, a_ref, b_ref, xl_ref, xr_ref):
    if pairs:
        xr_ref[...], xl_ref[...] = in_swap_order(pairs, a_ref[...], b_ref[...])
    else:
        xl_ref[...], xr_ref[...] = a_ref[...], b_ref[...]


def wall_of(wet, wall_ref):
    wall = jnp.zeros(wet.shape, jnp.float32)
    for c in range(wall_ref.shape[0]):
        wall = jnp.where(wet == c, wall_ref[c], wall)
    return wall


def face_kernel(pairs, f_hbm, mask_hbm, wet_hbm, wall_hbm, a_ref, b_ref, rows_ref, *scratch):
    layer_in, row_in, mask_in, wet_in, wall_in, layer_sems, row_sems, sems = scratch
    layers, rows = row_in.shape[2], layer_in.shape[2]
    small = [
        pltpu.make_async_copy(source, target, sems.at[i])
        for i, (source, target) in enumerate(
            ((wall_hbm, wall_in), (mask_hbm, mask_in), (wet_hbm, wet_in))
        )
    ]
    large = []
    for s, layer in enumerate((0, layers - 1)):
        for row in range(rows):
            source = f_hbm.at[:, pl.ds(row * layers + layer, 1)]
            target = layer_in.at[s, :, pl.ds(row, 1)]
            large.append(pltpu.make_async_copy(source, target, layer_sems.at[s, row]))
    for s, row in enumerate((0, rows - 1)):
        source = f_hbm.at[:, pl.ds(row * layers, layers)]
        large.append(pltpu.make_async_copy(source, row_in.at[s], row_sems.at[s]))
    for copy in small + large:
        copy.start()
    for copy in small + large:
        copy.wait()
    faces = []
    for s, layer in enumerate((0, layers - 1)):
        at = pl.ds(layer, rows, stride=layers)
        pore = mask_in[at] == 1
        density = total([layer_in[s, k] for k in range(N)])
        pot = potential_of(density, pore, wall_of(wet_in[at], wall_in))
        faces.append((pot, jnp.where(pore, 1.0, 0.0)))
    for i in range(2):
        at = slice(i * rows, (i + 1) * rows)
        a_ref[at], b_ref[at] = in_swap_order(pairs, faces[1][i], faces[0][i])
    for s, row in enumerate((0, rows - 1)):
        at = slice(row * layers, (row + 1) * layers)
        pore = mask_in[at] == 1
        density = total([row_in[s, k] for k in range(N)])
        rows_ref[s, :layers] = potential_of(density, pore, wall_of(wet_in[at], wall_in))
        rows_ref[s, layers:] = jnp.where(pore, 1.0, 0.0)


def load_kernel(f_hbm, mask_hbm, wet_hbm, after_ref, f_ref, mask_ref, wet_ref, f_sems, sems):
    del after_ref
    copies = [pltpu.make_async_copy(f_hbm.at[k], f_ref.at[k], f_sems.at[k]) for k in range(N)]
    copies.append(pltpu.make_async_copy(mask_hbm, mask_ref, sems.at[0]))
    copies.append(pltpu.make_async_copy(wet_hbm, wet_ref, sems.at[1]))
    for copy in copies:
        copy.start()
    for copy in copies:
        copy.wait()


def turn_kernel(raw_ref, mask_in, wet_in, wall_ref, rate_ref, f_ref, rates_ref, flat_ref, mask_ref, pot_ref):
    layers, rows = f_ref.shape[1], f_ref.shape[2]
    for k in range(N):
        rates_ref[k] = jnp.full(rates_ref.shape[1:], rate_ref[k], jnp.float32)
    for i in range(0, layers * rows, TILE):
        at = slice(i, i + TILE)
        pore = mask_in[at] == 1
        density = total([raw_ref[k, at] for k in range(N)])
        flat_ref[0, at] = jnp.where(pore, 1.0, 0.0)
        flat_ref[1, at] = potential_of(density, pore, wall_of(wet_in[at], wall_ref))
    for i in range(layers):
        mask_ref[i] = flat_ref[0, pl.ds(i, rows, stride=layers)]
        pot_ref[i] = flat_ref[1, pl.ds(i, rows, stride=layers)]
    for k in range(N):
        for i in range(layers):
            f_ref[k, i] = raw_ref[k, pl.ds(i, rows, stride=layers)]


def start_pack_kernel(pairs, rows_ref, a_ref, b_ref, up_ref, down_ref, from_left, from_right):
    size_x = rows_ref.shape[1] // 2
    size_y = a_ref.shape[0] // 2
    sort_received(pairs, a_ref, b_ref, from_left, from_right)
    for s, ref, y in ((1, up_ref, size_y - 1), (0, down_ref, 0)):
        ref[: 2 * size_x] = rows_ref[s]
        ref[2 * size_x :] = jnp.zeros((TILE, ref.shape[1]), jnp.float32)
        for i, side in enumerate((from_left, from_right)):
            row = 2 * size_x + i
            ref[row : row + 1] = side[y : y + 1]
            ref[row + 2 : row + 3] = side[size_y + y : size_y + y + 1]


def bits_kernel(mask_ref, x0l, x0r, bits_ref, pad_ref):
    size_x, size_y, size_z = mask_ref.shape
    nothing = jnp.zeros((TILE, size_z), jnp.float32)
    for x in range(size_x + 2):
        pad_ref[x, :TILE] = nothing
        pad_ref[x, TILE + size_y :] = nothing
    for x in range(size_x):
        pad_ref[1 + x, TILE : TILE + size_y] = mask_ref[x]
    for x, side in ((0, x0l), (1 + size_x, x0r)):
        pad_ref[x, TILE : TILE + size_y] = side[size_y:]
    for x in range(size_x):
        for y in range(0, size_y, TILE):
            bits = jnp.zeros((TILE, size_z), jnp.int32)
            for k in range(N):
                ex, ey, ez = SHIFT[k]
                row = TILE + y - ey
                source = roll_z(pad_ref[1 + x - ex, row : row + TILE], ez)
                bits = bits | jnp.where(source > 0.5, 1 << k, 0)
            bits_ref[x, y : y + TILE] = bits


def more_bits_kernel(bits_in, y0d, y0u, bits_ref, pad_ref):
    size_x, size_y, size_z = bits_ref.shape
    row_of = lax.broadcasted_iota(jnp.int32, (TILE, size_z), 0)
    found = []
    for i, (side, ks) in enumerate(((y0d, UP), (y0u, DOWN))):
        pad_ref[i, TILE : TILE + size_x] = side[size_x : 2 * size_x]
        for row, x in ((TILE - 1, 2 * size_x + 2), (TILE + size_x, 2 * size_x + 3)):
            pad_ref[i, row : row + 1] = side[x : x + 1]
        bits = jnp.zeros((size_x, size_z), jnp.int32)
        for k in ks:
            ex, _, ez = SHIFT[k]
            source = roll_z(pad_ref[i, TILE - ex : TILE - ex + size_x], ez)
            bits = bits | jnp.where(source > 0.5, 1 << k, 0)
        found.append(bits)
    for x in range(size_x):
        for y in range(0, size_y, TILE):
            bits = bits_in[x, y : y + TILE]
            for at, more in ((0, found[0]), (size_y - 1, found[1])):
                if y <= at < y + TILE:
                    bits = bits | jnp.where(row_of == at - y, more[x : x + 1], 0)
            bits_ref[x, y : y + TILE] = bits


class Layers:
    def __init__(self, edge_ref, middle_ref, size_x, edge):
        self.where = {}
        middle = [x for x in range(size_x) if x not in edge]
        for ref, xs in ((edge_ref, edge), (middle_ref, middle)):
            for i, x in enumerate(xs):
                self.where[x] = (ref, i)

    def load(self, x, y, k=None):
        ref, i = self.where[x]
        return ref[i, y : y + TILE] if k is None else ref[k, i, y : y + TILE]

    def row(self, x, y, k=None):
        ref, i = self.where[x]
        return ref[i, y : y + 1] if k is None else ref[k, i, y : y + 1]

    def store(self, x, y, value, k=None):
        ref, i = self.where[x]
        if k is None:
            ref[i, y : y + TILE] = value
        else:
            ref[k, i, y : y + TILE] = value


def two_layers(size_x):
    return [0, 1, size_x - 2, size_x - 1]


def one_layer(size_x):
    return [0, size_x - 1]


def fluid_at(bits_ref, x, y):
    return (bits_ref[x, y : y + TILE] & 1) != 0


def clear_outside(post, layers, size_y):
    nothing = jnp.zeros((TILE, post.shape[-1]), jnp.float32)
    for i in range(layers):
        for k in UP:
            post[k, i, :TILE] = nothing
        for k in DOWN:
            post[k, i, TILE + size_y :] = nothing


def collide_layers(xs, rates, f, bits_ref, pot, sides, post, speed):
    size_x, size_y, size_z = bits_ref.shape
    row_of = lax.broadcasted_iota(jnp.int32, (TILE, size_z), 0)
    for x in xs:
        for y in range(0, size_y, TILE):
            near = {
                (i, j): pot[1 + x + i, TILE + y + j : 2 * TILE + y + j]
                for i in (-1, 0, 1)
                for j in (-1, 0, 1)
            }
            scale = near[0, 0] * (STRENGTH / 36.0)
            dx = near[1, 0] - near[-1, 0]
            dy = near[0, 1] - near[0, -1]
            pp, pm, mp, mm = near[1, 1], near[1, -1], near[-1, 1], near[-1, -1]
            both = near[1, 0] + near[-1, 0] + near[0, 1] + near[0, -1] + 2.0 * near[0, 0]
            diag1, diag2 = pp - mm, pm - mp
            force = (
                scale * (2.0 * dy + (diag1 - diag2) + (roll_z(dy, 1) + roll_z(dy, -1))),
                scale * (2.0 * dx + (diag1 + diag2) + (roll_z(dx, 1) + roll_z(dx, -1))),
                scale * (roll_z(both, -1) - roll_z(both, 1)),
            )
            now = [f(k, x, y) for k in range(N)]
            if sides is not None:
                xl, xr, yd, yu = sides
                for at, side, ks in ((0, xl, RIGHT), (size_x - 1, xr, LEFT)):
                    if x == at:
                        for j, k in enumerate(ks):
                            now[k] = now[k] + side[j * size_y + y : j * size_y + y + TILE]
                for at, side, ks in ((0, yd, UP), (size_y - 1, yu, DOWN)):
                    if y <= at < y + TILE:
                        for j, k in enumerate(ks):
                            entering = side[j * size_x + x : j * size_x + x + 1]
                            now[k] = now[k] + jnp.where(row_of == at - y, entering, 0.0)
            fluid = fluid_at(bits_ref, x, y)
            after, at_speed = collide(now, fluid, force, lambda r: rates[r])
            for k in range(N):
                post.store(x, TILE + y, jnp.where(fluid, after[k], 0.0), k)
            if speed is not None:
                for c in range(3):
                    speed.store(x, y, jnp.where(fluid, at_speed[c], 0.0), c)


def stream_layers(xs, bits_ref, post, f, rho):
    size_x, size_y, _ = bits_ref.shape
    for x in xs:
        for y in range(0, size_y, TILE):
            bits = bits_ref[x, y : y + TILE]
            arrived = []
            for k in range(N):
                ex, ey, ez = SHIFT[k]
                value = post.load(x, TILE + y, OPPOSITE[k])
                if k > 0:
                    come = 0.0
                    if 0 <= x - ex < size_x:
                        come = roll_z(post.load(x - ex, TILE + y - ey, k), ez)
                    value = jnp.where((bits & (1 << k)) != 0, come, value)
                f.store(x, y, value, k)
                arrived.append(value)
            if rho is not None:
                rho.store(x, y, total(arrived))


def edge_kernel(first, last, pairs, *refs):
    refs = list(refs)
    take = lambda count: [refs.pop(0) for _ in range(count)]
    rates, bits_ref, pot0_ref, x0l, x0r, y0d, y0u = take(7)
    if first:
        f_ref = take(1)[0]
    else:
        f_edge, f_middle, rho_edge, rho_middle, xl, xr, yd, yu = take(8)
        own_right, own_left, own_up, own_down = take(4)
    pot, post_out, f_out, right_ref, left_ref, a_ref, b_ref, rest = take(8)
    size_x, size_y, size_z = bits_ref.shape
    edge2, edge1 = two_layers(size_x), one_layer(size_x)
    sides = None
    if first:
        f = lambda k, x, y: f_ref[k, x, y : y + TILE]
    else:
        sides = (xl, xr, yd, yu)
        held = Layers(f_edge, f_middle, size_x, edge1)
        density_of = Layers(rho_edge, rho_middle, size_x, edge1)
        f = lambda k, x, y: held.load(x, y, k)
    clear_outside(post_out, len(edge2), size_y)

    if first:
        for x in range(size_x):
            pot[1 + x, TILE : TILE + size_y] = pot0_ref[x]
        for x, side in ((0, x0l), (1 + size_x, x0r)):
            pot[x, TILE : TILE + size_y] = side[:size_y]
        for y, side in ((TILE - 1, y0d), (TILE + size_y, y0u)):
            for x in range(size_x):
                pot[1 + x, y : y + 1] = side[x : x + 1]
            for x, row in ((0, 2 * size_x), (1 + size_x, 2 * size_x + 1)):
                pot[x, y : y + 1] = side[row : row + 1]
    else:
        end = 6 * size_x
        row_of = lax.broadcasted_iota(jnp.int32, (TILE, size_z), 0)
        entering = {
            at: total([side[j * size_x : (j + 1) * size_x] for j in range(5)])
            for at, side in ((0, yd), (size_y - 1, yu))
        }
        for x in range(size_x):
            for y in range(0, size_y, TILE):
                density = density_of.load(x, y)
                for at, side in ((0, xl), (size_x - 1, xr)):
                    if x == at:
                        density = density + total(
                            [side[j * size_y + y : j * size_y + y + TILE] for j in range(5)]
                        )
                for at, rows in entering.items():
                    if y <= at < y + TILE:
                        density = density + jnp.where(row_of == at - y, rows[x : x + 1], 0.0)
                pot[1 + x, TILE + y : 2 * TILE + y] = potential_of(
                    density, fluid_at(bits_ref, x, y), pot0_ref[x, y : y + TILE]
                )
        for x, side, own, side0, g in (
            (0, xl, own_left, x0l, G_L),
            (1 + size_x, xr, own_right, x0r, G_R),
        ):
            for y in range(0, size_y, TILE):
                density = side[5 * size_y + y : 5 * size_y + y + TILE] + total(
                    [own[j * size_y + y : j * size_y + y + TILE] for j in range(5)]
                )
                for at, row in ((0, yd), (size_y - 1, yu)):
                    if y <= at < y + TILE:
                        more = row[end + g : end + g + 1]
                        density = density + jnp.where(row_of == at - y, more, 0.0)
                pot[x, TILE + y : 2 * TILE + y] = potential_of(
                    density,
                    side0[size_y + y : size_y + y + TILE] > 0.5,
                    side0[y : y + TILE],
                )
        for y, side, own, side0 in (
            (TILE - 1, yd, own_down, y0d),
            (TILE + size_y, yu, own_up, y0u),
        ):
            density = side[5 * size_x : 6 * size_x] + total(
                [own[j * size_x : (j + 1) * size_x] for j in range(5)]
            )
            value = potential_of(density, side0[size_x : 2 * size_x] > 0.5, side0[:size_x])
            for x in range(size_x):
                pot[1 + x, y : y + 1] = value[x : x + 1]
            for x, rc, g, i in ((0, RC_L, G_L, 0), (1 + size_x, RC_R, G_R, 1)):
                density = side[end + rc : end + rc + 1] + own[end + g : end + g + 1]
                row = 2 * size_x + i
                pot[x, y : y + 1] = potential_of(
                    density, side0[row + 2 : row + 3] > 0.5, side0[row : row + 1]
                )

    post = Layers(post_out, None, size_x, edge2)
    speed = Layers(rest, None, size_x, edge2) if last else None
    collide_layers(edge2, rates, f, bits_ref, pot, sides, post, speed)
    rho = None if last else Layers(rest, None, size_x, edge1)
    stream_layers(edge1, bits_ref, post, Layers(f_out, None, size_x, edge1), rho)

    at = (5 if last else 6) * size_y
    for i, (ref, x, ks, dirs) in enumerate(
        ((left_ref, 0, LEFT, corner_pops(-1)), (right_ref, size_x - 1, RIGHT, corner_pops(1)))
    ):
        for j, k in enumerate(ks):
            _, ey, ez = SHIFT[k]
            for y in range(0, size_y, TILE):
                row = j * size_y + y
                ref[row : row + TILE] = roll_z(post.load(x, TILE + y - ey, k), ez)
        ref[at : at + TILE] = jnp.zeros((TILE, size_z), jnp.float32)
        ref[at + C_UP : at + C_UP + 1] = post.row(x, TILE + size_y - 1, dirs[0])
        ref[at + C_DN : at + C_DN + 1] = post.row(x, TILE, dirs[1])
        if not last:
            ref[5 * size_y : 6 * size_y] = rest[i]
            for h, y, leave in ((H_UP, size_y - 1, UP), (H_DN, 0, DOWN)):
                ref[at + h : at + h + 1] = total(
                    [
                        roll_z(post.row(x - SHIFT[k][0], TILE + y, k), SHIFT[k][2])
                        for k in leave
                        if 0 <= x - SHIFT[k][0] < size_x
                    ]
                )
    a_ref[...], b_ref[...] = in_swap_order(pairs, right_ref[...], left_ref[...])


def middle_kernel(first, last, *refs):
    refs = list(refs)
    take = lambda count: [refs.pop(0) for _ in range(count)]
    rates, bits_ref, pot, post_edge, edge_rest = take(5)
    if first:
        f_ref = take(1)[0]
    else:
        f_edge, f_middle, yd, yu = take(4)
    f_out, up_ref, down_ref, rest = take(4)
    post_middle = take(1)[0]
    size_x, size_y, size_z = bits_ref.shape
    edge2, edge1 = two_layers(size_x), one_layer(size_x)
    sides = None
    if first:
        f = lambda k, x, y: f_ref[k, x, y : y + TILE]
    else:
        sides = (None, None, yd, yu)
        held = Layers(f_edge, f_middle, size_x, edge1)
        f = lambda k, x, y: held.load(x, y, k)
    clear_outside(post_middle, size_x - len(edge2), size_y)
    post = Layers(post_edge, post_middle, size_x, edge2)
    speed = None
    if last:
        speed = Layers(None, None, size_x, [])
        speed.store = lambda x, y, value, c: rest.__setitem__((c, turned(x, y, size_x)), value)
        for c in range(3):
            for i, x in enumerate(edge2):
                for y in range(0, size_y, TILE):
                    rest[c, turned(x, y, size_x)] = edge_rest[c, i, y : y + TILE]
    inner = [x for x in range(size_x) if x not in edge2]
    collide_layers(inner, rates, f, bits_ref, pot, sides, post, speed)
    rho = None if last else Layers(edge_rest, rest, size_x, edge1)
    inner = [x for x in range(size_x) if x not in edge1]
    stream_layers(inner, bits_ref, post, Layers(None, f_out, size_x, edge1), rho)
    for ref, y, ks in ((up_ref, size_y - 1, UP), (down_ref, 0, DOWN)):
        for j, k in enumerate(ks):
            ex, _, ez = SHIFT[k]
            for x in range(size_x):
                row = j * size_x + x
                if 0 <= x - ex < size_x:
                    ref[row : row + 1] = post.row(x - ex, TILE + y, k)
                else:
                    ref[row : row + 1] = jnp.zeros((1, size_z), jnp.float32)
            if ez != 0:
                rows = slice(j * size_x, (j + 1) * size_x)
                ref[rows] = roll_z(ref[rows], ez)
        if not last:
            for x in range(size_x):
                ref[5 * size_x + x : 5 * size_x + x + 1] = rho.row(x, y)


def pack_kernel(last, pairs, size_x, size_y, *refs):
    up_in, down_in, a_ref, b_ref, own_right, own_left, up_ref, down_ref, xl, xr = refs
    sort_received(pairs, a_ref, b_ref, xl, xr)
    parts = 5 if last else 6
    at = parts * size_y
    for ref, source, y, ks, c, h in (
        (up_ref, up_in, size_y - 1, UP, C_UP, H_UP),
        (down_ref, down_in, 0, DOWN, C_DN, H_DN),
    ):
        ref[...] = jnp.zeros(ref.shape, jnp.float32)
        ref[: parts * size_x] = source[: parts * size_x]
        for side, own, x, ex, rc, g in (
            (xl, own_left, 0, 1, RC_L, G_L),
            (xr, own_right, size_x - 1, -1, RC_R, G_R),
        ):
            j = [i for i, k in enumerate(ks) if SHIFT[k][0] == ex][0]
            row = j * size_x + x
            ref[row : row + 1] = side[at + c : at + c + 1]
            if not last:
                row = 5 * size_x + x
                ref[row : row + 1] = source[row : row + 1] + total(
                    [side[i * size_y + y : i * size_y + y + 1] for i in range(5)]
                )
                row = 6 * size_x
                ref[row + rc : row + rc + 1] = side[5 * size_y + y : 5 * size_y + y + 1] + total(
                    [own[i * size_y + y : i * size_y + y + 1] for i in range(5)]
                )
                ref[row + g : row + g + 1] = (
                    side[at + h : at + h + 1] + own[at + c : at + c + 1]
                )


def turned(layer, row, layers):
    return pl.ds(layer + row * layers, TILE, stride=layers)


def write_kernel(f_edge, f_middle, bits_ref, xl, xr, speed_ref, out_hbm, flat_ref, speed_hbm, sems, speed_sem):
    size_x, size_y, _ = bits_ref.shape
    held = Layers(f_edge, f_middle, size_x, one_layer(size_x))
    copies = [pltpu.make_async_copy(speed_ref, speed_hbm, speed_sem)]
    copies[0].start()
    for k in range(N):
        for x in range(size_x):
            for y in range(0, size_y, TILE):
                value = held.load(x, y, k)
                for at, side, ks in ((0, xl, RIGHT), (size_x - 1, xr, LEFT)):
                    if x == at and k in ks:
                        row = ks.index(k) * size_y + y
                        value = value + side[row : row + TILE]
                value = jnp.where(fluid_at(bits_ref, x, y), value, 0.0)
                flat_ref[k, turned(x, y, size_x)] = value
        copies.append(pltpu.make_async_copy(flat_ref.at[k], out_hbm.at[k], sems.at[k]))
        copies[-1].start()
    for copy in copies:
        copy.wait()


def end_kernel(out_in, flat_ref, mask_ref, yd, yu, out_hbm, planes, sems):
    del out_in
    layers = planes.shape[1]
    last = flat_ref.shape[1] - layers
    copies = []
    for at, side, ks in ((0, yd, UP), (last, yu, DOWN)):
        for j, k in enumerate(ks):
            i = len(copies)
            entering = side[j * layers : (j + 1) * layers]
            fluid = mask_ref[0, at : at + layers] > 0.5
            planes[i] = jnp.where(fluid, flat_ref[k, at : at + layers] + entering, 0.0)
            target = out_hbm.at[k, pl.ds(at, layers)]
            copies.append(pltpu.make_async_copy(planes.at[i], target, sems.at[i]))
            copies[-1].start()
    for copy in copies:
        copy.wait()


VMEM = pl.BlockSpec(memory_space=pltpu.VMEM)
SMEM = pl.BlockSpec(memory_space=pltpu.SMEM)
HBM = pl.BlockSpec(memory_space=pltpu.HBM)


def call(kernel, outs, args, special=None, special_out=None, scratch=(), cost=None, **kwargs):
    special, special_out = special or {}, special_out or {}
    return pl.pallas_call(
        kernel,
        out_shape=[jax.ShapeDtypeStruct(shape, dtype) for shape, dtype in outs],
        in_specs=[special.get(i, VMEM) for i in range(len(args))],
        out_specs=[special_out.get(i, VMEM) for i in range(len(outs))],
        scratch_shapes=[
            pltpu.VMEM(item, jnp.float32) if isinstance(item, tuple) else item for item in scratch
        ],
        compiler_params=pltpu.CompilerParams(vmem_limit_bytes=16 * 2**20),
        cost_estimate=cost,
        **kwargs,
    )(*args)


def shift(forward, backward, axis):
    count = lax.axis_size(axis)
    ahead = [(i, (i + 1) % count) for i in range(count)]
    return (
        lax.ppermute(forward, axis, ahead),
        lax.ppermute(backward, axis, [(b, a) for a, b in ahead]),
    )


def swap(a, b, axis):
    count = lax.axis_size(axis)
    partners = [
        [(i, (i + (1 if i % 2 == parity else -1)) % count) for i in range(count)]
        for parity in range(2)
    ]
    b = lax.ppermute(b, axis, partners[1])
    return lax.ppermute(a, axis, partners[0]), b


def per_device(populations, fluid_mask, wet_class, wall_potential, relax_rates):
    rows_x, rows_y, size_z = fluid_mask.shape
    pairs = lax.axis_size("gy") % 2 == 0
    exchange = swap if pairs else shift
    size_x, size_y = rows_y, rows_x
    cells = size_x * size_y
    f32, i32 = jnp.float32, jnp.int32
    whole = ((size_x, size_y, size_z), f32)
    rows = lambda count: ((count, size_z), f32)
    fields = lambda count: ((N, count, size_y, size_z), f32)
    flat = lambda count: ((count, cells, size_z), f32)
    padded = (size_x + 2, size_y + PAD, size_z)
    operations = 400 * cells * size_z
    cost = pl.CostEstimate(flops=operations, bytes_accessed=4 * operations // 20, transcendentals=0)

    operands = (
        populations.reshape(N, cells, size_z),
        fluid_mask.reshape(cells, size_z),
        wet_class.reshape(cells, size_z),
        wall_potential,
    )
    operands = [pltpu.with_memory_space_constraint(item, pltpu.HBM) for item in operands]
    start_rows = rows(2 * size_x + TILE)
    a, b, row_faces = call(
        functools.partial(face_kernel, pairs),
        [rows(2 * size_y), rows(2 * size_y), ((2, 2 * size_x, size_z), f32)],
        operands,
        special={i: HBM for i in range(4)},
        scratch=[
            (2, N, size_y, size_z),
            (2, N, size_x, size_z),
            pltpu.VMEM((cells, size_z), i32),
            pltpu.VMEM((cells, size_z), i32),
            pltpu.SMEM(wall_potential.shape, f32),
            pltpu.SemaphoreType.DMA((2, size_y)),
            pltpu.SemaphoreType.DMA((2,)),
            pltpu.SemaphoreType.DMA((3,)),
        ],
    )
    tile = call(
        load_kernel,
        [flat(N), ((cells, size_z), i32), ((cells, size_z), i32)],
        (*operands[:3], a),
        special={i: HBM for i in range(3)},
        scratch=[pltpu.SemaphoreType.DMA((N,)), pltpu.SemaphoreType.DMA((2,))],
        cost=cost,
    )
    a, b = exchange(a, b, "gy")
    up, down, x0l, x0r = call(
        functools.partial(start_pack_kernel, pairs),
        [start_rows, start_rows, rows(2 * size_y), rows(2 * size_y)],
        (row_faces, a, b),
    )
    f, rates, flat_mask, mask, pot0 = call(
        turn_kernel,
        [fields(size_x), ((N, TILE, size_z), f32), flat(2), whole, whole],
        (*tile, wall_potential, relax_rates),
        special={3: SMEM, 4: SMEM},
        cost=cost,
    )
    y0d, y0u = shift(up, down, "gx")
    whole_bits = [((size_x, size_y, size_z), i32)]
    (bits,) = call(bits_kernel, whole_bits, (mask, x0l, x0r), scratch=[padded], cost=cost)
    (bits,) = call(
        more_bits_kernel, whole_bits, (bits, y0d, y0u), scratch=[(2, size_x + PAD, size_z)]
    )
    edge2, edge1 = len(two_layers(size_x)), len(one_layer(size_x))
    held, sent = (f,), ()
    for step in range(STEPS):
        first, last = step == 0, step == STEPS - 1
        parts = 5 if last else 6
        x_rows, y_rows = rows(parts * size_y + TILE), rows(parts * size_x + (0 if last else TILE))
        pot, post, f_edge, right, left, a, b, rest = call(
            functools.partial(edge_kernel, first, last, pairs),
            [
                (padded, f32),
                ((N, edge2, size_y + PAD, size_z), f32),
                fields(edge1),
                x_rows,
                x_rows,
                x_rows,
                x_rows,
                ((3, edge2, size_y, size_z) if last else (edge1, size_y, size_z), f32),
            ],
            (rates, bits, pot0, x0l, x0r, y0d, y0u, *held, *sent),
            cost=cost,
        )
        a, b = exchange(a, b, "gy")
        f_middle, up, down, more = call(
            functools.partial(middle_kernel, first, last),
            [
                fields(size_x - edge1),
                y_rows,
                y_rows,
                flat(3) if last else ((size_x - edge1, size_y, size_z), f32),
            ],
            (rates, bits, pot, post, rest, *held[:2], *sent[2:4]),
            scratch=[(N, size_x - edge2, size_y + PAD, size_z)],
            cost=cost,
        )
        up, down, xl, xr = call(
            functools.partial(pack_kernel, last, pairs, size_x, size_y),
            [y_rows, y_rows, x_rows, x_rows],
            (up, down, a, b, right, left),
        )
        yd, yu = shift(up, down, "gx")
        held = (f_edge, f_middle, rest, more)
        sent = (xl, xr, yd, yu, right, left, up, down)
    out, flat_f, speed = call(
        write_kernel,
        [flat(N), flat(N), flat(3)],
        (f_edge, f_middle, bits, xl, xr, more),
        special_out={0: HBM, 2: HBM},
        scratch=[pltpu.SemaphoreType.DMA((N,)), pltpu.SemaphoreType.DMA(())],
        cost=cost,
    )
    (out,) = call(
        end_kernel,
        [flat(N)],
        (out, flat_f, flat_mask, yd, yu),
        special={0: HBM},
        special_out={0: HBM},
        scratch=[(10, size_x, size_z), pltpu.SemaphoreType.DMA((10,))],
        input_output_aliases={0: 0},
    )
    shape = (rows_x, rows_y, size_z)
    return out.reshape(N, *shape), speed.reshape(3, *shape)


def solution(mesh):
    return jax.shard_map(
        per_device,
        mesh=mesh,
        in_specs=(
            P(None, ("groups", "gx"), "gy", None),
            P(("groups", "gx"), "gy", None),
            P(("groups", "gx"), "gy", None),
            P("groups"),
            P(),
        ),
        out_specs=(P(None, ("groups", "gx"), "gy", None), P(None, ("groups", "gx"), "gy", None)),
        check_vma=False,
    )
```

```python
import functools

import jax
import jax.numpy as jnp
from jax import lax
from jax.experimental import pallas as pl
from jax.experimental.pallas import tpu as pltpu
from jax.sharding import PartitionSpec as P

STEPS = 4
STRENGTH = 2.5
VELOCITY = (
    (0, 0, 0),
    (1, 0, 0),
    (-1, 0, 0),
    (0, 1, 0),
    (0, -1, 0),
    (0, 0, 1),
    (0, 0, -1),
    (1, 1, 0),
    (-1, -1, 0),
    (1, -1, 0),
    (-1, 1, 0),
    (1, 0, 1),
    (-1, 0, -1),
    (1, 0, -1),
    (-1, 0, 1),
    (0, 1, 1),
    (0, -1, -1),
    (0, 1, -1),
    (0, -1, 1),
)
N = len(VELOCITY)
OPPOSITE = [0] + [k + 1 if k % 2 == 1 else k - 1 for k in range(1, N)]
SHIFT = [(y, x, z) for x, y, z in VELOCITY]
RIGHT = [k for k in range(N) if SHIFT[k][0] == 1]
LEFT = [k for k in range(N) if SHIFT[k][0] == -1]
UP = [k for k in range(N) if SHIFT[k][1] == 1]
DOWN = [k for k in range(N) if SHIFT[k][1] == -1]
TILE = 8
PAD = 2 * TILE

C_UP, C_DN, H_UP, H_DN = 0, 1, 2, 3
RC_L, RC_R, G_L, G_R = 0, 1, 2, 3


def roll_z(value, step):
    if step == 0:
        return value
    return pltpu.roll(value, step % value.shape[-1], value.ndim - 1)


def total(values):
    values = list(values)
    while len(values) > 1:
        values = [
            values[i] + values[i + 1] if i + 1 < len(values) else values[i]
            for i in range(0, len(values), 2)
        ]
    return values[0]


def potential_of(density, fluid, solid_value):
    return jnp.where(fluid, 1.0 - jnp.exp(-density), solid_value)


def collide(f, fluid, force, rate):
    fx, fy, fz = force
    s = {k: f[k] + f[k + 1] for k in range(1, N, 2)}
    d = {k: f[k] - f[k + 1] for k in range(1, N, 2)}
    xxyy, xxzz, yyzz = s[7] + s[9], s[11] + s[13], s[15] + s[17]
    xy, xz, yz = s[7] - s[9], s[11] - s[13], s[15] - s[17]
    xyy, yxx = d[7] + d[9], d[7] - d[9]
    xzz, zxx = d[11] + d[13], d[11] - d[13]
    yzz, zyy = d[15] + d[17], d[15] - d[17]
    jx, jy, jz = d[1] + (xyy + xzz), d[3] + (yxx + yzz), d[5] + (zxx + zyy)
    xx, yy, zz = s[1] + (xxyy + xxzz), s[3] + (xxyy + yyzz), s[5] + (xxzz + yyzz)
    rho = (f[0] + s[1]) + (s[3] + s[5]) + (xxyy + (xxzz + yyzz))
    safe = jnp.where(fluid, rho, 1.0)
    inverse = 1.0 / safe
    hx, hy, hz = 0.5 * fx, 0.5 * fy, 0.5 * fz
    gx, gy, gz = jx + hx, jy + hy, jz + hz
    ux, uy, uz = gx * inverse, gy * inverse, gz * inverse
    third = safe * (1.0 / 3.0)
    ninth = safe * (1.0 / 9.0)
    px, py, pz = gx - fx, gy - fy, gz - fz
    txx, tyy, tzz = ux * px, uy * py, uz * pz
    sx, sy, sz = ux * fx, uy * fy, uz * fz
    pxy = ux * fy + uy * fx
    pxz = ux * fz + uz * fx
    pyz = uy * fz + uz * fy
    t3, s3 = (txx + tyy + tzz) * (1.0 / 3.0), (sx + sy + sz) * (2.0 / 3.0)
    rho = rho - rate(0) * (rho - safe)
    nx = jx + fx - rate(1) * (jx - safe * ux + hx)
    ny = jy + fy - rate(2) * (jy - safe * uy + hy)
    nz = jz + fz - rate(3) * (jz - safe * uz + hz)
    xy = xy + rate(4) * (gx * uy - 0.5 * pxy - xy) + pxy
    xz = xz + rate(5) * (gx * uz - 0.5 * pxz - xz) + pxz
    yz = yz + rate(6) * (gy * uz - 0.5 * pyz - yz) + pyz
    xx = xx + rate(7) * (third + txx - xx) + 2.0 * sx
    yy = yy + rate(8) * (third + tyy - yy) + 2.0 * sy
    zz = zz + rate(9) * (third + tzz - zz) + 2.0 * sz
    ex, ey, ez = jx * (1.0 / 3.0), jy * (1.0 / 3.0), jz * (1.0 / 3.0)
    qx, qy, qz = fx * (1.0 / 3.0), fy * (1.0 / 3.0), fz * (1.0 / 3.0)
    xyy = xyy + rate(10) * (ex - xyy) + qx
    xzz = xzz + rate(11) * (ex - xzz) + qx
    yxx = yxx + rate(12) * (ey - yxx) + qy
    yzz = yzz + rate(13) * (ey - yzz) + qy
    zxx = zxx + rate(14) * (ez - zxx) + qz
    zyy = zyy + rate(15) * (ez - zyy) + qz
    base = ninth + t3
    xxyy = xxyy + rate(16) * (base - 0.5 * tzz - xxyy) + (s3 - sz)
    xxzz = xxzz + rate(17) * (base - 0.5 * tyy - xxzz) + (s3 - sy)
    yyzz = yyzz + rate(18) * (base - 0.5 * txx - yyzz) + (s3 - sx)
    out = [None] * N
    for first, even, cross, odd1, odd2 in (
        (7, xxyy, xy, xyy, yxx),
        (11, xxzz, xz, xzz, zxx),
        (15, yyzz, yz, yzz, zyy),
    ):
        even, cross, odd1, odd2 = 0.25 * even, 0.25 * cross, 0.25 * odd1, 0.25 * odd2
        plus, minus = even + cross, even - cross
        both, diff = odd1 + odd2, odd1 - odd2
        out[first], out[first + 1] = plus + both, plus - both
        out[first + 2], out[first + 3] = minus + diff, minus - diff
    pairs = []
    for first, even, odd in (
        (1, xx - (xxyy + xxzz), nx - (xyy + xzz)),
        (3, yy - (xxyy + yyzz), ny - (yxx + yzz)),
        (5, zz - (xxzz + yyzz), nz - (zxx + zyy)),
    ):
        half_even, half_odd = 0.5 * even, 0.5 * odd
        out[first], out[first + 1] = half_even + half_odd, half_even - half_odd
        pairs.append(even)
    out[0] = rho - (pairs[0] + pairs[1] + pairs[2]) - (xxyy + xxzz + yyzz)
    return out, (ux, uy, uz)


def corner_pops(side):
    return SHIFT.index((side, 1, 0)), SHIFT.index((side, -1, 0))


def in_swap_order(pairs, right, left):
    if not pairs:
        return right, left
    odd = lax.axis_index("gy") % 2 == 1
    return jnp.where(odd, left, right), jnp.where(odd, right, left)


def sort_received(pairs, a_ref, b_ref, xl_ref, xr_ref):
    if pairs:
        xr_ref[...], xl_ref[...] = in_swap_order(pairs, a_ref[...], b_ref[...])
    else:
        xl_ref[...], xr_ref[...] = a_ref[...], b_ref[...]


def wall_of(wet, wall_ref):
    wall = jnp.zeros(wet.shape, jnp.float32)
    for c in range(wall_ref.shape[0]):
        wall = jnp.where(wet == c, wall_ref[c], wall)
    return wall


def face_kernel(f_hbm, mask_hbm, wet_hbm, wall_hbm, up_ref, down_ref, *scratch):
    row_in, mask_in, wet_in, wall_in, sems = scratch
    layers = row_in.shape[2]
    sides = ((0, down_ref, 0), (1, up_ref, f_hbm.shape[1] - layers))
    copies = [pltpu.make_async_copy(wall_hbm, wall_in, sems.at[0])]
    for s, _, at in sides:
        for i, (source, target) in enumerate(((mask_hbm, mask_in), (wet_hbm, wet_in))):
            sem = sems.at[1 + 2 * s + i]
            copies.append(
                pltpu.make_async_copy(source.at[pl.ds(at, layers)], target.at[s], sem)
            )
        sem = sems.at[5 + s]
        copies.append(
            pltpu.make_async_copy(f_hbm.at[:, pl.ds(at, layers)], row_in.at[s], sem)
        )
    for copy in copies:
        copy.start()
    for copy in copies:
        copy.wait()
    for s, ref, _ in sides:
        pore = mask_in[s] == 1
        density = total([row_in[s, k] for k in range(N)])
        ref[:layers] = potential_of(density, pore, wall_of(wet_in[s], wall_in))
        ref[layers:] = jnp.where(pore, 1.0, 0.0)


def turn_kernel(raw_ref, mask_in, wet_in, wall_ref, rate_ref, f_ref, rates_ref, flat_ref, mask_ref, pot_ref):
    layers, rows = f_ref.shape[1], f_ref.shape[2]
    for k in range(N):
        rates_ref[k] = jnp.full(rates_ref.shape[1:], rate_ref[k], jnp.float32)
    for i in range(0, layers * rows, TILE):
        at = slice(i, i + TILE)
        pore = mask_in[at] == 1
        density = total([raw_ref[k, at] for k in range(N)])
        flat_ref[0, at] = jnp.where(pore, 1.0, 0.0)
        flat_ref[1, at] = potential_of(density, pore, wall_of(wet_in[at], wall_ref))
    for i in range(layers):
        mask_ref[i] = flat_ref[0, pl.ds(i, rows, stride=layers)]
        pot_ref[i] = flat_ref[1, pl.ds(i, rows, stride=layers)]
    for k in range(N):
        for i in range(layers):
            f_ref[k, i] = raw_ref[k, pl.ds(i, rows, stride=layers)]


def start_pack_kernel(pairs, pot_ref, mask_ref, from_below, from_above, a_ref, b_ref, left_ref, right_ref):
    layers, rows = mask_ref.shape[0], mask_ref.shape[1]
    for ref, layer in ((left_ref, 0), (right_ref, layers - 1)):
        ref[:rows] = pot_ref[layer]
        ref[rows : 2 * rows] = mask_ref[layer]
        ref[2 * rows :] = jnp.zeros((TILE, ref.shape[1]), jnp.float32)
        for i, side in enumerate((from_below, from_above)):
            row = 2 * rows + i
            ref[row : row + 1] = side[layer : layer + 1]
            ref[row + 2 : row + 3] = side[layers + layer : layers + layer + 1]
    a_ref[...], b_ref[...] = in_swap_order(pairs, right_ref[...], left_ref[...])


def bits_kernel(mask_ref, from_below, from_above, bits_ref, pad_ref):
    size_x, size_y, size_z = mask_ref.shape
    nothing = jnp.zeros((TILE, size_z), jnp.float32)
    for x in (0, size_x + 1):
        for y in range(0, size_y + PAD, TILE):
            pad_ref[x, y : y + TILE] = nothing
    for x in range(size_x):
        pad_ref[1 + x, TILE : TILE + size_y] = mask_ref[x]
        for y, side in ((TILE - 1, from_below), (TILE + size_y, from_above)):
            pad_ref[1 + x, y : y + 1] = side[size_x + x : size_x + x + 1]
    for x in range(size_x):
        for y in range(0, size_y, TILE):
            bits = jnp.zeros((TILE, size_z), jnp.int32)
            for k in range(N):
                ex, ey, ez = SHIFT[k]
                row = TILE + y - ey
                source = roll_z(pad_ref[1 + x - ex, row : row + TILE], ez)
                bits = bits | jnp.where(source > 0.5, 1 << k, 0)
            bits_ref[x, y : y + TILE] = bits


def ring_kernel(pairs, bits_in, a_ref, b_ref, from_below, from_above, bits_ref, xl, xr, yd, yu, pad_ref):
    size_x, size_y, _ = bits_ref.shape
    sort_received(pairs, a_ref, b_ref, xl, xr)
    corner = 2 * size_y
    for i, (ref, side) in enumerate(((yd, from_below), (yu, from_above))):
        ref[: 2 * size_x] = side[...]
        ref[2 * size_x :] = jnp.zeros((TILE, ref.shape[1]), jnp.float32)
        for j, layer in enumerate((xl, xr)):
            row = 2 * size_x + j
            ref[row : row + 1] = layer[corner + i : corner + i + 1]
            ref[row + 2 : row + 3] = layer[corner + 2 + i : corner + 3 + i]
    bits_ref[...] = bits_in[...]
    for i, (side, ks, x) in enumerate(((xl, RIGHT, 0), (xr, LEFT, size_x - 1))):
        pad_ref[i, TILE : TILE + size_y] = side[size_y : 2 * size_y]
        for row, at in ((TILE - 1, corner + 2), (TILE + size_y, corner + 3)):
            pad_ref[i, row : row + 1] = side[at : at + 1]
        for y in range(0, size_y, TILE):
            bits = bits_in[x, y : y + TILE]
            for k in ks:
                _, ey, ez = SHIFT[k]
                row = TILE + y - ey
                source = roll_z(pad_ref[i, row : row + TILE], ez)
                bits = bits | jnp.where(source > 0.5, 1 << k, 0)
            bits_ref[x, y : y + TILE] = bits


class Layers:
    def __init__(self, edge_ref, middle_ref, size_x, edge):
        self.where = {}
        middle = [x for x in range(size_x) if x not in edge]
        for ref, xs in ((edge_ref, edge), (middle_ref, middle)):
            for i, x in enumerate(xs):
                self.where[x] = (ref, i)

    def load(self, x, y, k=None):
        ref, i = self.where[x]
        return ref[i, y : y + TILE] if k is None else ref[k, i, y : y + TILE]

    def row(self, x, y, k=None):
        ref, i = self.where[x]
        return ref[i, y : y + 1] if k is None else ref[k, i, y : y + 1]

    def store(self, x, y, value, k=None):
        ref, i = self.where[x]
        if k is None:
            ref[i, y : y + TILE] = value
        else:
            ref[k, i, y : y + TILE] = value


def two_layers(size_x):
    return [0, 1, size_x - 2, size_x - 1]


def one_layer(size_x):
    return [0, size_x - 1]


def fluid_at(bits_ref, x, y):
    return (bits_ref[x, y : y + TILE] & 1) != 0


def clear_outside(post, layers, size_y):
    nothing = jnp.zeros((TILE, post.shape[-1]), jnp.float32)
    for i in range(layers):
        for k in UP:
            post[k, i, :TILE] = nothing
        for k in DOWN:
            post[k, i, TILE + size_y :] = nothing


def collide_layers(xs, rates, f, bits_ref, pot, sides, post, speed):
    size_x, size_y, size_z = bits_ref.shape
    row_of = lax.broadcasted_iota(jnp.int32, (TILE, size_z), 0)
    for x in xs:
        for y in range(0, size_y, TILE):
            near = {
                (i, j): pot[1 + x + i, TILE + y + j : 2 * TILE + y + j]
                for i in (-1, 0, 1)
                for j in (-1, 0, 1)
            }
            scale = near[0, 0] * (STRENGTH / 36.0)
            dx = near[1, 0] - near[-1, 0]
            dy = near[0, 1] - near[0, -1]
            pp, pm, mp, mm = near[1, 1], near[1, -1], near[-1, 1], near[-1, -1]
            both = near[1, 0] + near[-1, 0] + near[0, 1] + near[0, -1] + 2.0 * near[0, 0]
            diag1, diag2 = pp - mm, pm - mp
            force = (
                scale * (2.0 * dy + (diag1 - diag2) + (roll_z(dy, 1) + roll_z(dy, -1))),
                scale * (2.0 * dx + (diag1 + diag2) + (roll_z(dx, 1) + roll_z(dx, -1))),
                scale * (roll_z(both, -1) - roll_z(both, 1)),
            )
            now = [f(k, x, y) for k in range(N)]
            if sides is not None:
                xl, xr, yd, yu = sides
                for at, side, ks in ((0, xl, RIGHT), (size_x - 1, xr, LEFT)):
                    if x == at:
                        for j, k in enumerate(ks):
                            now[k] = now[k] + side[j * size_y + y : j * size_y + y + TILE]
                for at, side, ks in ((0, yd, UP), (size_y - 1, yu, DOWN)):
                    if y <= at < y + TILE:
                        for j, k in enumerate(ks):
                            entering = side[j * size_x + x : j * size_x + x + 1]
                            now[k] = now[k] + jnp.where(row_of == at - y, entering, 0.0)
            fluid = fluid_at(bits_ref, x, y)
            after, at_speed = collide(now, fluid, force, lambda r: rates[r])
            for k in range(N):
                post.store(x, TILE + y, jnp.where(fluid, after[k], 0.0), k)
            if speed is not None:
                for c in range(3):
                    speed.store(x, y, jnp.where(fluid, at_speed[c], 0.0), c)


def stream_layers(xs, bits_ref, post, f, rho):
    size_x, size_y, _ = bits_ref.shape
    for x in xs:
        for y in range(0, size_y, TILE):
            bits = bits_ref[x, y : y + TILE]
            arrived = []
            for k in range(N):
                ex, ey, ez = SHIFT[k]
                value = post.load(x, TILE + y, OPPOSITE[k])
                if k > 0:
                    come = 0.0
                    if 0 <= x - ex < size_x:
                        come = roll_z(post.load(x - ex, TILE + y - ey, k), ez)
                    value = jnp.where((bits & (1 << k)) != 0, come, value)
                f.store(x, y, value, k)
                arrived.append(value)
            if rho is not None:
                rho.store(x, y, total(arrived))


def edge_kernel(first, last, pairs, *refs):
    refs = list(refs)
    take = lambda count: [refs.pop(0) for _ in range(count)]
    rates, bits_ref, pot0_ref, x0l, x0r, y0d, y0u = take(7)
    if first:
        f_ref = take(1)[0]
    else:
        f_edge, f_middle, rho_edge, rho_middle, xl, xr, yd, yu = take(8)
        own_right, own_left, own_up, own_down = take(4)
    pot, post_out, f_out, right_ref, left_ref, a_ref, b_ref, rest = take(8)
    size_x, size_y, size_z = bits_ref.shape
    edge2, edge1 = two_layers(size_x), one_layer(size_x)
    sides = None
    if first:
        f = lambda k, x, y: f_ref[k, x, y : y + TILE]
    else:
        sides = (xl, xr, yd, yu)
        held = Layers(f_edge, f_middle, size_x, edge1)
        density_of = Layers(rho_edge, rho_middle, size_x, edge1)
        f = lambda k, x, y: held.load(x, y, k)
    clear_outside(post_out, len(edge2), size_y)

    if first:
        for x in range(size_x):
            pot[1 + x, TILE : TILE + size_y] = pot0_ref[x]
        for x, side in ((0, x0l), (1 + size_x, x0r)):
            pot[x, TILE : TILE + size_y] = side[:size_y]
        for y, side in ((TILE - 1, y0d), (TILE + size_y, y0u)):
            for x in range(size_x):
                pot[1 + x, y : y + 1] = side[x : x + 1]
            for x, row in ((0, 2 * size_x), (1 + size_x, 2 * size_x + 1)):
                pot[x, y : y + 1] = side[row : row + 1]
    else:
        end = 6 * size_x
        row_of = lax.broadcasted_iota(jnp.int32, (TILE, size_z), 0)
        entering = {
            at: total([side[j * size_x : (j + 1) * size_x] for j in range(5)])
            for at, side in ((0, yd), (size_y - 1, yu))
        }
        for x in range(size_x):
            for y in range(0, size_y, TILE):
                density = density_of.load(x, y)
                for at, side in ((0, xl), (size_x - 1, xr)):
                    if x == at:
                        density = density + total(
                            [side[j * size_y + y : j * size_y + y + TILE] for j in range(5)]
                        )
                for at, rows in entering.items():
                    if y <= at < y + TILE:
                        density = density + jnp.where(row_of == at - y, rows[x : x + 1], 0.0)
                pot[1 + x, TILE + y : 2 * TILE + y] = potential_of(
                    density, fluid_at(bits_ref, x, y), pot0_ref[x, y : y + TILE]
                )
        for x, side, own, side0, g in (
            (0, xl, own_left, x0l, G_L),
            (1 + size_x, xr, own_right, x0r, G_R),
        ):
            for y in range(0, size_y, TILE):
                density = side[5 * size_y + y : 5 * size_y + y + TILE] + total(
                    [own[j * size_y + y : j * size_y + y + TILE] for j in range(5)]
                )
                for at, row in ((0, yd), (size_y - 1, yu)):
                    if y <= at < y + TILE:
                        more = row[end + g : end + g + 1]
                        density = density + jnp.where(row_of == at - y, more, 0.0)
                pot[x, TILE + y : 2 * TILE + y] = potential_of(
                    density,
                    side0[size_y + y : size_y + y + TILE] > 0.5,
                    side0[y : y + TILE],
                )
        for y, side, own, side0 in (
            (TILE - 1, yd, own_down, y0d),
            (TILE + size_y, yu, own_up, y0u),
        ):
            density = side[5 * size_x : 6 * size_x] + total(
                [own[j * size_x : (j + 1) * size_x] for j in range(5)]
            )
            value = potential_of(density, side0[size_x : 2 * size_x] > 0.5, side0[:size_x])
            for x in range(size_x):
                pot[1 + x, y : y + 1] = value[x : x + 1]
            for x, rc, g, i in ((0, RC_L, G_L, 0), (1 + size_x, RC_R, G_R, 1)):
                density = side[end + rc : end + rc + 1] + own[end + g : end + g + 1]
                row = 2 * size_x + i
                pot[x, y : y + 1] = potential_of(
                    density, side0[row + 2 : row + 3] > 0.5, side0[row : row + 1]
                )

    post = Layers(post_out, None, size_x, edge2)
    speed = Layers(rest, None, size_x, edge2) if last else None
    collide_layers(edge2, rates, f, bits_ref, pot, sides, post, speed)
    rho = None if last else Layers(rest, None, size_x, edge1)
    stream_layers(edge1, bits_ref, post, Layers(f_out, None, size_x, edge1), rho)

    at = (5 if last else 6) * size_y
    for i, (ref, x, ks, dirs) in enumerate(
        ((left_ref, 0, LEFT, corner_pops(-1)), (right_ref, size_x - 1, RIGHT, corner_pops(1)))
    ):
        for j, k in enumerate(ks):
            _, ey, ez = SHIFT[k]
            for y in range(0, size_y, TILE):
                row = j * size_y + y
                ref[row : row + TILE] = roll_z(post.load(x, TILE + y - ey, k), ez)
        ref[at : at + TILE] = jnp.zeros((TILE, size_z), jnp.float32)
        ref[at + C_UP : at + C_UP + 1] = post.row(x, TILE + size_y - 1, dirs[0])
        ref[at + C_DN : at + C_DN + 1] = post.row(x, TILE, dirs[1])
        if not last:
            ref[5 * size_y : 6 * size_y] = rest[i]
            for h, y, leave in ((H_UP, size_y - 1, UP), (H_DN, 0, DOWN)):
                ref[at + h : at + h + 1] = total(
                    [
                        roll_z(post.row(x - SHIFT[k][0], TILE + y, k), SHIFT[k][2])
                        for k in leave
                        if 0 <= x - SHIFT[k][0] < size_x
                    ]
                )
    a_ref[...], b_ref[...] = in_swap_order(pairs, right_ref[...], left_ref[...])


def middle_kernel(first, last, *refs):
    refs = list(refs)
    take = lambda count: [refs.pop(0) for _ in range(count)]
    rates, bits_ref, pot, post_edge, edge_rest = take(5)
    if first:
        f_ref = take(1)[0]
    else:
        f_edge, f_middle, yd, yu = take(4)
    f_out, up_ref, down_ref, rest = take(4)
    post_middle = take(1)[0]
    size_x, size_y, size_z = bits_ref.shape
    edge2, edge1 = two_layers(size_x), one_layer(size_x)
    sides = None
    if first:
        f = lambda k, x, y: f_ref[k, x, y : y + TILE]
    else:
        sides = (None, None, yd, yu)
        held = Layers(f_edge, f_middle, size_x, edge1)
        f = lambda k, x, y: held.load(x, y, k)
    clear_outside(post_middle, size_x - len(edge2), size_y)
    post = Layers(post_edge, post_middle, size_x, edge2)
    speed = None
    if last:
        speed = Layers(None, None, size_x, [])
        speed.store = lambda x, y, value, c: rest.__setitem__((c, turned(x, y, size_x)), value)
        for c in range(3):
            for i, x in enumerate(edge2):
                for y in range(0, size_y, TILE):
                    rest[c, turned(x, y, size_x)] = edge_rest[c, i, y : y + TILE]
    inner = [x for x in range(size_x) if x not in edge2]
    collide_layers(inner, rates, f, bits_ref, pot, sides, post, speed)
    rho = None if last else Layers(edge_rest, rest, size_x, edge1)
    inner = [x for x in range(size_x) if x not in edge1]
    stream_layers(inner, bits_ref, post, Layers(None, f_out, size_x, edge1), rho)
    for ref, y, ks in ((up_ref, size_y - 1, UP), (down_ref, 0, DOWN)):
        for j, k in enumerate(ks):
            ex, _, ez = SHIFT[k]
            for x in range(size_x):
                row = j * size_x + x
                if 0 <= x - ex < size_x:
                    ref[row : row + 1] = post.row(x - ex, TILE + y, k)
                else:
                    ref[row : row + 1] = jnp.zeros((1, size_z), jnp.float32)
            if ez != 0:
                rows = slice(j * size_x, (j + 1) * size_x)
                ref[rows] = roll_z(ref[rows], ez)
        if not last:
            for x in range(size_x):
                ref[5 * size_x + x : 5 * size_x + x + 1] = rho.row(x, y)


def pack_kernel(last, pairs, size_x, size_y, *refs):
    up_in, down_in, a_ref, b_ref, own_right, own_left, up_ref, down_ref, xl, xr = refs
    sort_received(pairs, a_ref, b_ref, xl, xr)
    parts = 5 if last else 6
    at = parts * size_y
    for ref, source, y, ks, c, h in (
        (up_ref, up_in, size_y - 1, UP, C_UP, H_UP),
        (down_ref, down_in, 0, DOWN, C_DN, H_DN),
    ):
        ref[...] = jnp.zeros(ref.shape, jnp.float32)
        ref[: parts * size_x] = source[: parts * size_x]
        for side, own, x, ex, rc, g in (
            (xl, own_left, 0, 1, RC_L, G_L),
            (xr, own_right, size_x - 1, -1, RC_R, G_R),
        ):
            j = [i for i, k in enumerate(ks) if SHIFT[k][0] == ex][0]
            row = j * size_x + x
            ref[row : row + 1] = side[at + c : at + c + 1]
            if not last:
                row = 5 * size_x + x
                ref[row : row + 1] = source[row : row + 1] + total(
                    [side[i * size_y + y : i * size_y + y + 1] for i in range(5)]
                )
                row = 6 * size_x
                ref[row + rc : row + rc + 1] = side[5 * size_y + y : 5 * size_y + y + 1] + total(
                    [own[i * size_y + y : i * size_y + y + 1] for i in range(5)]
                )
                ref[row + g : row + g + 1] = (
                    side[at + h : at + h + 1] + own[at + c : at + c + 1]
                )


def turned(layer, row, layers):
    return pl.ds(layer + row * layers, TILE, stride=layers)


def write_kernel(f_edge, f_middle, bits_ref, xl, xr, speed_ref, out_hbm, flat_ref, speed_hbm, sems, speed_sem):
    size_x, size_y, _ = bits_ref.shape
    held = Layers(f_edge, f_middle, size_x, one_layer(size_x))
    copies = [pltpu.make_async_copy(speed_ref, speed_hbm, speed_sem)]
    copies[0].start()
    for k in range(N):
        for x in range(size_x):
            for y in range(0, size_y, TILE):
                value = held.load(x, y, k)
                for at, side, ks in ((0, xl, RIGHT), (size_x - 1, xr, LEFT)):
                    if x == at and k in ks:
                        row = ks.index(k) * size_y + y
                        value = value + side[row : row + TILE]
                value = jnp.where(fluid_at(bits_ref, x, y), value, 0.0)
                flat_ref[k, turned(x, y, size_x)] = value
        copies.append(pltpu.make_async_copy(flat_ref.at[k], out_hbm.at[k], sems.at[k]))
        copies[-1].start()
    for copy in copies:
        copy.wait()


def end_kernel(out_in, flat_ref, mask_ref, yd, yu, out_hbm, planes, sems):
    del out_in
    layers = planes.shape[1]
    last = flat_ref.shape[1] - layers
    copies = []
    for at, side, ks in ((0, yd, UP), (last, yu, DOWN)):
        for j, k in enumerate(ks):
            i = len(copies)
            entering = side[j * layers : (j + 1) * layers]
            fluid = mask_ref[0, at : at + layers] > 0.5
            planes[i] = jnp.where(fluid, flat_ref[k, at : at + layers] + entering, 0.0)
            target = out_hbm.at[k, pl.ds(at, layers)]
            copies.append(pltpu.make_async_copy(planes.at[i], target, sems.at[i]))
            copies[-1].start()
    for copy in copies:
        copy.wait()


VMEM = pl.BlockSpec(memory_space=pltpu.VMEM)
SMEM = pl.BlockSpec(memory_space=pltpu.SMEM)
HBM = pl.BlockSpec(memory_space=pltpu.HBM)


def call(kernel, outs, args, special=None, special_out=None, scratch=(), cost=None, **kwargs):
    special, special_out = special or {}, special_out or {}
    return pl.pallas_call(
        kernel,
        out_shape=[jax.ShapeDtypeStruct(shape, dtype) for shape, dtype in outs],
        in_specs=[special.get(i, VMEM) for i in range(len(args))],
        out_specs=[special_out.get(i, VMEM) for i in range(len(outs))],
        scratch_shapes=[
            pltpu.VMEM(item, jnp.float32) if isinstance(item, tuple) else item for item in scratch
        ],
        compiler_params=pltpu.CompilerParams(vmem_limit_bytes=16 * 2**20),
        cost_estimate=cost,
        **kwargs,
    )(*args)


def shift(forward, backward, axis):
    count = lax.axis_size(axis)
    ahead = [(i, (i + 1) % count) for i in range(count)]
    return (
        lax.ppermute(forward, axis, ahead),
        lax.ppermute(backward, axis, [(b, a) for a, b in ahead]),
    )


def swap(a, b, axis):
    count = lax.axis_size(axis)
    partners = [
        [(i, (i + (1 if i % 2 == parity else -1)) % count) for i in range(count)]
        for parity in range(2)
    ]
    b = lax.ppermute(b, axis, partners[1])
    return lax.ppermute(a, axis, partners[0]), b


def per_device(populations, fluid_mask, wet_class, wall_potential, relax_rates):
    rows_x, rows_y, size_z = fluid_mask.shape
    pairs = lax.axis_size("gy") % 2 == 0
    exchange = swap if pairs else shift
    size_x, size_y = rows_y, rows_x
    cells = size_x * size_y
    f32, i32 = jnp.float32, jnp.int32
    whole = ((size_x, size_y, size_z), f32)
    rows = lambda count: ((count, size_z), f32)
    fields = lambda count: ((N, count, size_y, size_z), f32)
    flat = lambda count: ((count, cells, size_z), f32)
    padded = (size_x + 2, size_y + PAD, size_z)
    operations = 400 * cells * size_z
    cost = pl.CostEstimate(flops=operations, bytes_accessed=4 * operations // 20, transcendentals=0)

    operands = (
        populations.reshape(N, cells, size_z),
        fluid_mask.reshape(cells, size_z),
        wet_class.reshape(cells, size_z),
        wall_potential,
    )
    row_face = rows(2 * size_x)
    layer_face = rows(2 * size_y + TILE)
    ring_rows = rows(2 * size_x + TILE)
    up, down = call(
        face_kernel,
        [row_face, row_face],
        [pltpu.with_memory_space_constraint(item, pltpu.HBM) for item in operands],
        special={i: HBM for i in range(4)},
        scratch=[
            (2, N, size_x, size_z),
            pltpu.VMEM((2, size_x, size_z), i32),
            pltpu.VMEM((2, size_x, size_z), i32),
            pltpu.SMEM(wall_potential.shape, f32),
            pltpu.SemaphoreType.DMA((7,)),
        ],
    )
    *operands, up = lax.optimization_barrier((*operands, up))
    below, above = shift(up, down, "gx")
    f, rates, flat_mask, mask, pot0 = call(
        turn_kernel,
        [fields(size_x), ((N, TILE, size_z), f32), flat(2), whole, whole],
        (*operands, relax_rates),
        special={3: SMEM, 4: SMEM},
        cost=cost,
    )
    a, b = call(
        functools.partial(start_pack_kernel, pairs),
        [layer_face, layer_face],
        (pot0, mask, below, above),
        scratch=[layer_face[0]] * 2,
    )
    a, b = exchange(a, b, "gy")
    whole_bits = ((size_x, size_y, size_z), i32)
    (bits,) = call(bits_kernel, [whole_bits], (mask, below, above), scratch=[padded], cost=cost)
    bits, x0l, x0r, y0d, y0u = call(
        functools.partial(ring_kernel, pairs),
        [whole_bits, layer_face, layer_face, ring_rows, ring_rows],
        (bits, a, b, below, above),
        scratch=[(2, size_y + PAD, size_z)],
    )
    edge2, edge1 = len(two_layers(size_x)), len(one_layer(size_x))
    held, sent = (f,), ()
    for step in range(STEPS):
        first, last = step == 0, step == STEPS - 1
        parts = 5 if last else 6
        x_rows, y_rows = rows(parts * size_y + TILE), rows(parts * size_x + (0 if last else TILE))
        pot, post, f_edge, right, left, a, b, rest = call(
            functools.partial(edge_kernel, first, last, pairs),
            [
                (padded, f32),
                ((N, edge2, size_y + PAD, size_z), f32),
                fields(edge1),
                x_rows,
                x_rows,
                x_rows,
                x_rows,
                ((3, edge2, size_y, size_z) if last else (edge1, size_y, size_z), f32),
            ],
            (rates, bits, pot0, x0l, x0r, y0d, y0u, *held, *sent),
            cost=cost,
        )
        a, b = exchange(a, b, "gy")
        f_middle, up, down, more = call(
            functools.partial(middle_kernel, first, last),
            [
                fields(size_x - edge1),
                y_rows,
                y_rows,
                flat(3) if last else ((size_x - edge1, size_y, size_z), f32),
            ],
            (rates, bits, pot, post, rest, *held[:2], *sent[2:4]),
            scratch=[(N, size_x - edge2, size_y + PAD, size_z)],
            cost=cost,
        )
        up, down, xl, xr = call(
            functools.partial(pack_kernel, last, pairs, size_x, size_y),
            [y_rows, y_rows, x_rows, x_rows],
            (up, down, a, b, right, left),
        )
        yd, yu = shift(up, down, "gx")
        held = (f_edge, f_middle, rest, more)
        sent = (xl, xr, yd, yu, right, left, up, down)
    out, flat_f, speed = call(
        write_kernel,
        [flat(N), flat(N), flat(3)],
        (f_edge, f_middle, bits, xl, xr, more),
        special_out={0: HBM, 2: HBM},
        scratch=[pltpu.SemaphoreType.DMA((N,)), pltpu.SemaphoreType.DMA(())],
        cost=cost,
    )
    (out,) = call(
        end_kernel,
        [flat(N)],
        (out, flat_f, flat_mask, yd, yu),
        special={0: HBM},
        special_out={0: HBM},
        scratch=[(10, size_x, size_z), pltpu.SemaphoreType.DMA((10,))],
        input_output_aliases={0: 0},
    )
    shape = (rows_x, rows_y, size_z)
    return out.reshape(N, *shape), speed.reshape(3, *shape)


def solution(mesh):
    return jax.shard_map(
        per_device,
        mesh=mesh,
        in_specs=(
            P(None, ("groups", "gx"), "gy", None),
            P(("groups", "gx"), "gy", None),
            P(("groups", "gx"), "gy", None),
            P("groups"),
            P(),
        ),
        out_specs=(P(None, ("groups", "gx"), "gy", None), P(None, ("groups", "gx"), "gy", None)),
        check_vma=False,
    )
```

```python
import functools

import jax
import jax.numpy as jnp
from jax import lax
from jax.experimental import pallas as pl
from jax.experimental.pallas import tpu as pltpu
from jax.sharding import PartitionSpec as P

STEPS = 4
STRENGTH = 2.5
VELOCITY = (
    (0, 0, 0),
    (1, 0, 0),
    (-1, 0, 0),
    (0, 1, 0),
    (0, -1, 0),
    (0, 0, 1),
    (0, 0, -1),
    (1, 1, 0),
    (-1, -1, 0),
    (1, -1, 0),
    (-1, 1, 0),
    (1, 0, 1),
    (-1, 0, -1),
    (1, 0, -1),
    (-1, 0, 1),
    (0, 1, 1),
    (0, -1, -1),
    (0, 1, -1),
    (0, -1, 1),
)
N = len(VELOCITY)
OPPOSITE = [0] + [k + 1 if k % 2 == 1 else k - 1 for k in range(1, N)]
SHIFT = [(y, x, z) for x, y, z in VELOCITY]
RIGHT = [k for k in range(N) if SHIFT[k][0] == 1]
LEFT = [k for k in range(N) if SHIFT[k][0] == -1]
UP = [k for k in range(N) if SHIFT[k][1] == 1]
DOWN = [k for k in range(N) if SHIFT[k][1] == -1]
TILE = 8
PAD = 2 * TILE

C_UP, C_DN, H_UP, H_DN = 0, 1, 2, 3
RC_L, RC_R, G_L, G_R = 0, 1, 2, 3


def roll_z(value, step):
    if step == 0:
        return value
    return pltpu.roll(value, step % value.shape[-1], value.ndim - 1)


def total(values):
    values = list(values)
    while len(values) > 1:
        values = [
            values[i] + values[i + 1] if i + 1 < len(values) else values[i]
            for i in range(0, len(values), 2)
        ]
    return values[0]


def potential_of(density, fluid, solid_value):
    return jnp.where(fluid, 1.0 - jnp.exp(-density), solid_value)


def collide(f, fluid, force, rate):
    fx, fy, fz = force
    s = {k: f[k] + f[k + 1] for k in range(1, N, 2)}
    d = {k: f[k] - f[k + 1] for k in range(1, N, 2)}
    xxyy, xxzz, yyzz = s[7] + s[9], s[11] + s[13], s[15] + s[17]
    xy, xz, yz = s[7] - s[9], s[11] - s[13], s[15] - s[17]
    xyy, yxx = d[7] + d[9], d[7] - d[9]
    xzz, zxx = d[11] + d[13], d[11] - d[13]
    yzz, zyy = d[15] + d[17], d[15] - d[17]
    jx, jy, jz = d[1] + (xyy + xzz), d[3] + (yxx + yzz), d[5] + (zxx + zyy)
    xx, yy, zz = s[1] + (xxyy + xxzz), s[3] + (xxyy + yyzz), s[5] + (xxzz + yyzz)
    rho = (f[0] + s[1]) + (s[3] + s[5]) + (xxyy + (xxzz + yyzz))
    safe = jnp.where(fluid, rho, 1.0)
    inverse = 1.0 / safe
    hx, hy, hz = 0.5 * fx, 0.5 * fy, 0.5 * fz
    gx, gy, gz = jx + hx, jy + hy, jz + hz
    ux, uy, uz = gx * inverse, gy * inverse, gz * inverse
    third = safe * (1.0 / 3.0)
    ninth = safe * (1.0 / 9.0)
    px, py, pz = gx - fx, gy - fy, gz - fz
    txx, tyy, tzz = ux * px, uy * py, uz * pz
    sx, sy, sz = ux * fx, uy * fy, uz * fz
    pxy = ux * fy + uy * fx
    pxz = ux * fz + uz * fx
    pyz = uy * fz + uz * fy
    t3, s3 = (txx + tyy + tzz) * (1.0 / 3.0), (sx + sy + sz) * (2.0 / 3.0)
    rho = rho - rate(0) * (rho - safe)
    nx = jx + fx - rate(1) * (jx - safe * ux + hx)
    ny = jy + fy - rate(2) * (jy - safe * uy + hy)
    nz = jz + fz - rate(3) * (jz - safe * uz + hz)
    xy = xy + rate(4) * (gx * uy - 0.5 * pxy - xy) + pxy
    xz = xz + rate(5) * (gx * uz - 0.5 * pxz - xz) + pxz
    yz = yz + rate(6) * (gy * uz - 0.5 * pyz - yz) + pyz
    xx = xx + rate(7) * (third + txx - xx) + 2.0 * sx
    yy = yy + rate(8) * (third + tyy - yy) + 2.0 * sy
    zz = zz + rate(9) * (third + tzz - zz) + 2.0 * sz
    ex, ey, ez = jx * (1.0 / 3.0), jy * (1.0 / 3.0), jz * (1.0 / 3.0)
    qx, qy, qz = fx * (1.0 / 3.0), fy * (1.0 / 3.0), fz * (1.0 / 3.0)
    xyy = xyy + rate(10) * (ex - xyy) + qx
    xzz = xzz + rate(11) * (ex - xzz) + qx
    yxx = yxx + rate(12) * (ey - yxx) + qy
    yzz = yzz + rate(13) * (ey - yzz) + qy
    zxx = zxx + rate(14) * (ez - zxx) + qz
    zyy = zyy + rate(15) * (ez - zyy) + qz
    base = ninth + t3
    xxyy = xxyy + rate(16) * (base - 0.5 * tzz - xxyy) + (s3 - sz)
    xxzz = xxzz + rate(17) * (base - 0.5 * tyy - xxzz) + (s3 - sy)
    yyzz = yyzz + rate(18) * (base - 0.5 * txx - yyzz) + (s3 - sx)
    out = [None] * N
    for first, even, cross, odd1, odd2 in (
        (7, xxyy, xy, xyy, yxx),
        (11, xxzz, xz, xzz, zxx),
        (15, yyzz, yz, yzz, zyy),
    ):
        even, cross, odd1, odd2 = 0.25 * even, 0.25 * cross, 0.25 * odd1, 0.25 * odd2
        plus, minus = even + cross, even - cross
        both, diff = odd1 + odd2, odd1 - odd2
        out[first], out[first + 1] = plus + both, plus - both
        out[first + 2], out[first + 3] = minus + diff, minus - diff
    pairs = []
    for first, even, odd in (
        (1, xx - (xxyy + xxzz), nx - (xyy + xzz)),
        (3, yy - (xxyy + yyzz), ny - (yxx + yzz)),
        (5, zz - (xxzz + yyzz), nz - (zxx + zyy)),
    ):
        half_even, half_odd = 0.5 * even, 0.5 * odd
        out[first], out[first + 1] = half_even + half_odd, half_even - half_odd
        pairs.append(even)
    out[0] = rho - (pairs[0] + pairs[1] + pairs[2]) - (xxyy + xxzz + yyzz)
    return out, (ux, uy, uz)


def corner_pops(side):
    return SHIFT.index((side, 1, 0)), SHIFT.index((side, -1, 0))


def in_swap_order(pairs, right, left):
    if not pairs:
        return right, left
    odd = lax.axis_index("gy") % 2 == 1
    return jnp.where(odd, left, right), jnp.where(odd, right, left)


def sort_received(pairs, a_ref, b_ref, xl_ref, xr_ref):
    if pairs:
        xr_ref[...], xl_ref[...] = in_swap_order(pairs, a_ref[...], b_ref[...])
    else:
        xl_ref[...], xr_ref[...] = a_ref[...], b_ref[...]


def wall_of(wet, wall_ref):
    wall = jnp.zeros(wet.shape, jnp.float32)
    for c in range(wall_ref.shape[0]):
        wall = jnp.where(wet == c, wall_ref[c], wall)
    return wall


def face_kernel(f_hbm, mask_hbm, wet_hbm, wall_hbm, up_ref, down_ref, *scratch):
    row_in, mask_in, wet_in, wall_in, sems = scratch
    layers = row_in.shape[2]
    sides = ((0, down_ref, 0), (1, up_ref, f_hbm.shape[1] - layers))
    copies = [pltpu.make_async_copy(wall_hbm, wall_in, sems.at[0])]
    for s, _, at in sides:
        for i, (source, target) in enumerate(((mask_hbm, mask_in), (wet_hbm, wet_in))):
            sem = sems.at[1 + 2 * s + i]
            copies.append(
                pltpu.make_async_copy(source.at[pl.ds(at, layers)], target.at[s], sem)
            )
        sem = sems.at[5 + s]
        copies.append(
            pltpu.make_async_copy(f_hbm.at[:, pl.ds(at, layers)], row_in.at[s], sem)
        )
    for copy in copies:
        copy.start()
    for copy in copies:
        copy.wait()
    for s, ref, _ in sides:
        pore = mask_in[s] == 1
        density = total([row_in[s, k] for k in range(N)])
        ref[:layers] = potential_of(density, pore, wall_of(wet_in[s], wall_in))
        ref[layers:] = jnp.where(pore, 1.0, 0.0)


def turn_kernel(f_hbm, mask_hbm, wet_hbm, wall_hbm, rate_hbm, after_ref, *refs):
    del after_ref
    f_ref, rates_ref, flat_ref, mask_ref, pot_ref = refs[:5]
    raw, mask_in, wet_in, wall_in, rate_in, f_sems, sems = refs[5:]
    layers, rows = f_ref.shape[1], f_ref.shape[2]
    small = [
        pltpu.make_async_copy(source, target, sems.at[i])
        for i, (source, target) in enumerate(
            (
                (wall_hbm, wall_in),
                (rate_hbm, rate_in),
                (mask_hbm, mask_in),
                (wet_hbm, wet_in),
            )
        )
    ]
    large = [pltpu.make_async_copy(f_hbm.at[k], raw.at[k], f_sems.at[k]) for k in range(N)]
    for copy in small + large:
        copy.start()
    for copy in small:
        copy.wait()
    for k in range(N):
        rates_ref[k] = jnp.full(rates_ref.shape[1:], rate_in[k], jnp.float32)
    blocks = [slice(i, i + TILE) for i in range(0, layers * rows, TILE)]
    for at in blocks:
        flat_ref[0, at] = jnp.where(mask_in[at] == 1, 1.0, 0.0)
        flat_ref[1, at] = wall_of(wet_in[at], wall_in)
    density = None
    for k, copy in enumerate(large):
        copy.wait()
        for i in range(layers):
            f_ref[k, i] = raw[k, pl.ds(i, rows, stride=layers)]
        here = [raw[k, at] for at in blocks]
        density = here if density is None else [a + b for a, b in zip(density, here)]
    for at, value in zip(blocks, density):
        flat_ref[1, at] = potential_of(value, flat_ref[0, at] > 0.5, flat_ref[1, at])
    for i in range(layers):
        mask_ref[i] = flat_ref[0, pl.ds(i, rows, stride=layers)]
        pot_ref[i] = flat_ref[1, pl.ds(i, rows, stride=layers)]


def start_pack_kernel(pairs, pot_ref, mask_ref, from_below, from_above, a_ref, b_ref, left_ref, right_ref):
    layers, rows = mask_ref.shape[0], mask_ref.shape[1]
    for ref, layer in ((left_ref, 0), (right_ref, layers - 1)):
        ref[:rows] = pot_ref[layer]
        ref[rows : 2 * rows] = mask_ref[layer]
        ref[2 * rows :] = jnp.zeros((TILE, ref.shape[1]), jnp.float32)
        for i, side in enumerate((from_below, from_above)):
            row = 2 * rows + i
            ref[row : row + 1] = side[layer : layer + 1]
            ref[row + 2 : row + 3] = side[layers + layer : layers + layer + 1]
    a_ref[...], b_ref[...] = in_swap_order(pairs, right_ref[...], left_ref[...])


def bits_kernel(mask_ref, from_below, from_above, bits_ref, pad_ref):
    size_x, size_y, size_z = mask_ref.shape
    nothing = jnp.zeros((TILE, size_z), jnp.float32)
    for x in (0, size_x + 1):
        for y in range(0, size_y + PAD, TILE):
            pad_ref[x, y : y + TILE] = nothing
    for x in range(size_x):
        pad_ref[1 + x, TILE : TILE + size_y] = mask_ref[x]
        for y, side in ((TILE - 1, from_below), (TILE + size_y, from_above)):
            pad_ref[1 + x, y : y + 1] = side[size_x + x : size_x + x + 1]
    for x in range(size_x):
        for y in range(0, size_y, TILE):
            bits = jnp.zeros((TILE, size_z), jnp.int32)
            for k in range(N):
                ex, ey, ez = SHIFT[k]
                row = TILE + y - ey
                source = roll_z(pad_ref[1 + x - ex, row : row + TILE], ez)
                bits = bits | jnp.where(source > 0.5, 1 << k, 0)
            bits_ref[x, y : y + TILE] = bits


def ring_kernel(pairs, bits_in, a_ref, b_ref, from_below, from_above, bits_ref, xl, xr, yd, yu, pad_ref):
    size_x, size_y, _ = bits_ref.shape
    sort_received(pairs, a_ref, b_ref, xl, xr)
    corner = 2 * size_y
    for i, (ref, side) in enumerate(((yd, from_below), (yu, from_above))):
        ref[: 2 * size_x] = side[...]
        ref[2 * size_x :] = jnp.zeros((TILE, ref.shape[1]), jnp.float32)
        for j, layer in enumerate((xl, xr)):
            row = 2 * size_x + j
            ref[row : row + 1] = layer[corner + i : corner + i + 1]
            ref[row + 2 : row + 3] = layer[corner + 2 + i : corner + 3 + i]
    bits_ref[...] = bits_in[...]
    for i, (side, ks, x) in enumerate(((xl, RIGHT, 0), (xr, LEFT, size_x - 1))):
        pad_ref[i, TILE : TILE + size_y] = side[size_y : 2 * size_y]
        for row, at in ((TILE - 1, corner + 2), (TILE + size_y, corner + 3)):
            pad_ref[i, row : row + 1] = side[at : at + 1]
        for y in range(0, size_y, TILE):
            bits = bits_in[x, y : y + TILE]
            for k in ks:
                _, ey, ez = SHIFT[k]
                row = TILE + y - ey
                source = roll_z(pad_ref[i, row : row + TILE], ez)
                bits = bits | jnp.where(source > 0.5, 1 << k, 0)
            bits_ref[x, y : y + TILE] = bits


class Layers:
    def __init__(self, edge_ref, middle_ref, size_x, edge):
        self.where = {}
        middle = [x for x in range(size_x) if x not in edge]
        for ref, xs in ((edge_ref, edge), (middle_ref, middle)):
            for i, x in enumerate(xs):
                self.where[x] = (ref, i)

    def load(self, x, y, k=None):
        ref, i = self.where[x]
        return ref[i, y : y + TILE] if k is None else ref[k, i, y : y + TILE]

    def row(self, x, y, k=None):
        ref, i = self.where[x]
        return ref[i, y : y + 1] if k is None else ref[k, i, y : y + 1]

    def store(self, x, y, value, k=None):
        ref, i = self.where[x]
        if k is None:
            ref[i, y : y + TILE] = value
        else:
            ref[k, i, y : y + TILE] = value


def two_layers(size_x):
    return [0, 1, size_x - 2, size_x - 1]


def one_layer(size_x):
    return [0, size_x - 1]


def fluid_at(bits_ref, x, y):
    return (bits_ref[x, y : y + TILE] & 1) != 0


def clear_outside(post, layers, size_y):
    nothing = jnp.zeros((TILE, post.shape[-1]), jnp.float32)
    for i in range(layers):
        for k in UP:
            post[k, i, :TILE] = nothing
        for k in DOWN:
            post[k, i, TILE + size_y :] = nothing


def collide_layers(xs, rates, f, bits_ref, pot, sides, post, speed):
    size_x, size_y, size_z = bits_ref.shape
    row_of = lax.broadcasted_iota(jnp.int32, (TILE, size_z), 0)
    for x in xs:
        for y in range(0, size_y, TILE):
            near = {
                (i, j): pot[1 + x + i, TILE + y + j : 2 * TILE + y + j]
                for i in (-1, 0, 1)
                for j in (-1, 0, 1)
            }
            scale = near[0, 0] * (STRENGTH / 36.0)
            dx = near[1, 0] - near[-1, 0]
            dy = near[0, 1] - near[0, -1]
            pp, pm, mp, mm = near[1, 1], near[1, -1], near[-1, 1], near[-1, -1]
            both = near[1, 0] + near[-1, 0] + near[0, 1] + near[0, -1] + 2.0 * near[0, 0]
            diag1, diag2 = pp - mm, pm - mp
            force = (
                scale * (2.0 * dy + (diag1 - diag2) + (roll_z(dy, 1) + roll_z(dy, -1))),
                scale * (2.0 * dx + (diag1 + diag2) + (roll_z(dx, 1) + roll_z(dx, -1))),
                scale * (roll_z(both, -1) - roll_z(both, 1)),
            )
            now = [f(k, x, y) for k in range(N)]
            if sides is not None:
                xl, xr, yd, yu = sides
                for at, side, ks in ((0, xl, RIGHT), (size_x - 1, xr, LEFT)):
                    if x == at:
                        for j, k in enumerate(ks):
                            now[k] = now[k] + side[j * size_y + y : j * size_y + y + TILE]
                for at, side, ks in ((0, yd, UP), (size_y - 1, yu, DOWN)):
                    if y <= at < y + TILE:
                        for j, k in enumerate(ks):
                            entering = side[j * size_x + x : j * size_x + x + 1]
                            now[k] = now[k] + jnp.where(row_of == at - y, entering, 0.0)
            fluid = fluid_at(bits_ref, x, y)
            after, at_speed = collide(now, fluid, force, lambda r: rates[r])
            for k in range(N):
                post.store(x, TILE + y, jnp.where(fluid, after[k], 0.0), k)
            if speed is not None:
                for c in range(3):
                    speed.store(x, y, jnp.where(fluid, at_speed[c], 0.0), c)


def stream_layers(xs, bits_ref, post, f, rho):
    size_x, size_y, _ = bits_ref.shape
    for x in xs:
        for y in range(0, size_y, TILE):
            bits = bits_ref[x, y : y + TILE]
            arrived = []
            for k in range(N):
                ex, ey, ez = SHIFT[k]
                value = post.load(x, TILE + y, OPPOSITE[k])
                if k > 0:
                    come = 0.0
                    if 0 <= x - ex < size_x:
                        come = roll_z(post.load(x - ex, TILE + y - ey, k), ez)
                    value = jnp.where((bits & (1 << k)) != 0, come, value)
                f.store(x, y, value, k)
                arrived.append(value)
            if rho is not None:
                rho.store(x, y, total(arrived))


def edge_kernel(first, last, pairs, *refs):
    refs = list(refs)
    take = lambda count: [refs.pop(0) for _ in range(count)]
    rates, bits_ref, pot0_ref, x0l, x0r, y0d, y0u = take(7)
    if first:
        f_ref = take(1)[0]
    else:
        f_edge, f_middle, rho_edge, rho_middle, xl, xr, yd, yu = take(8)
        own_right, own_left, own_up, own_down = take(4)
    pot, post_out, f_out, right_ref, left_ref, a_ref, b_ref, rest = take(8)
    size_x, size_y, size_z = bits_ref.shape
    edge2, edge1 = two_layers(size_x), one_layer(size_x)
    sides = None
    if first:
        f = lambda k, x, y: f_ref[k, x, y : y + TILE]
    else:
        sides = (xl, xr, yd, yu)
        held = Layers(f_edge, f_middle, size_x, edge1)
        density_of = Layers(rho_edge, rho_middle, size_x, edge1)
        f = lambda k, x, y: held.load(x, y, k)
    clear_outside(post_out, len(edge2), size_y)

    if first:
        for x in range(size_x):
            pot[1 + x, TILE : TILE + size_y] = pot0_ref[x]
        for x, side in ((0, x0l), (1 + size_x, x0r)):
            pot[x, TILE : TILE + size_y] = side[:size_y]
        for y, side in ((TILE - 1, y0d), (TILE + size_y, y0u)):
            for x in range(size_x):
                pot[1 + x, y : y + 1] = side[x : x + 1]
            for x, row in ((0, 2 * size_x), (1 + size_x, 2 * size_x + 1)):
                pot[x, y : y + 1] = side[row : row + 1]
    else:
        end = 6 * size_x
        row_of = lax.broadcasted_iota(jnp.int32, (TILE, size_z), 0)
        entering = {
            at: total([side[j * size_x : (j + 1) * size_x] for j in range(5)])
            for at, side in ((0, yd), (size_y - 1, yu))
        }
        for x in range(size_x):
            for y in range(0, size_y, TILE):
                density = density_of.load(x, y)
                for at, side in ((0, xl), (size_x - 1, xr)):
                    if x == at:
                        density = density + total(
                            [side[j * size_y + y : j * size_y + y + TILE] for j in range(5)]
                        )
                for at, rows in entering.items():
                    if y <= at < y + TILE:
                        density = density + jnp.where(row_of == at - y, rows[x : x + 1], 0.0)
                pot[1 + x, TILE + y : 2 * TILE + y] = potential_of(
                    density, fluid_at(bits_ref, x, y), pot0_ref[x, y : y + TILE]
                )
        for x, side, own, side0, g in (
            (0, xl, own_left, x0l, G_L),
            (1 + size_x, xr, own_right, x0r, G_R),
        ):
            for y in range(0, size_y, TILE):
                density = side[5 * size_y + y : 5 * size_y + y + TILE] + total(
                    [own[j * size_y + y : j * size_y + y + TILE] for j in range(5)]
                )
                for at, row in ((0, yd), (size_y - 1, yu)):
                    if y <= at < y + TILE:
                        more = row[end + g : end + g + 1]
                        density = density + jnp.where(row_of == at - y, more, 0.0)
                pot[x, TILE + y : 2 * TILE + y] = potential_of(
                    density,
                    side0[size_y + y : size_y + y + TILE] > 0.5,
                    side0[y : y + TILE],
                )
        for y, side, own, side0 in (
            (TILE - 1, yd, own_down, y0d),
            (TILE + size_y, yu, own_up, y0u),
        ):
            density = side[5 * size_x : 6 * size_x] + total(
                [own[j * size_x : (j + 1) * size_x] for j in range(5)]
            )
            value = potential_of(density, side0[size_x : 2 * size_x] > 0.5, side0[:size_x])
            for x in range(size_x):
                pot[1 + x, y : y + 1] = value[x : x + 1]
            for x, rc, g, i in ((0, RC_L, G_L, 0), (1 + size_x, RC_R, G_R, 1)):
                density = side[end + rc : end + rc + 1] + own[end + g : end + g + 1]
                row = 2 * size_x + i
                pot[x, y : y + 1] = potential_of(
                    density, side0[row + 2 : row + 3] > 0.5, side0[row : row + 1]
                )

    post = Layers(post_out, None, size_x, edge2)
    speed = Layers(rest, None, size_x, edge2) if last else None
    collide_layers(edge2, rates, f, bits_ref, pot, sides, post, speed)
    rho = None if last else Layers(rest, None, size_x, edge1)
    stream_layers(edge1, bits_ref, post, Layers(f_out, None, size_x, edge1), rho)

    at = (5 if last else 6) * size_y
    for i, (ref, x, ks, dirs) in enumerate(
        ((left_ref, 0, LEFT, corner_pops(-1)), (right_ref, size_x - 1, RIGHT, corner_pops(1)))
    ):
        for j, k in enumerate(ks):
            _, ey, ez = SHIFT[k]
            for y in range(0, size_y, TILE):
                row = j * size_y + y
                ref[row : row + TILE] = roll_z(post.load(x, TILE + y - ey, k), ez)
        ref[at : at + TILE] = jnp.zeros((TILE, size_z), jnp.float32)
        ref[at + C_UP : at + C_UP + 1] = post.row(x, TILE + size_y - 1, dirs[0])
        ref[at + C_DN : at + C_DN + 1] = post.row(x, TILE, dirs[1])
        if not last:
            ref[5 * size_y : 6 * size_y] = rest[i]
            for h, y, leave in ((H_UP, size_y - 1, UP), (H_DN, 0, DOWN)):
                ref[at + h : at + h + 1] = total(
                    [
                        roll_z(post.row(x - SHIFT[k][0], TILE + y, k), SHIFT[k][2])
                        for k in leave
                        if 0 <= x - SHIFT[k][0] < size_x
                    ]
                )
    a_ref[...], b_ref[...] = in_swap_order(pairs, right_ref[...], left_ref[...])


def middle_kernel(first, last, *refs):
    refs = list(refs)
    take = lambda count: [refs.pop(0) for _ in range(count)]
    rates, bits_ref, pot, post_edge, edge_rest = take(5)
    if first:
        f_ref = take(1)[0]
    else:
        f_edge, f_middle, yd, yu = take(4)
    f_out, up_ref, down_ref, rest = take(4)
    post_middle = take(1)[0]
    size_x, size_y, size_z = bits_ref.shape
    edge2, edge1 = two_layers(size_x), one_layer(size_x)
    sides = None
    if first:
        f = lambda k, x, y: f_ref[k, x, y : y + TILE]
    else:
        sides = (None, None, yd, yu)
        held = Layers(f_edge, f_middle, size_x, edge1)
        f = lambda k, x, y: held.load(x, y, k)
    clear_outside(post_middle, size_x - len(edge2), size_y)
    post = Layers(post_edge, post_middle, size_x, edge2)
    speed = None
    if last:
        speed = Layers(None, None, size_x, [])
        speed.store = lambda x, y, value, c: rest.__setitem__((c, turned(x, y, size_x)), value)
        for c in range(3):
            for i, x in enumerate(edge2):
                for y in range(0, size_y, TILE):
                    rest[c, turned(x, y, size_x)] = edge_rest[c, i, y : y + TILE]
    inner = [x for x in range(size_x) if x not in edge2]
    collide_layers(inner, rates, f, bits_ref, pot, sides, post, speed)
    rho = None if last else Layers(edge_rest, rest, size_x, edge1)
    inner = [x for x in range(size_x) if x not in edge1]
    stream_layers(inner, bits_ref, post, Layers(None, f_out, size_x, edge1), rho)
    for ref, y, ks in ((up_ref, size_y - 1, UP), (down_ref, 0, DOWN)):
        for j, k in enumerate(ks):
            ex, _, ez = SHIFT[k]
            for x in range(size_x):
                row = j * size_x + x
                if 0 <= x - ex < size_x:
                    ref[row : row + 1] = post.row(x - ex, TILE + y, k)
                else:
                    ref[row : row + 1] = jnp.zeros((1, size_z), jnp.float32)
            if ez != 0:
                rows = slice(j * size_x, (j + 1) * size_x)
                ref[rows] = roll_z(ref[rows], ez)
        if not last:
            for x in range(size_x):
                ref[5 * size_x + x : 5 * size_x + x + 1] = rho.row(x, y)


def pack_kernel(last, pairs, size_x, size_y, *refs):
    up_in, down_in, a_ref, b_ref, own_right, own_left, up_ref, down_ref, xl, xr = refs
    sort_received(pairs, a_ref, b_ref, xl, xr)
    parts = 5 if last else 6
    at = parts * size_y
    for ref, source, y, ks, c, h in (
        (up_ref, up_in, size_y - 1, UP, C_UP, H_UP),
        (down_ref, down_in, 0, DOWN, C_DN, H_DN),
    ):
        ref[...] = jnp.zeros(ref.shape, jnp.float32)
        ref[: parts * size_x] = source[: parts * size_x]
        for side, own, x, ex, rc, g in (
            (xl, own_left, 0, 1, RC_L, G_L),
            (xr, own_right, size_x - 1, -1, RC_R, G_R),
        ):
            j = [i for i, k in enumerate(ks) if SHIFT[k][0] == ex][0]
            row = j * size_x + x
            ref[row : row + 1] = side[at + c : at + c + 1]
            if not last:
                row = 5 * size_x + x
                ref[row : row + 1] = source[row : row + 1] + total(
                    [side[i * size_y + y : i * size_y + y + 1] for i in range(5)]
                )
                row = 6 * size_x
                ref[row + rc : row + rc + 1] = side[5 * size_y + y : 5 * size_y + y + 1] + total(
                    [own[i * size_y + y : i * size_y + y + 1] for i in range(5)]
                )
                ref[row + g : row + g + 1] = (
                    side[at + h : at + h + 1] + own[at + c : at + c + 1]
                )


def turned(layer, row, layers):
    return pl.ds(layer + row * layers, TILE, stride=layers)


def write_kernel(f_edge, f_middle, bits_ref, xl, xr, speed_ref, out_hbm, flat_ref, speed_hbm, sems, speed_sem):
    size_x, size_y, _ = bits_ref.shape
    held = Layers(f_edge, f_middle, size_x, one_layer(size_x))
    copies = [pltpu.make_async_copy(speed_ref, speed_hbm, speed_sem)]
    copies[0].start()
    for k in range(N):
        for x in range(size_x):
            for y in range(0, size_y, TILE):
                value = held.load(x, y, k)
                for at, side, ks in ((0, xl, RIGHT), (size_x - 1, xr, LEFT)):
                    if x == at and k in ks:
                        row = ks.index(k) * size_y + y
                        value = value + side[row : row + TILE]
                value = jnp.where(fluid_at(bits_ref, x, y), value, 0.0)
                flat_ref[k, turned(x, y, size_x)] = value
        copies.append(pltpu.make_async_copy(flat_ref.at[k], out_hbm.at[k], sems.at[k]))
        copies[-1].start()
    for copy in copies:
        copy.wait()


def end_kernel(out_in, flat_ref, mask_ref, yd, yu, out_hbm, planes, sems):
    del out_in
    layers = planes.shape[1]
    last = flat_ref.shape[1] - layers
    copies = []
    for at, side, ks in ((0, yd, UP), (last, yu, DOWN)):
        for j, k in enumerate(ks):
            i = len(copies)
            entering = side[j * layers : (j + 1) * layers]
            fluid = mask_ref[0, at : at + layers] > 0.5
            planes[i] = jnp.where(fluid, flat_ref[k, at : at + layers] + entering, 0.0)
            target = out_hbm.at[k, pl.ds(at, layers)]
            copies.append(pltpu.make_async_copy(planes.at[i], target, sems.at[i]))
            copies[-1].start()
    for copy in copies:
        copy.wait()


VMEM = pl.BlockSpec(memory_space=pltpu.VMEM)
HBM = pl.BlockSpec(memory_space=pltpu.HBM)


def call(kernel, outs, args, special=None, special_out=None, scratch=(), cost=None, **kwargs):
    special, special_out = special or {}, special_out or {}
    return pl.pallas_call(
        kernel,
        out_shape=[jax.ShapeDtypeStruct(shape, dtype) for shape, dtype in outs],
        in_specs=[special.get(i, VMEM) for i in range(len(args))],
        out_specs=[special_out.get(i, VMEM) for i in range(len(outs))],
        scratch_shapes=[
            pltpu.VMEM(item, jnp.float32) if isinstance(item, tuple) else item for item in scratch
        ],
        compiler_params=pltpu.CompilerParams(vmem_limit_bytes=16 * 2**20),
        cost_estimate=cost,
        **kwargs,
    )(*args)


def shift(forward, backward, axis):
    count = lax.axis_size(axis)
    ahead = [(i, (i + 1) % count) for i in range(count)]
    return (
        lax.ppermute(forward, axis, ahead),
        lax.ppermute(backward, axis, [(b, a) for a, b in ahead]),
    )


def swap(a, b, axis):
    count = lax.axis_size(axis)
    partners = [
        [(i, (i + (1 if i % 2 == parity else -1)) % count) for i in range(count)]
        for parity in range(2)
    ]
    b = lax.ppermute(b, axis, partners[1])
    return lax.ppermute(a, axis, partners[0]), b


def per_device(populations, fluid_mask, wet_class, wall_potential, relax_rates):
    rows_x, rows_y, size_z = fluid_mask.shape
    pairs = lax.axis_size("gy") % 2 == 0
    exchange = swap if pairs else shift
    size_x, size_y = rows_y, rows_x
    cells = size_x * size_y
    f32, i32 = jnp.float32, jnp.int32
    whole = ((size_x, size_y, size_z), f32)
    rows = lambda count: ((count, size_z), f32)
    fields = lambda count: ((N, count, size_y, size_z), f32)
    flat = lambda count: ((count, cells, size_z), f32)
    padded = (size_x + 2, size_y + PAD, size_z)
    operations = 400 * cells * size_z
    cost = pl.CostEstimate(flops=operations, bytes_accessed=4 * operations // 20, transcendentals=0)

    operands = [
        pltpu.with_memory_space_constraint(item, pltpu.HBM)
        for item in (
            populations.reshape(N, cells, size_z),
            fluid_mask.reshape(cells, size_z),
            wet_class.reshape(cells, size_z),
            wall_potential,
            relax_rates,
        )
    ]
    row_face = rows(2 * size_x)
    layer_face = rows(2 * size_y + TILE)
    ring_rows = rows(2 * size_x + TILE)
    up, down = call(
        face_kernel,
        [row_face, row_face],
        operands[:4],
        special={i: HBM for i in range(4)},
        scratch=[
            (2, N, size_x, size_z),
            pltpu.VMEM((2, size_x, size_z), i32),
            pltpu.VMEM((2, size_x, size_z), i32),
            pltpu.SMEM(wall_potential.shape, f32),
            pltpu.SemaphoreType.DMA((7,)),
        ],
    )
    below, above = shift(up, down, "gx")
    f, rates, flat_mask, mask, pot0 = call(
        turn_kernel,
        [fields(size_x), ((N, TILE, size_z), f32), flat(2), whole, whole],
        (*operands, up),
        special={i: HBM for i in range(5)},
        scratch=[
            flat(N)[0],
            pltpu.VMEM((cells, size_z), i32),
            pltpu.VMEM((cells, size_z), i32),
            pltpu.SMEM(wall_potential.shape, f32),
            pltpu.SMEM(relax_rates.shape, f32),
            pltpu.SemaphoreType.DMA((N,)),
            pltpu.SemaphoreType.DMA((4,)),
        ],
        cost=cost,
    )
    a, b = call(
        functools.partial(start_pack_kernel, pairs),
        [layer_face, layer_face],
        (pot0, mask, below, above),
        scratch=[layer_face[0]] * 2,
    )
    a, b = exchange(a, b, "gy")
    whole_bits = ((size_x, size_y, size_z), i32)
    (bits,) = call(bits_kernel, [whole_bits], (mask, below, above), scratch=[padded], cost=cost)
    bits, x0l, x0r, y0d, y0u = call(
        functools.partial(ring_kernel, pairs),
        [whole_bits, layer_face, layer_face, ring_rows, ring_rows],
        (bits, a, b, below, above),
        scratch=[(2, size_y + PAD, size_z)],
    )
    edge2, edge1 = len(two_layers(size_x)), len(one_layer(size_x))
    held, sent = (f,), ()
    for step in range(STEPS):
        first, last = step == 0, step == STEPS - 1
        parts = 5 if last else 6
        x_rows, y_rows = rows(parts * size_y + TILE), rows(parts * size_x + (0 if last else TILE))
        pot, post, f_edge, right, left, a, b, rest = call(
            functools.partial(edge_kernel, first, last, pairs),
            [
                (padded, f32),
                ((N, edge2, size_y + PAD, size_z), f32),
                fields(edge1),
                x_rows,
                x_rows,
                x_rows,
                x_rows,
                ((3, edge2, size_y, size_z) if last else (edge1, size_y, size_z), f32),
            ],
            (rates, bits, pot0, x0l, x0r, y0d, y0u, *held, *sent),
            cost=cost,
        )
        a, b = exchange(a, b, "gy")
        f_middle, up, down, more = call(
            functools.partial(middle_kernel, first, last),
            [
                fields(size_x - edge1),
                y_rows,
                y_rows,
                flat(3) if last else ((size_x - edge1, size_y, size_z), f32),
            ],
            (rates, bits, pot, post, rest, *held[:2], *sent[2:4]),
            scratch=[(N, size_x - edge2, size_y + PAD, size_z)],
            cost=cost,
        )
        up, down, xl, xr = call(
            functools.partial(pack_kernel, last, pairs, size_x, size_y),
            [y_rows, y_rows, x_rows, x_rows],
            (up, down, a, b, right, left),
        )
        yd, yu = shift(up, down, "gx")
        held = (f_edge, f_middle, rest, more)
        sent = (xl, xr, yd, yu, right, left, up, down)
    out, flat_f, speed = call(
        write_kernel,
        [flat(N), flat(N), flat(3)],
        (f_edge, f_middle, bits, xl, xr, more),
        special_out={0: HBM, 2: HBM},
        scratch=[pltpu.SemaphoreType.DMA((N,)), pltpu.SemaphoreType.DMA(())],
        cost=cost,
    )
    (out,) = call(
        end_kernel,
        [flat(N)],
        (out, flat_f, flat_mask, yd, yu),
        special={0: HBM},
        special_out={0: HBM},
        scratch=[(10, size_x, size_z), pltpu.SemaphoreType.DMA((10,))],
        input_output_aliases={0: 0},
    )
    shape = (rows_x, rows_y, size_z)
    return out.reshape(N, *shape), speed.reshape(3, *shape)


def solution(mesh):
    return jax.shard_map(
        per_device,
        mesh=mesh,
        in_specs=(
            P(None, ("groups", "gx"), "gy", None),
            P(("groups", "gx"), "gy", None),
            P(("groups", "gx"), "gy", None),
            P("groups"),
            P(),
        ),
        out_specs=(P(None, ("groups", "gx"), "gy", None), P(None, ("groups", "gx"), "gy", None)),
        check_vma=False,
    )
```

```python
import functools

import jax
import jax.numpy as jnp
from jax import lax
from jax.experimental import pallas as pl
from jax.experimental.pallas import tpu as pltpu
from jax.sharding import PartitionSpec as P

STEPS = 4
STRENGTH = 2.5
VELOCITY = (
    (0, 0, 0),
    (1, 0, 0),
    (-1, 0, 0),
    (0, 1, 0),
    (0, -1, 0),
    (0, 0, 1),
    (0, 0, -1),
    (1, 1, 0),
    (-1, -1, 0),
    (1, -1, 0),
    (-1, 1, 0),
    (1, 0, 1),
    (-1, 0, -1),
    (1, 0, -1),
    (-1, 0, 1),
    (0, 1, 1),
    (0, -1, -1),
    (0, 1, -1),
    (0, -1, 1),
)
N = len(VELOCITY)
OPPOSITE = [0] + [k + 1 if k % 2 == 1 else k - 1 for k in range(1, N)]
SHIFT = [(y, x, z) for x, y, z in VELOCITY]
RIGHT = [k for k in range(N) if SHIFT[k][0] == 1]
LEFT = [k for k in range(N) if SHIFT[k][0] == -1]
UP = [k for k in range(N) if SHIFT[k][1] == 1]
DOWN = [k for k in range(N) if SHIFT[k][1] == -1]
TILE = 8
PAD = 2 * TILE

C_UP, C_DN, H_UP, H_DN = 0, 1, 2, 3
RC_L, RC_R, G_L, G_R = 0, 1, 2, 3


def roll_z(value, step):
    if step == 0:
        return value
    return pltpu.roll(value, step % value.shape[-1], value.ndim - 1)


def total(values):
    values = list(values)
    while len(values) > 1:
        values = [
            values[i] + values[i + 1] if i + 1 < len(values) else values[i]
            for i in range(0, len(values), 2)
        ]
    return values[0]


def potential_of(density, fluid, solid_value):
    return jnp.where(fluid, 1.0 - jnp.exp(-density), solid_value)


def collide(f, fluid, force, rate):
    fx, fy, fz = force
    s = {k: f[k] + f[k + 1] for k in range(1, N, 2)}
    d = {k: f[k] - f[k + 1] for k in range(1, N, 2)}
    xxyy, xxzz, yyzz = s[7] + s[9], s[11] + s[13], s[15] + s[17]
    xy, xz, yz = s[7] - s[9], s[11] - s[13], s[15] - s[17]
    xyy, yxx = d[7] + d[9], d[7] - d[9]
    xzz, zxx = d[11] + d[13], d[11] - d[13]
    yzz, zyy = d[15] + d[17], d[15] - d[17]
    jx, jy, jz = d[1] + (xyy + xzz), d[3] + (yxx + yzz), d[5] + (zxx + zyy)
    xx, yy, zz = s[1] + (xxyy + xxzz), s[3] + (xxyy + yyzz), s[5] + (xxzz + yyzz)
    rho = (f[0] + s[1]) + (s[3] + s[5]) + (xxyy + (xxzz + yyzz))
    safe = jnp.where(fluid, rho, 1.0)
    inverse = 1.0 / safe
    hx, hy, hz = 0.5 * fx, 0.5 * fy, 0.5 * fz
    gx, gy, gz = jx + hx, jy + hy, jz + hz
    ux, uy, uz = gx * inverse, gy * inverse, gz * inverse
    third = safe * (1.0 / 3.0)
    ninth = safe * (1.0 / 9.0)
    px, py, pz = gx - fx, gy - fy, gz - fz
    txx, tyy, tzz = ux * px, uy * py, uz * pz
    sx, sy, sz = ux * fx, uy * fy, uz * fz
    pxy = ux * fy + uy * fx
    pxz = ux * fz + uz * fx
    pyz = uy * fz + uz * fy
    t3, s3 = (txx + tyy + tzz) * (1.0 / 3.0), (sx + sy + sz) * (2.0 / 3.0)
    rho = rho - rate(0) * (rho - safe)
    nx = jx + fx - rate(1) * (jx - safe * ux + hx)
    ny = jy + fy - rate(2) * (jy - safe * uy + hy)
    nz = jz + fz - rate(3) * (jz - safe * uz + hz)
    xy = xy + rate(4) * (gx * uy - 0.5 * pxy - xy) + pxy
    xz = xz + rate(5) * (gx * uz - 0.5 * pxz - xz) + pxz
    yz = yz + rate(6) * (gy * uz - 0.5 * pyz - yz) + pyz
    xx = xx + rate(7) * (third + txx - xx) + 2.0 * sx
    yy = yy + rate(8) * (third + tyy - yy) + 2.0 * sy
    zz = zz + rate(9) * (third + tzz - zz) + 2.0 * sz
    ex, ey, ez = jx * (1.0 / 3.0), jy * (1.0 / 3.0), jz * (1.0 / 3.0)
    qx, qy, qz = fx * (1.0 / 3.0), fy * (1.0 / 3.0), fz * (1.0 / 3.0)
    xyy = xyy + rate(10) * (ex - xyy) + qx
    xzz = xzz + rate(11) * (ex - xzz) + qx
    yxx = yxx + rate(12) * (ey - yxx) + qy
    yzz = yzz + rate(13) * (ey - yzz) + qy
    zxx = zxx + rate(14) * (ez - zxx) + qz
    zyy = zyy + rate(15) * (ez - zyy) + qz
    base = ninth + t3
    xxyy = xxyy + rate(16) * (base - 0.5 * tzz - xxyy) + (s3 - sz)
    xxzz = xxzz + rate(17) * (base - 0.5 * tyy - xxzz) + (s3 - sy)
    yyzz = yyzz + rate(18) * (base - 0.5 * txx - yyzz) + (s3 - sx)
    out = [None] * N
    for first, even, cross, odd1, odd2 in (
        (7, xxyy, xy, xyy, yxx),
        (11, xxzz, xz, xzz, zxx),
        (15, yyzz, yz, yzz, zyy),
    ):
        even, cross, odd1, odd2 = 0.25 * even, 0.25 * cross, 0.25 * odd1, 0.25 * odd2
        plus, minus = even + cross, even - cross
        both, diff = odd1 + odd2, odd1 - odd2
        out[first], out[first + 1] = plus + both, plus - both
        out[first + 2], out[first + 3] = minus + diff, minus - diff
    pairs = []
    for first, even, odd in (
        (1, xx - (xxyy + xxzz), nx - (xyy + xzz)),
        (3, yy - (xxyy + yyzz), ny - (yxx + yzz)),
        (5, zz - (xxzz + yyzz), nz - (zxx + zyy)),
    ):
        half_even, half_odd = 0.5 * even, 0.5 * odd
        out[first], out[first + 1] = half_even + half_odd, half_even - half_odd
        pairs.append(even)
    out[0] = rho - (pairs[0] + pairs[1] + pairs[2]) - (xxyy + xxzz + yyzz)
    return out, (ux, uy, uz)


def corner_pops(side):
    return SHIFT.index((side, 1, 0)), SHIFT.index((side, -1, 0))


def in_swap_order(pairs, right, left):
    if not pairs:
        return right, left
    odd = lax.axis_index("gy") % 2 == 1
    return jnp.where(odd, left, right), jnp.where(odd, right, left)


def sort_received(pairs, a_ref, b_ref, xl_ref, xr_ref):
    if pairs:
        xr_ref[...], xl_ref[...] = in_swap_order(pairs, a_ref[...], b_ref[...])
    else:
        xl_ref[...], xr_ref[...] = a_ref[...], b_ref[...]


def wall_of(wet, wall_ref):
    wall = jnp.zeros(wet.shape, jnp.float32)
    for c in range(wall_ref.shape[0]):
        wall = jnp.where(wet == c, wall_ref[c], wall)
    return wall


def face_kernel(f_hbm, mask_hbm, wet_hbm, wall_hbm, up_ref, down_ref, *scratch):
    row_in, mask_in, wet_in, wall_in, sems = scratch
    layers = row_in.shape[2]
    sides = ((0, down_ref, 0), (1, up_ref, f_hbm.shape[1] - layers))
    copies = [pltpu.make_async_copy(wall_hbm, wall_in, sems.at[0])]
    for s, _, at in sides:
        for i, (source, target) in enumerate(((mask_hbm, mask_in), (wet_hbm, wet_in))):
            sem = sems.at[1 + 2 * s + i]
            copies.append(
                pltpu.make_async_copy(source.at[pl.ds(at, layers)], target.at[s], sem)
            )
        sem = sems.at[5 + s]
        copies.append(
            pltpu.make_async_copy(f_hbm.at[:, pl.ds(at, layers)], row_in.at[s], sem)
        )
    for copy in copies:
        copy.start()
    for copy in copies:
        copy.wait()
    for s, ref, _ in sides:
        pore = mask_in[s] == 1
        density = total([row_in[s, k] for k in range(N)])
        ref[:layers] = potential_of(density, pore, wall_of(wet_in[s], wall_in))
        ref[layers:] = jnp.where(pore, 1.0, 0.0)


def turn_kernel(raw_ref, mask_in, wet_in, wall_ref, rate_ref, f_ref, rates_ref, flat_ref, mask_ref, pot_ref):
    layers, rows = f_ref.shape[1], f_ref.shape[2]
    for k in range(N):
        rates_ref[k] = jnp.full(rates_ref.shape[1:], rate_ref[k], jnp.float32)
    for i in range(0, layers * rows, TILE):
        at = slice(i, i + TILE)
        pore = mask_in[at] == 1
        density = total([raw_ref[k, at] for k in range(N)])
        flat_ref[0, at] = jnp.where(pore, 1.0, 0.0)
        flat_ref[1, at] = potential_of(density, pore, wall_of(wet_in[at], wall_ref))
    for i in range(layers):
        mask_ref[i] = flat_ref[0, pl.ds(i, rows, stride=layers)]
        pot_ref[i] = flat_ref[1, pl.ds(i, rows, stride=layers)]
    for k in range(N):
        for i in range(layers):
            f_ref[k, i] = raw_ref[k, pl.ds(i, rows, stride=layers)]


def start_pack_kernel(pairs, pot_ref, mask_ref, from_below, from_above, a_ref, b_ref, left_ref, right_ref):
    layers, rows = mask_ref.shape[0], mask_ref.shape[1]
    for ref, layer in ((left_ref, 0), (right_ref, layers - 1)):
        ref[:rows] = pot_ref[layer]
        ref[rows : 2 * rows] = mask_ref[layer]
        ref[2 * rows :] = jnp.zeros((TILE, ref.shape[1]), jnp.float32)
        for i, side in enumerate((from_below, from_above)):
            row = 2 * rows + i
            ref[row : row + 1] = side[layer : layer + 1]
            ref[row + 2 : row + 3] = side[layers + layer : layers + layer + 1]
    a_ref[...], b_ref[...] = in_swap_order(pairs, right_ref[...], left_ref[...])


def bits_kernel(mask_ref, from_below, from_above, bits_ref, pad_ref):
    size_x, size_y, size_z = mask_ref.shape
    nothing = jnp.zeros((TILE, size_z), jnp.float32)
    for x in (0, size_x + 1):
        for y in range(0, size_y + PAD, TILE):
            pad_ref[x, y : y + TILE] = nothing
    for x in range(size_x):
        pad_ref[1 + x, TILE : TILE + size_y] = mask_ref[x]
        for y, side in ((TILE - 1, from_below), (TILE + size_y, from_above)):
            pad_ref[1 + x, y : y + 1] = side[size_x + x : size_x + x + 1]
    for x in range(size_x):
        for y in range(0, size_y, TILE):
            bits = jnp.zeros((TILE, size_z), jnp.int32)
            for k in range(N):
                ex, ey, ez = SHIFT[k]
                row = TILE + y - ey
                source = roll_z(pad_ref[1 + x - ex, row : row + TILE], ez)
                bits = bits | jnp.where(source > 0.5, 1 << k, 0)
            bits_ref[x, y : y + TILE] = bits


def ring_kernel(pairs, bits_in, a_ref, b_ref, from_below, from_above, bits_ref, xl, xr, yd, yu, pad_ref):
    size_x, size_y, _ = bits_ref.shape
    sort_received(pairs, a_ref, b_ref, xl, xr)
    corner = 2 * size_y
    for i, (ref, side) in enumerate(((yd, from_below), (yu, from_above))):
        ref[: 2 * size_x] = side[...]
        ref[2 * size_x :] = jnp.zeros((TILE, ref.shape[1]), jnp.float32)
        for j, layer in enumerate((xl, xr)):
            row = 2 * size_x + j
            ref[row : row + 1] = layer[corner + i : corner + i + 1]
            ref[row + 2 : row + 3] = layer[corner + 2 + i : corner + 3 + i]
    bits_ref[...] = bits_in[...]
    for i, (side, ks, x) in enumerate(((xl, RIGHT, 0), (xr, LEFT, size_x - 1))):
        pad_ref[i, TILE : TILE + size_y] = side[size_y : 2 * size_y]
        for row, at in ((TILE - 1, corner + 2), (TILE + size_y, corner + 3)):
            pad_ref[i, row : row + 1] = side[at : at + 1]
        for y in range(0, size_y, TILE):
            bits = bits_in[x, y : y + TILE]
            for k in ks:
                _, ey, ez = SHIFT[k]
                row = TILE + y - ey
                source = roll_z(pad_ref[i, row : row + TILE], ez)
                bits = bits | jnp.where(source > 0.5, 1 << k, 0)
            bits_ref[x, y : y + TILE] = bits


class Layers:
    def __init__(self, edge_ref, middle_ref, size_x, edge):
        self.where = {}
        middle = [x for x in range(size_x) if x not in edge]
        for ref, xs in ((edge_ref, edge), (middle_ref, middle)):
            for i, x in enumerate(xs):
                self.where[x] = (ref, i)

    def load(self, x, y, k=None):
        ref, i = self.where[x]
        return ref[i, y : y + TILE] if k is None else ref[k, i, y : y + TILE]

    def row(self, x, y, k=None):
        ref, i = self.where[x]
        return ref[i, y : y + 1] if k is None else ref[k, i, y : y + 1]

    def store(self, x, y, value, k=None):
        ref, i = self.where[x]
        if k is None:
            ref[i, y : y + TILE] = value
        else:
            ref[k, i, y : y + TILE] = value


def two_layers(size_x):
    return [0, 1, size_x - 2, size_x - 1]


def one_layer(size_x):
    return [0, size_x - 1]


def fluid_at(bits_ref, x, y):
    return (bits_ref[x, y : y + TILE] & 1) != 0


def clear_outside(post, layers, size_y):
    nothing = jnp.zeros((TILE, post.shape[-1]), jnp.float32)
    for i in range(layers):
        for k in UP:
            post[k, i, :TILE] = nothing
        for k in DOWN:
            post[k, i, TILE + size_y :] = nothing


def collide_layers(xs, rates, f, bits_ref, pot, sides, post, speed):
    size_x, size_y, size_z = bits_ref.shape
    row_of = lax.broadcasted_iota(jnp.int32, (TILE, size_z), 0)
    for x in xs:
        for y in range(0, size_y, TILE):
            near = {
                (i, j): pot[1 + x + i, TILE + y + j : 2 * TILE + y + j]
                for i in (-1, 0, 1)
                for j in (-1, 0, 1)
            }
            scale = near[0, 0] * (STRENGTH / 36.0)
            dx = near[1, 0] - near[-1, 0]
            dy = near[0, 1] - near[0, -1]
            pp, pm, mp, mm = near[1, 1], near[1, -1], near[-1, 1], near[-1, -1]
            both = near[1, 0] + near[-1, 0] + near[0, 1] + near[0, -1] + 2.0 * near[0, 0]
            diag1, diag2 = pp - mm, pm - mp
            force = (
                scale * (2.0 * dy + (diag1 - diag2) + (roll_z(dy, 1) + roll_z(dy, -1))),
                scale * (2.0 * dx + (diag1 + diag2) + (roll_z(dx, 1) + roll_z(dx, -1))),
                scale * (roll_z(both, -1) - roll_z(both, 1)),
            )
            now = [f(k, x, y) for k in range(N)]
            if sides is not None:
                xl, xr, yd, yu = sides
                for at, side, ks in ((0, xl, RIGHT), (size_x - 1, xr, LEFT)):
                    if x == at:
                        for j, k in enumerate(ks):
                            now[k] = now[k] + side[j * size_y + y : j * size_y + y + TILE]
                for at, side, ks in ((0, yd, UP), (size_y - 1, yu, DOWN)):
                    if y <= at < y + TILE:
                        for j, k in enumerate(ks):
                            entering = side[j * size_x + x : j * size_x + x + 1]
                            now[k] = now[k] + jnp.where(row_of == at - y, entering, 0.0)
            fluid = fluid_at(bits_ref, x, y)
            after, at_speed = collide(now, fluid, force, lambda r: rates[r])
            for k in range(N):
                post.store(x, TILE + y, jnp.where(fluid, after[k], 0.0), k)
            if speed is not None:
                for c in range(3):
                    speed.store(x, y, jnp.where(fluid, at_speed[c], 0.0), c)


def stream_layers(xs, bits_ref, post, f, rho):
    size_x, size_y, _ = bits_ref.shape
    for x in xs:
        for y in range(0, size_y, TILE):
            bits = bits_ref[x, y : y + TILE]
            arrived = []
            for k in range(N):
                ex, ey, ez = SHIFT[k]
                value = post.load(x, TILE + y, OPPOSITE[k])
                if k > 0:
                    come = 0.0
                    if 0 <= x - ex < size_x:
                        come = roll_z(post.load(x - ex, TILE + y - ey, k), ez)
                    value = jnp.where((bits & (1 << k)) != 0, come, value)
                f.store(x, y, value, k)
                arrived.append(value)
            if rho is not None:
                rho.store(x, y, total(arrived))


def edge_kernel(first, last, pairs, *refs):
    refs = list(refs)
    take = lambda count: [refs.pop(0) for _ in range(count)]
    rates, bits_ref, pot0_ref, x0l, x0r, y0d, y0u = take(7)
    if first:
        f_ref = take(1)[0]
    else:
        f_edge, f_middle, rho_edge, rho_middle, xl, xr, yd, yu = take(8)
        own_right, own_left, own_up, own_down = take(4)
    pot, post_out, f_out, right_ref, left_ref, a_ref, b_ref, rest = take(8)
    size_x, size_y, size_z = bits_ref.shape
    edge2, edge1 = two_layers(size_x), one_layer(size_x)
    sides = None
    if first:
        f = lambda k, x, y: f_ref[k, x, y : y + TILE]
    else:
        sides = (xl, xr, yd, yu)
        held = Layers(f_edge, f_middle, size_x, edge1)
        density_of = Layers(rho_edge, rho_middle, size_x, edge1)
        f = lambda k, x, y: held.load(x, y, k)
    clear_outside(post_out, len(edge2), size_y)

    if first:
        for x in range(size_x):
            pot[1 + x, TILE : TILE + size_y] = pot0_ref[x]
        for x, side in ((0, x0l), (1 + size_x, x0r)):
            pot[x, TILE : TILE + size_y] = side[:size_y]
        for y, side in ((TILE - 1, y0d), (TILE + size_y, y0u)):
            for x in range(size_x):
                pot[1 + x, y : y + 1] = side[x : x + 1]
            for x, row in ((0, 2 * size_x), (1 + size_x, 2 * size_x + 1)):
                pot[x, y : y + 1] = side[row : row + 1]
    else:
        end = 6 * size_x
        row_of = lax.broadcasted_iota(jnp.int32, (TILE, size_z), 0)
        entering = {
            at: total([side[j * size_x : (j + 1) * size_x] for j in range(5)])
            for at, side in ((0, yd), (size_y - 1, yu))
        }
        for x in range(size_x):
            for y in range(0, size_y, TILE):
                density = density_of.load(x, y)
                for at, side in ((0, xl), (size_x - 1, xr)):
                    if x == at:
                        density = density + total(
                            [side[j * size_y + y : j * size_y + y + TILE] for j in range(5)]
                        )
                for at, rows in entering.items():
                    if y <= at < y + TILE:
                        density = density + jnp.where(row_of == at - y, rows[x : x + 1], 0.0)
                pot[1 + x, TILE + y : 2 * TILE + y] = potential_of(
                    density, fluid_at(bits_ref, x, y), pot0_ref[x, y : y + TILE]
                )
        for x, side, own, side0, g in (
            (0, xl, own_left, x0l, G_L),
            (1 + size_x, xr, own_right, x0r, G_R),
        ):
            for y in range(0, size_y, TILE):
                density = side[5 * size_y + y : 5 * size_y + y + TILE] + total(
                    [own[j * size_y + y : j * size_y + y + TILE] for j in range(5)]
                )
                for at, row in ((0, yd), (size_y - 1, yu)):
                    if y <= at < y + TILE:
                        more = row[end + g : end + g + 1]
                        density = density + jnp.where(row_of == at - y, more, 0.0)
                pot[x, TILE + y : 2 * TILE + y] = potential_of(
                    density,
                    side0[size_y + y : size_y + y + TILE] > 0.5,
                    side0[y : y + TILE],
                )
        for y, side, own, side0 in (
            (TILE - 1, yd, own_down, y0d),
            (TILE + size_y, yu, own_up, y0u),
        ):
            density = side[5 * size_x : 6 * size_x] + total(
                [own[j * size_x : (j + 1) * size_x] for j in range(5)]
            )
            value = potential_of(density, side0[size_x : 2 * size_x] > 0.5, side0[:size_x])
            for x in range(size_x):
                pot[1 + x, y : y + 1] = value[x : x + 1]
            for x, rc, g, i in ((0, RC_L, G_L, 0), (1 + size_x, RC_R, G_R, 1)):
                density = side[end + rc : end + rc + 1] + own[end + g : end + g + 1]
                row = 2 * size_x + i
                pot[x, y : y + 1] = potential_of(
                    density, side0[row + 2 : row + 3] > 0.5, side0[row : row + 1]
                )

    post = Layers(post_out, None, size_x, edge2)
    speed = Layers(rest, None, size_x, edge2) if last else None
    collide_layers(edge2, rates, f, bits_ref, pot, sides, post, speed)
    rho = None if last else Layers(rest, None, size_x, edge1)
    stream_layers(edge1, bits_ref, post, Layers(f_out, None, size_x, edge1), rho)

    at = (5 if last else 6) * size_y
    for i, (ref, x, ks, dirs) in enumerate(
        ((left_ref, 0, LEFT, corner_pops(-1)), (right_ref, size_x - 1, RIGHT, corner_pops(1)))
    ):
        for j, k in enumerate(ks):
            _, ey, ez = SHIFT[k]
            for y in range(0, size_y, TILE):
                row = j * size_y + y
                ref[row : row + TILE] = roll_z(post.load(x, TILE + y - ey, k), ez)
        ref[at : at + TILE] = jnp.zeros((TILE, size_z), jnp.float32)
        ref[at + C_UP : at + C_UP + 1] = post.row(x, TILE + size_y - 1, dirs[0])
        ref[at + C_DN : at + C_DN + 1] = post.row(x, TILE, dirs[1])
        if not last:
            ref[5 * size_y : 6 * size_y] = rest[i]
            for h, y, leave in ((H_UP, size_y - 1, UP), (H_DN, 0, DOWN)):
                ref[at + h : at + h + 1] = total(
                    [
                        roll_z(post.row(x - SHIFT[k][0], TILE + y, k), SHIFT[k][2])
                        for k in leave
                        if 0 <= x - SHIFT[k][0] < size_x
                    ]
                )
    a_ref[...], b_ref[...] = in_swap_order(pairs, right_ref[...], left_ref[...])


def middle_kernel(first, last, *refs):
    refs = list(refs)
    take = lambda count: [refs.pop(0) for _ in range(count)]
    rates, bits_ref, pot, post_edge, edge_rest = take(5)
    if first:
        f_ref = take(1)[0]
    else:
        f_edge, f_middle, yd, yu = take(4)
    f_out, up_ref, down_ref, rest = take(4)
    post_middle = take(1)[0]
    size_x, size_y, size_z = bits_ref.shape
    edge2, edge1 = two_layers(size_x), one_layer(size_x)
    sides = None
    if first:
        f = lambda k, x, y: f_ref[k, x, y : y + TILE]
    else:
        sides = (None, None, yd, yu)
        held = Layers(f_edge, f_middle, size_x, edge1)
        f = lambda k, x, y: held.load(x, y, k)
    clear_outside(post_middle, size_x - len(edge2), size_y)
    post = Layers(post_edge, post_middle, size_x, edge2)
    speed = None
    if last:
        speed = Layers(None, None, size_x, [])
        speed.store = lambda x, y, value, c: rest.__setitem__((c, turned(x, y, size_x)), value)
        for c in range(3):
            for i, x in enumerate(edge2):
                for y in range(0, size_y, TILE):
                    rest[c, turned(x, y, size_x)] = edge_rest[c, i, y : y + TILE]
    inner = [x for x in range(size_x) if x not in edge2]
    collide_layers(inner, rates, f, bits_ref, pot, sides, post, speed)
    rho = None if last else Layers(edge_rest, rest, size_x, edge1)
    inner = [x for x in range(size_x) if x not in edge1]
    stream_layers(inner, bits_ref, post, Layers(None, f_out, size_x, edge1), rho)
    for ref, y, ks in ((up_ref, size_y - 1, UP), (down_ref, 0, DOWN)):
        for j, k in enumerate(ks):
            ex, _, ez = SHIFT[k]
            for x in range(size_x):
                row = j * size_x + x
                if 0 <= x - ex < size_x:
                    ref[row : row + 1] = post.row(x - ex, TILE + y, k)
                else:
                    ref[row : row + 1] = jnp.zeros((1, size_z), jnp.float32)
            if ez != 0:
                rows = slice(j * size_x, (j + 1) * size_x)
                ref[rows] = roll_z(ref[rows], ez)
        if not last:
            for x in range(size_x):
                ref[5 * size_x + x : 5 * size_x + x + 1] = rho.row(x, y)


def pack_kernel(last, pairs, size_x, size_y, *refs):
    up_in, down_in, a_ref, b_ref, own_right, own_left, up_ref, down_ref, xl, xr = refs
    sort_received(pairs, a_ref, b_ref, xl, xr)
    parts = 5 if last else 6
    at = parts * size_y
    for ref, source, y, ks, c, h in (
        (up_ref, up_in, size_y - 1, UP, C_UP, H_UP),
        (down_ref, down_in, 0, DOWN, C_DN, H_DN),
    ):
        ref[...] = jnp.zeros(ref.shape, jnp.float32)
        ref[: parts * size_x] = source[: parts * size_x]
        for side, own, x, ex, rc, g in (
            (xl, own_left, 0, 1, RC_L, G_L),
            (xr, own_right, size_x - 1, -1, RC_R, G_R),
        ):
            j = [i for i, k in enumerate(ks) if SHIFT[k][0] == ex][0]
            row = j * size_x + x
            ref[row : row + 1] = side[at + c : at + c + 1]
            if not last:
                row = 5 * size_x + x
                ref[row : row + 1] = source[row : row + 1] + total(
                    [side[i * size_y + y : i * size_y + y + 1] for i in range(5)]
                )
                row = 6 * size_x
                ref[row + rc : row + rc + 1] = side[5 * size_y + y : 5 * size_y + y + 1] + total(
                    [own[i * size_y + y : i * size_y + y + 1] for i in range(5)]
                )
                ref[row + g : row + g + 1] = (
                    side[at + h : at + h + 1] + own[at + c : at + c + 1]
                )


def turned(layer, row, layers):
    return pl.ds(layer + row * layers, TILE, stride=layers)


def write_kernel(f_edge, f_middle, bits_ref, xl, xr, speed_ref, out_hbm, flat_ref, speed_hbm, sems, speed_sem):
    size_x, size_y, _ = bits_ref.shape
    held = Layers(f_edge, f_middle, size_x, one_layer(size_x))
    copies = [pltpu.make_async_copy(speed_ref, speed_hbm, speed_sem)]
    copies[0].start()
    for k in range(N):
        for x in range(size_x):
            for y in range(0, size_y, TILE):
                value = held.load(x, y, k)
                for at, side, ks in ((0, xl, RIGHT), (size_x - 1, xr, LEFT)):
                    if x == at and k in ks:
                        row = ks.index(k) * size_y + y
                        value = value + side[row : row + TILE]
                value = jnp.where(fluid_at(bits_ref, x, y), value, 0.0)
                flat_ref[k, turned(x, y, size_x)] = value
        copies.append(pltpu.make_async_copy(flat_ref.at[k], out_hbm.at[k], sems.at[k]))
        copies[-1].start()
    for copy in copies:
        copy.wait()


def end_kernel(out_in, flat_ref, mask_ref, yd, yu, out_hbm, planes, sems):
    del out_in
    layers = planes.shape[1]
    last = flat_ref.shape[1] - layers
    copies = []
    for at, side, ks in ((0, yd, UP), (last, yu, DOWN)):
        for j, k in enumerate(ks):
            i = len(copies)
            entering = side[j * layers : (j + 1) * layers]
            fluid = mask_ref[0, at : at + layers] > 0.5
            planes[i] = jnp.where(fluid, flat_ref[k, at : at + layers] + entering, 0.0)
            target = out_hbm.at[k, pl.ds(at, layers)]
            copies.append(pltpu.make_async_copy(planes.at[i], target, sems.at[i]))
            copies[-1].start()
    for copy in copies:
        copy.wait()


VMEM = pl.BlockSpec(memory_space=pltpu.VMEM)
SMEM = pl.BlockSpec(memory_space=pltpu.SMEM)
HBM = pl.BlockSpec(memory_space=pltpu.HBM)


def call(kernel, outs, args, special=None, special_out=None, scratch=(), cost=None, **kwargs):
    special, special_out = special or {}, special_out or {}
    return pl.pallas_call(
        kernel,
        out_shape=[jax.ShapeDtypeStruct(shape, dtype) for shape, dtype in outs],
        in_specs=[special.get(i, VMEM) for i in range(len(args))],
        out_specs=[special_out.get(i, VMEM) for i in range(len(outs))],
        scratch_shapes=[
            pltpu.VMEM(item, jnp.float32) if isinstance(item, tuple) else item for item in scratch
        ],
        compiler_params=pltpu.CompilerParams(vmem_limit_bytes=16 * 2**20),
        cost_estimate=cost,
        **kwargs,
    )(*args)


def shift(forward, backward, axis):
    count = lax.axis_size(axis)
    ahead = [(i, (i + 1) % count) for i in range(count)]
    return (
        lax.ppermute(forward, axis, ahead),
        lax.ppermute(backward, axis, [(b, a) for a, b in ahead]),
    )


def swap(a, b, axis):
    count = lax.axis_size(axis)
    partners = [
        [(i, (i + (1 if i % 2 == parity else -1)) % count) for i in range(count)]
        for parity in range(2)
    ]
    b = lax.ppermute(b, axis, partners[1])
    return lax.ppermute(a, axis, partners[0]), b


def per_device(populations, fluid_mask, wet_class, wall_potential, relax_rates):
    rows_x, rows_y, size_z = fluid_mask.shape
    pairs = lax.axis_size("gy") % 2 == 0
    exchange = swap if pairs else shift
    size_x, size_y = rows_y, rows_x
    cells = size_x * size_y
    f32, i32 = jnp.float32, jnp.int32
    whole = ((size_x, size_y, size_z), f32)
    rows = lambda count: ((count, size_z), f32)
    fields = lambda count: ((N, count, size_y, size_z), f32)
    flat = lambda count: ((count, cells, size_z), f32)
    padded = (size_x + 2, size_y + PAD, size_z)
    operations = 400 * cells * size_z
    cost = pl.CostEstimate(flops=operations, bytes_accessed=4 * operations // 20, transcendentals=0)

    operands = (
        populations.reshape(N, cells, size_z),
        fluid_mask.reshape(cells, size_z),
        wet_class.reshape(cells, size_z),
        wall_potential,
    )
    row_face = rows(2 * size_x)
    layer_face = rows(2 * size_y + TILE)
    ring_rows = rows(2 * size_x + TILE)
    up, down = call(
        face_kernel,
        [row_face, row_face],
        [pltpu.with_memory_space_constraint(item, pltpu.HBM) for item in operands],
        special={i: HBM for i in range(4)},
        scratch=[
            (2, N, size_x, size_z),
            pltpu.VMEM((2, size_x, size_z), i32),
            pltpu.VMEM((2, size_x, size_z), i32),
            pltpu.SMEM(wall_potential.shape, f32),
            pltpu.SemaphoreType.DMA((7,)),
        ],
    )
    *operands, up = lax.optimization_barrier((*operands, up))
    below, above = shift(up, down, "gx")
    f, rates, flat_mask, mask, pot0 = call(
        turn_kernel,
        [fields(size_x), ((N, TILE, size_z), f32), flat(2), whole, whole],
        (*operands, relax_rates),
        special={3: SMEM, 4: SMEM},
        cost=cost,
    )
    a, b = call(
        functools.partial(start_pack_kernel, False),
        [layer_face, layer_face],
        (pot0, mask, below, above),
        scratch=[layer_face[0]] * 2,
    )
    a, b = shift(a, b, "gy")
    whole_bits = ((size_x, size_y, size_z), i32)
    (bits,) = call(bits_kernel, [whole_bits], (mask, below, above), scratch=[padded], cost=cost)
    bits, x0l, x0r, y0d, y0u = call(
        functools.partial(ring_kernel, False),
        [whole_bits, layer_face, layer_face, ring_rows, ring_rows],
        (bits, a, b, below, above),
        scratch=[(2, size_y + PAD, size_z)],
    )
    edge2, edge1 = len(two_layers(size_x)), len(one_layer(size_x))
    held, sent = (f,), ()
    for step in range(STEPS):
        first, last = step == 0, step == STEPS - 1
        parts = 5 if last else 6
        x_rows, y_rows = rows(parts * size_y + TILE), rows(parts * size_x + (0 if last else TILE))
        pot, post, f_edge, right, left, a, b, rest = call(
            functools.partial(edge_kernel, first, last, pairs),
            [
                (padded, f32),
                ((N, edge2, size_y + PAD, size_z), f32),
                fields(edge1),
                x_rows,
                x_rows,
                x_rows,
                x_rows,
                ((3, edge2, size_y, size_z) if last else (edge1, size_y, size_z), f32),
            ],
            (rates, bits, pot0, x0l, x0r, y0d, y0u, *held, *sent),
            cost=cost,
        )
        a, b = exchange(a, b, "gy")
        f_middle, up, down, more = call(
            functools.partial(middle_kernel, first, last),
            [
                fields(size_x - edge1),
                y_rows,
                y_rows,
                flat(3) if last else ((size_x - edge1, size_y, size_z), f32),
            ],
            (rates, bits, pot, post, rest, *held[:2], *sent[2:4]),
            scratch=[(N, size_x - edge2, size_y + PAD, size_z)],
            cost=cost,
        )
        up, down, xl, xr = call(
            functools.partial(pack_kernel, last, pairs, size_x, size_y),
            [y_rows, y_rows, x_rows, x_rows],
            (up, down, a, b, right, left),
        )
        yd, yu = shift(up, down, "gx")
        held = (f_edge, f_middle, rest, more)
        sent = (xl, xr, yd, yu, right, left, up, down)
    out, flat_f, speed = call(
        write_kernel,
        [flat(N), flat(N), flat(3)],
        (f_edge, f_middle, bits, xl, xr, more),
        special_out={0: HBM, 2: HBM},
        scratch=[pltpu.SemaphoreType.DMA((N,)), pltpu.SemaphoreType.DMA(())],
        cost=cost,
    )
    (out,) = call(
        end_kernel,
        [flat(N)],
        (out, flat_f, flat_mask, yd, yu),
        special={0: HBM},
        special_out={0: HBM},
        scratch=[(10, size_x, size_z), pltpu.SemaphoreType.DMA((10,))],
        input_output_aliases={0: 0},
    )
    shape = (rows_x, rows_y, size_z)
    return out.reshape(N, *shape), speed.reshape(3, *shape)


def solution(mesh):
    return jax.shard_map(
        per_device,
        mesh=mesh,
        in_specs=(
            P(None, ("groups", "gx"), "gy", None),
            P(("groups", "gx"), "gy", None),
            P(("groups", "gx"), "gy", None),
            P("groups"),
            P(),
        ),
        out_specs=(P(None, ("groups", "gx"), "gy", None), P(None, ("groups", "gx"), "gy", None)),
        check_vma=False,
    )
```
